32 devices in a mesh: dp: 8 (over z, x), tensor: 4 (over y, core).
Axes of the slice: x: 2, y: 2, z: 4, core: 2. Of those that a mesh axis runs over, the one named last changes fastest.
Arguments:
- stream: bfloat16 [8192, 2048], P('dp'), may hold values from -24 to 24
- cotangent: bfloat16 [8192, 2048], P('dp'), may hold values from -6 to 6
- live_mask: int32 [8192], P('dp'), may hold values from 0 to 1, as said below
- piece_start: int32 [8, 2], P('dp'), may hold values from 0 to 768, as said below
- piece_len: int32 [8, 2], P('dp'), may hold values from 128 to 256
- norm1_gain: float32 [2048], replicated, may hold values from 0.1 to 1.9
- w_q: bfloat16 [2048, 2048], P(None, 'tensor'), may hold values from -0.125 to 0.125
- key_value_weight: bfloat16 [2048, 2, 1024], P(None, None, 'tensor'), may hold values from -0.125 to 0.125
- q_gain: float32 [128], replicated, may hold values from 0.1 to 1.9
- k_gain: float32 [128], replicated, may hold values from 0.1 to 1.9
- w_o: bfloat16 [2048, 2048], P(None, 'tensor'), may hold values from -0.5 to 0.5
- norm2_gain: float32 [2048], replicated, may hold values from 0.1 to 1.9
- w_gu: bfloat16 [2048, 2, 6144], P(None, None, 'tensor'), may hold values from -0.125 to 0.125
- w_down: bfloat16 [2048, 6144], P(None, 'tensor'), may hold values from -0.078125 to 0.078125
Outputs:
- out: bfloat16 [8192, 2048], P(('dp', 'tensor'))
- grad_stream: bfloat16 [8192, 2048], P(('dp', 'tensor'))
- grad_w_q: float32 [2048, 2048], P('dp', 'tensor')
- grad_w_kv: float32 [2048, 2, 1024], P('dp', None, 'tensor')
- grad_w_o: float32 [2048, 2048], P('dp', 'tensor')
- grad_w_gu: float32 [2048, 2, 6144], P('dp', None, 'tensor')
- grad_w_down: float32 [2048, 6144], P('dp', 'tensor')
- grad_norm1: float32 [2048], replicated
- grad_norm2: float32 [2048], replicated
- grad_q_gain: float32 [128], replicated
- grad_k_gain: float32 [128], replicated
- stats: float32 [3], replicated
The draws below stay inside these ranges and needn't reach their ends.
Inputs may be any that keep to these rules, and one draw needn't show every extreme that they name: `live_mask`: in each sequence the live tokens come first, and the first token of each sequence is live. `piece_start`: piece k of a sequence starts at k * 512 or later and ends, with its length, before (k + 1) * 512.
All inputs are finite; a program needn't handle non-finite values.
Results may differ from the reference program's by a relative error of at most 0.023.
Values may be sent and summed in bfloat16 or wider, within the bound.
A program may use at most 320 MiB of HBM per device.

```python
import math
import jax
import jax.numpy as jnp
from jax import lax

MODEL_WIDTH = 2048
QUERY_HEADS = 16
KEY_VALUE_HEADS = 8
HEAD_SIZE = 128
FF = 6144
SEQ_LEN = 1024
PIECE = 256
PIECES = 2
NSEQ = 8
TOKENS = 8192


def draw_stream(key, part):
    key_base, key_rows, key_cols = jax.random.split(key, 3)
    tok_rows = NSEQ * SEQ_LEN
    sequence = jnp.arange(tok_rows, dtype=jnp.int32) // SEQ_LEN
    fraction = sequence.astype(jnp.float32) / max(NSEQ - 1, 1)
    col_scale = jnp.exp(jax.random.uniform(key_cols, (1, MODEL_WIDTH), jnp.float32, math.log(0.6), math.log(1.6)))
    base_values = jax.random.normal(key_base, (tok_rows, MODEL_WIDTH), jnp.float32)
    seq_scale = jnp.exp(fraction * (0.5 * math.log(3.0)))
    row_scale = jnp.exp(jax.random.uniform(key_rows, (tok_rows, 1), jnp.float32, math.log(0.5), math.log(2.0)))
    return jnp.clip(base_values * seq_scale[:, None] * row_scale * col_scale, -24.0, 24.0).astype(jnp.bfloat16)


def draw_live_mask(key, part):
    sequence = jnp.arange(NSEQ, dtype=jnp.int32)
    lowest = SEQ_LEN // 3
    base_len = lowest + (SEQ_LEN - lowest) * sequence // max(NSEQ - 1, 1)
    jitter = jax.random.randint(key, (NSEQ,), 0, SEQ_LEN // 16 + 1)
    live_len = jnp.maximum(base_len - jitter, 1)
    position = jnp.arange(SEQ_LEN, dtype=jnp.int32)
    return (position[None, :] < live_len[:, None]).astype(jnp.int32).reshape(NSEQ * SEQ_LEN)


def draw_piece_start(key, part):
    piece_span = SEQ_LEN // PIECES
    offset = jax.random.randint(key, (NSEQ, PIECES), 0, piece_span - PIECE + 1)
    sequence = jnp.arange(NSEQ, dtype=jnp.int32)[:, None]
    piece_index = jnp.arange(PIECES, dtype=jnp.int32)[None, :]
    offset = jnp.where((sequence == 0) & (piece_index == 0), 0, offset)
    offset = jnp.where((sequence == NSEQ - 1) & (piece_index == PIECES - 1), piece_span - PIECE, offset)
    return (piece_index * piece_span + offset).astype(jnp.int32)


def set_ends(entries, key, least, largest):
    longest = entries.shape.index(max(entries.shape))
    spots = []
    for shift in (0, 1):
        where = [jax.random.randint(jax.random.fold_in(key, axis), (), 0, length) for axis, length in enumerate(entries.shape)]
        where[longest] = (where[longest] + shift) % entries.shape[longest]
        spots.append(tuple(where))
    return entries.at[spots[0]].set(least).at[spots[1]].set(largest)


def levels(rng, shape, pieces, smallest, high):
    loudness = 1.0
    for dim, shards_of in pieces:
        draws = jax.random.uniform(jax.random.fold_in(jax.random.fold_in(rng, 6), dim), (shards_of,), jnp.float32, smallest / len(pieces), high / len(pieces))
        loudness = loudness * jnp.repeat(jnp.exp(draws), shape[dim] // shards_of).reshape((-1,) + (1,) * (len(shape) - 1 - dim))
    return loudness


def scatter_about(rng, shape, spread, reach, pieces=(), held_as=jnp.bfloat16):
    array = spread * jax.random.normal(rng, shape, jnp.float32)
    if pieces:
        array = array * levels(rng, shape, pieces, -0.22, 0.18)
    return jnp.clip(array, -reach, reach).astype(held_as)


def setup_inputs(seed: int = 0) -> dict:
    seeds = jax.random.split(jax.random.key(seed), 15)
    return {
        "stream": draw_stream(jax.random.fold_in(seeds[14], 71), 0),
        "cotangent": scatter_about(seeds[1], (TOKENS, MODEL_WIDTH), 1.0, 6.0, ((0, 8),)),
        "live_mask": draw_live_mask(jax.random.fold_in(seeds[14], 71), 0),
        "piece_start": draw_piece_start(jax.random.fold_in(seeds[14], 71), 0),
        "piece_len": set_ends(jax.random.randint(seeds[4], (NSEQ, PIECES), PIECE // 2, PIECE + 1), jax.random.fold_in(seeds[4], 1), PIECE // 2, PIECE).astype(jnp.int32),
        "norm1_gain": jnp.clip(1.0 + 0.18 * jax.random.normal(seeds[5], (MODEL_WIDTH,), jnp.float32), 0.1, 1.9),
        "w_q": scatter_about(seeds[6], (MODEL_WIDTH, QUERY_HEADS * HEAD_SIZE), MODEL_WIDTH ** -0.5, 0.125, ((1, 4),)),
        "key_value_weight": scatter_about(seeds[7], (MODEL_WIDTH, 2, KEY_VALUE_HEADS * HEAD_SIZE), MODEL_WIDTH ** -0.5, 0.125, ((2, 4),)),
        "q_gain": jnp.clip(1.0 + 0.18 * jax.random.normal(seeds[8], (HEAD_SIZE,), jnp.float32), 0.1, 1.9),
        "k_gain": jnp.clip(1.0 + 0.18 * jax.random.normal(seeds[9], (HEAD_SIZE,), jnp.float32), 0.1, 1.9),
        "w_o": scatter_about(seeds[10], (MODEL_WIDTH, QUERY_HEADS * HEAD_SIZE), (QUERY_HEADS * HEAD_SIZE // 16) ** -0.5, 0.5, ((1, 4),)),
        "norm2_gain": jnp.clip(1.0 + 0.18 * jax.random.normal(seeds[11], (MODEL_WIDTH,), jnp.float32), 0.1, 1.9),
        "w_gu": scatter_about(seeds[12], (MODEL_WIDTH, 2, FF), MODEL_WIDTH ** -0.5, 0.125, ((2, 4),)),
        "w_down": scatter_about(seeds[13], (MODEL_WIDTH, FF), FF ** -0.5, 0.078125, ((1, 4),)),
    }


EPSILON = 1e-06
MASKED = -1e+30
highest = lax.Precision.HIGHEST

@jax.custom_vjp
def low(v):
    return lax.optimization_barrier(v.astype(jnp.bfloat16)).astype(jnp.float32)

@jax.custom_vjp
def low_back(v):
    return v

def low_keep(v):
    return (low(v), None)

def low_pass(kept, grad):
    return (grad,)

def back_keep(v):
    return (v, None)

def back_low(kept, grad):
    return (low(grad),)
low.defvjp(low_keep, low_pass)
low_back.defvjp(back_keep, back_low)

def rms_scale(values):
    return lax.rsqrt(lax.optimization_barrier(jnp.mean(values * values, axis=-1, keepdims=True)) + EPSILON)

def rope_tables(text_length):
    half_dim = HEAD_SIZE // 2
    inverse = jnp.exp(jnp.arange(half_dim, dtype=jnp.float32) * (-2.0 * math.log(1000000.0) / HEAD_SIZE))
    angles = jnp.arange(text_length, dtype=jnp.float32)[:, None] * inverse[None, :]
    return (jnp.cos(angles), jnp.sin(angles))

def rotate(values, cos_table, sin_table):
    half_dim = values.shape[-1] // 2
    first_half = values[..., :half_dim]
    second_half = values[..., half_dim:]
    cos_wide = cos_table[:, None, :]
    sin_wide = sin_table[:, None, :]
    return jnp.concatenate([first_half * cos_wide - second_half * sin_wide, second_half * cos_wide + first_half * sin_wide], axis=-1)

def piece_labels(starts, lengths, text_length):
    position = jnp.arange(text_length, dtype=jnp.int32)
    inside = (position >= starts[..., :, None]) & (position < (starts + lengths)[..., :, None])
    number = jnp.arange(1, starts.shape[-1] + 1, dtype=jnp.int32)
    return lax.optimization_barrier(jnp.sum(jnp.where(inside, number[:, None], 0), axis=-2)).astype(jnp.int32) - 1

def allowed_pairs(query_pos, key_pos, query_label, key_label, key_live):
    causal = key_pos[None, :] <= query_pos[:, None]
    same_piece = (query_label[:, None] == key_label[None, :]) & (query_label[:, None] >= 0)
    return (key_live[None, :] > 0) & (causal | same_piece)

def attend(packed):
    queries, key_vecs, value_vecs, key_live, labels = packed
    position = jnp.arange(key_vecs.shape[0], dtype=jnp.int32)
    scores = jnp.einsum('qkrd,jkd->krqj', queries, key_vecs, precision=highest) * HEAD_SIZE ** (-0.5)
    scores = low_back(scores)
    scores = jnp.where(allowed_pairs(position, position, labels, labels, key_live)[None, None], scores, MASKED)
    row_max = lax.optimization_barrier(jnp.max(scores, axis=-1, keepdims=True))
    exp_scores = jnp.exp(scores - row_max)
    soft_weights = low(exp_scores / lax.optimization_barrier(jnp.sum(exp_scores, axis=-1, keepdims=True)))
    return jnp.einsum('krqj,jkd->qkrd', soft_weights, value_vecs, precision=highest)

def block_forward(stream_in, w_q, key_value_weight, w_o, w_gu, w_down, norm1_gain, norm2_gain, q_gain, k_gain, live_group, label_group):
    query_groups = stream_in.shape[0]
    text_length = stream_in.shape[1]
    normed_in = low(stream_in * rms_scale(stream_in) * norm1_gain)
    q_raw = low_back(jnp.einsum('gld,dn->gln', normed_in, w_q, precision=highest))
    key_value_projected = low_back(jnp.einsum('gld,dcn->gcln', normed_in, key_value_weight, precision=highest))
    q_heads = q_raw.reshape(query_groups, text_length, QUERY_HEADS, HEAD_SIZE)
    key_head_rows = key_value_projected[:, 0].reshape(query_groups, text_length, KEY_VALUE_HEADS, HEAD_SIZE)
    value_head_rows = key_value_projected[:, 1].reshape(query_groups, text_length, KEY_VALUE_HEADS, HEAD_SIZE)
    cos_table, sin_table = rope_tables(text_length)
    query_rotated = low(rotate(q_heads * rms_scale(q_heads) * q_gain, cos_table, sin_table))
    k_rot = low(rotate(key_head_rows * rms_scale(key_head_rows) * k_gain, cos_table, sin_table))
    v_low = low(value_head_rows)
    query_group_rows = query_rotated.reshape(query_groups, text_length, KEY_VALUE_HEADS, QUERY_HEADS // KEY_VALUE_HEADS, HEAD_SIZE)
    attended = lax.map(jax.checkpoint(attend), (query_group_rows, k_rot, v_low, live_group, label_group))
    mixed_heads = low(low_back(attended.reshape(query_groups, text_length, QUERY_HEADS * HEAD_SIZE)))
    attn_out = low_back(jnp.einsum('gln,dn->gld', mixed_heads, w_o, precision=highest))
    residual = stream_in + attn_out
    normed_mid = low(residual * rms_scale(residual) * norm2_gain)
    gate_up = low_back(jnp.einsum('gld,dcf->gclf', normed_mid, w_gu, precision=highest))
    hidden = low(jax.nn.silu(gate_up[:, 0]) * gate_up[:, 1])
    ffn_out = low_back(jnp.einsum('glf,df->gld', hidden, w_down, precision=highest))
    return (residual + ffn_out, (attn_out, ffn_out))

def reference(stream, cotangent, live_mask, piece_start, piece_len, norm1_gain, w_q, key_value_weight, q_gain, k_gain, w_o, norm2_gain, w_gu, w_down):
    group_size = 1
    for candidate in range(1, NSEQ + 1):
        if NSEQ % candidate == 0 and candidate * SEQ_LEN <= 4096:
            group_size = candidate
    steps_count = NSEQ // group_size
    stream_all = stream.astype(jnp.float32).reshape(steps_count, group_size, SEQ_LEN, MODEL_WIDTH)
    cot_all = cotangent.astype(jnp.float32).reshape(steps_count, group_size, SEQ_LEN, MODEL_WIDTH)
    live_all = live_mask.reshape(steps_count, group_size, SEQ_LEN)
    label_all = piece_labels(piece_start, piece_len, SEQ_LEN).reshape(steps_count, group_size, SEQ_LEN)
    params = (w_q.astype(jnp.float32), key_value_weight.astype(jnp.float32), w_o.astype(jnp.float32), w_gu.astype(jnp.float32), w_down.astype(jnp.float32), norm1_gain, norm2_gain, q_gain, k_gain)

    def one_step(carry, packed):
        stream_in, cot_in, live_group, label_group = packed

        def forward_group(stream_arg, *weights):
            return block_forward(stream_arg, *weights, live_group, label_group)
        result, pull, aux = jax.vjp(forward_group, stream_in, *params, has_aux=True)
        grads = pull(cot_in)
        attn_out, ffn_out = aux
        live = live_group.astype(jnp.float32)[..., None]
        sums = jnp.stack([jnp.sum(live * result * result), jnp.sum(live * attn_out * attn_out), jnp.sum(live * ffn_out * ffn_out), jnp.sum(live_group.astype(jnp.float32))])
        new_carry = tuple((old + new for old, new in zip(carry, tuple(grads[1:]) + (sums,))))
        return (new_carry, (result.astype(jnp.bfloat16), grads[0].astype(jnp.bfloat16)))
    initial = tuple((jnp.zeros_like(param) for param in params)) + (jnp.zeros((4,), jnp.float32),)
    totals, outputs = lax.scan(one_step, initial, (stream_all, cot_all, live_all, label_all))
    result_all, grad_all = outputs
    sums = totals[9]
    stats = jnp.sqrt(sums[:3] / (sums[3] * MODEL_WIDTH))
    return (result_all.reshape(NSEQ * SEQ_LEN, MODEL_WIDTH), grad_all.reshape(NSEQ * SEQ_LEN, MODEL_WIDTH), totals[0], totals[1], totals[2], totals[3], totals[4], totals[5], totals[6], totals[7], totals[8], stats)
```

```python
import math

import jax
import jax.numpy as jnp
import numpy as np
from jax import lax
from jax.experimental import pallas as pl
from jax.experimental.pallas import tpu as pltpu
from jax.sharding import PartitionSpec as P

MODEL_WIDTH = 2048
HEAD_SIZE = 128
SEQ_LEN = 1024
EPSILON = 1e-06
MASKED = -1e30
SCALE = HEAD_SIZE ** (-0.5)
F32 = jnp.float32
BF16 = jnp.bfloat16
VMEM_BYTES = 60 * 1024 * 1024
NN = (((1,), (0,)), ((), ()))
NT = (((1,), (1,)), ((), ()))
TN = (((0,), (0,)), ((), ()))
PIECE_COLS = 768


def dot(left, right, dims=NN):
    return lax.dot_general(left, right, dims, preferred_element_type=F32)


def f32(values):
    return values.astype(F32)


def b16(values):
    return values.astype(BF16)


def shape(dims, kind=BF16):
    return jax.ShapeDtypeStruct(dims, kind)


def call(body, outs, grid, in_specs, out_specs, args, name, flops, scalars=None, scratch=(), alias=None):
    moved = sum(a.size * a.dtype.itemsize for a in args)
    outs_list = outs if isinstance(outs, (list, tuple)) else [outs]
    moved += sum(math.prod(o.shape) * jnp.dtype(o.dtype).itemsize for o in outs_list)
    count = 0 if scalars is None else 1
    return pl.pallas_call(
        body,
        out_shape=outs,
        grid_spec=pltpu.PrefetchScalarGridSpec(
            num_scalar_prefetch=count,
            grid=grid,
            in_specs=in_specs,
            out_specs=out_specs,
            scratch_shapes=scratch,
        ),
        compiler_params=pltpu.CompilerParams(vmem_limit_bytes=VMEM_BYTES),
        cost_estimate=pl.CostEstimate(flops=int(flops), bytes_accessed=int(moved), transcendentals=0),
        input_output_aliases=alias or {},
        name=name,
    )(*(() if scalars is None else (scalars,)), *args)


def whole(array):
    dims = array.shape
    return pl.BlockSpec(dims, lambda *_: (0,) * len(dims))


def rms_scale(values):
    return lax.rsqrt(jnp.mean(values * values, axis=-1, keepdims=True) + EPSILON)


def norm_back(values, gain, grad):
    scale = rms_scale(values)
    weighted = grad * gain
    along = jnp.mean(weighted * values, axis=-1, keepdims=True)
    grad_values = scale * weighted - values * (scale * scale * scale * along)
    grad_gain = jnp.sum(grad * (values * scale), axis=0, keepdims=True)
    return grad_values, grad_gain


def rope_tables():
    half = HEAD_SIZE // 2
    inverse = np.exp(np.arange(half) * (-2.0 * math.log(1000000.0) / HEAD_SIZE))
    angles = np.arange(SEQ_LEN)[:, None] * inverse[None, :]
    cos, sin = np.cos(angles), np.sin(angles)
    wide_cos = np.concatenate([cos, cos], axis=1).astype(np.float32)
    wide_sin = np.concatenate([-sin, sin], axis=1).astype(np.float32)
    return wide_cos, wide_sin


def rotate(values, cos, sin):
    return values * cos + pltpu.roll(values, HEAD_SIZE // 2, 1) * sin


def rotate_back(values, cos, sin):
    return values * cos - pltpu.roll(values, HEAD_SIZE // 2, 1) * sin


def head(index):
    return slice(index * HEAD_SIZE, (index + 1) * HEAD_SIZE)


def norm_query(stream, gain, w_q, rows):
    tokens, width = stream.shape
    cols = w_q.shape[1]

    def body(stream_ref, gain_ref, w_ref, normed_ref, query_ref):
        values = f32(stream_ref[...])
        normed = b16(values * rms_scale(values) * gain_ref[...])
        normed_ref[...] = normed
        query_ref[...] = dot(normed, w_ref[...])

    return call(
        body,
        [shape((tokens, width)), shape((tokens, cols), F32)],
        (tokens // rows,),
        [pl.BlockSpec((rows, width), lambda i: (i, 0)), whole(gain), whole(w_q)],
        [pl.BlockSpec((rows, width), lambda i: (i, 0)), pl.BlockSpec((rows, cols), lambda i: (i, 0))],
        (stream, gain, w_q),
        "norm_query",
        2 * tokens * width * cols,
    )


def rope_forward(q_raw, kv_raw, q_gain, k_gain, cos, sin, rows):
    tokens, q_cols = q_raw.shape
    kv_cols = kv_raw.shape[2]

    def body(q_ref, kv_ref, qg_ref, kg_ref, cos_ref, sin_ref, q_out, k_out, v_out):
        cos_rows, sin_rows = cos_ref[...], sin_ref[...]
        for h in range(q_cols // HEAD_SIZE):
            values = q_ref[:, head(h)]
            q_out[:, head(h)] = b16(rotate(values * rms_scale(values) * qg_ref[...], cos_rows, sin_rows))
        for h in range(kv_cols // HEAD_SIZE):
            values = kv_ref[0, :, head(h)]
            k_out[:, head(h)] = b16(rotate(values * rms_scale(values) * kg_ref[...], cos_rows, sin_rows))
        v_out[...] = b16(kv_ref[1])

    row = lambda cols: pl.BlockSpec((rows, cols), lambda i: (i, 0))
    return call(
        body,
        [shape((tokens, q_cols)), shape((tokens, kv_cols)), shape((tokens, kv_cols))],
        (tokens // rows,),
        [
            row(q_cols),
            pl.BlockSpec((2, rows, kv_cols), lambda i: (0, i, 0)),
            whole(q_gain),
            whole(k_gain),
            row(HEAD_SIZE),
            row(HEAD_SIZE),
        ],
        [row(q_cols), row(kv_cols), row(kv_cols)],
        (q_raw, kv_raw, q_gain, k_gain, cos, sin),
        "rope_forward",
        20 * tokens * q_cols,
    )


def key_limit(scalars, start, count, pieces):
    position = start + lax.broadcasted_iota(jnp.int32, (count, 1), 0)
    limit = position + 1
    for piece in range(pieces):
        first, last = scalars[2 + 2 * piece], scalars[3 + 2 * piece]
        inside = (position >= first) & (position < last)
        limit = jnp.where(inside, jnp.maximum(limit, last), limit)
    return jnp.minimum(limit, scalars[1])


def soft_weights(query, keys, limit):
    scores = dot(query, keys, NT) * SCALE
    key_pos = lax.broadcasted_iota(jnp.int32, scores.shape, 1)
    scores = jnp.where(key_pos < limit, scores, MASKED)
    shifted = jnp.exp(scores - jnp.max(scores, axis=-1, keepdims=True))
    return shifted / jnp.sum(shifted, axis=-1, keepdims=True)


def attend_forward(scalars, query, key, value, w_o, chunk, count, reach, pieces):
    q_cols, kv_cols, width = query.shape[1], key.shape[1], w_o.shape[0]
    heads, half = q_cols // HEAD_SIZE, count // 2
    repeat = q_cols // kv_cols

    def body(scalars, q_ref, k_ref, v_ref, w_ref, own_out, other_out, own_mix, other_mix, mixed):
        limit = key_limit(scalars, chunk * count, count, pieces)
        for h in range(heads):
            weights = soft_weights(q_ref[:, head(h)], k_ref[:, head(h // repeat)], limit)
            mixed[:, head(h)] = b16(dot(b16(weights), v_ref[:, head(h // repeat)]))
        core = scalars[0]
        other = mixed[pl.ds(pl.multiple_of((1 - core) * half, half), half), :]
        own = mixed[pl.ds(pl.multiple_of(core * half, half), half), :]
        other_mix[...] = other
        own_mix[...] = own
        other_out[...] = b16(dot(other, w_ref[...], NT))
        own_out[...] = b16(dot(own, w_ref[...], NT))

    return call(
        body,
        [shape((half, width)), shape((half, width)), shape((half, q_cols)), shape((half, q_cols))],
        (1,),
        [
            pl.BlockSpec((count, q_cols), lambda i, s: (chunk, 0)),
            pl.BlockSpec((reach, kv_cols), lambda i, s: (0, 0)),
            pl.BlockSpec((reach, kv_cols), lambda i, s: (0, 0)),
            whole(w_o),
        ],
        [
            pl.BlockSpec((half, width), lambda i, s: (0, 0)),
            pl.BlockSpec((half, width), lambda i, s: (0, 0)),
            pl.BlockSpec((half, q_cols), lambda i, s: (0, 0)),
            pl.BlockSpec((half, q_cols), lambda i, s: (0, 0)),
        ],
        (query, key, value, w_o),
        "attend_forward",
        4 * count * reach * q_cols + 2 * count * width * q_cols,
        scalars,
        [pltpu.VMEM((count, q_cols), BF16)],
    )


def middle(scalars, stream, chip, part, gain, chunk):
    rows, width = chip.shape

    def body(scalars, stream_ref, chip_ref, part_ref, gain_ref, resid_out, normed_out):
        resid = f32(stream_ref[...]) + (f32(chip_ref[...]) + f32(part_ref[...]))
        resid_out[...] = resid
        normed_out[...] = b16(resid * rms_scale(resid) * gain_ref[...])

    flat = pl.BlockSpec((rows, width), lambda i, s: (0, 0))
    return call(
        body,
        [shape((rows, width), F32), shape((rows, width))],
        (1,),
        [pl.BlockSpec((rows, width), lambda i, s: (2 * chunk + s[0], 0)), flat, flat, whole(gain)],
        [flat, flat],
        (stream, chip, part, gain),
        "middle",
        10 * rows * width,
        scalars,
    )


def gate_back(scalars, gate_up, grad_hidden, rows):
    planes, tokens, cols = gate_up.shape
    groups = tokens // (2 * rows)
    natural = lambda i, s: 2 * (i % groups) + (s[0] + i // groups) % 2

    def body(scalars, gu_ref, gh_ref, hidden_out, grad_out):
        gate, up, grad = gu_ref[0], gu_ref[1], gh_ref[...]
        logistic = 1.0 / (1.0 + jnp.exp(-gate))
        silu = gate * logistic
        hidden_out[...] = b16(silu * up)
        grad_out[0] = b16(grad * up * logistic * (1.0 + gate * (1.0 - logistic)))
        grad_out[1] = b16(grad * silu)

    return call(
        body,
        [shape((tokens, cols)), shape((planes, tokens, cols))],
        (tokens // rows,),
        [
            pl.BlockSpec((planes, rows, cols), lambda i, s: (0, i, 0)),
            pl.BlockSpec((rows, cols), lambda i, s: (natural(i, s), 0)),
        ],
        [
            pl.BlockSpec((rows, cols), lambda i, s: (natural(i, s), 0)),
            pl.BlockSpec((planes, rows, cols), lambda i, s: (0, i, 0)),
        ],
        (gate_up, grad_hidden),
        "gate_back",
        20 * tokens * cols,
        scalars,
    )


def project_other_first(scalars, values, weights, rows):
    tokens, depth = values.shape
    width = weights.shape[0]
    groups = tokens // (2 * rows)
    natural = lambda i, s: 2 * (i % groups) + (s[0] + 1 + i // groups) % 2

    def body(scalars, values_ref, weights_ref, out):
        out[...] = b16(dot(values_ref[...], weights_ref[...], NT))

    return call(
        body,
        shape((tokens, width)),
        (tokens // rows,),
        [pl.BlockSpec((rows, depth), lambda i, s: (natural(i, s), 0)), whole(weights)],
        pl.BlockSpec((rows, width), lambda i, s: (i, 0)),
        (values, weights),
        "project",
        2 * tokens * depth * width,
        scalars,
    )


def middle_back(scalars, resid, chip, part, cotangent, gain, chunk):
    rows, width = resid.shape

    def body(scalars, resid_ref, chip_ref, part_ref, cot_ref, gain_ref, resid_out, attn_out, gain_out):
        grad = f32(chip_ref[...]) + f32(part_ref[...])
        back, gain_out[...] = norm_back(resid_ref[...], gain_ref[...], grad)
        total = f32(cot_ref[...]) + back
        resid_out[...] = total
        attn_out[...] = b16(total)

    flat = pl.BlockSpec((rows, width), lambda i, s: (0, 0))
    return call(
        body,
        [shape((rows, width), F32), shape((rows, width)), shape((1, width), F32)],
        (1,),
        [flat, flat, flat, pl.BlockSpec((rows, width), lambda i, s: (2 * chunk + s[0], 0)), whole(gain)],
        [flat, flat, pl.BlockSpec((1, width), lambda i, s: (0, 0))],
        (resid, chip, part, cotangent, gain),
        "middle_back",
        20 * rows * width,
        scalars,
    )


def attend_backward(scalars, own, other, w_o, query, key, value, before, chunk, count, reach, pieces):
    tokens, q_cols = query.shape
    kv_cols, width = key.shape[1], w_o.shape[0]
    heads, half = q_cols // HEAD_SIZE, count // 2
    repeat = q_cols // kv_cols
    old = 0 if before is None else before[1].shape[0]

    def body(scalars, own_ref, other_ref, w_ref, q_ref, k_ref, v_ref, *rest):
        olds = rest[: len(rest) - 4]
        q_out, k_out, v_out, mixed = rest[len(rest) - 4 :]
        core = scalars[0]
        w = w_ref[...]
        mixed[pl.ds(pl.multiple_of(core * half, half), half), :] = b16(dot(own_ref[...], w))
        mixed[pl.ds(pl.multiple_of((1 - core) * half, half), half), :] = b16(dot(other_ref[...], w))
        limit = key_limit(scalars, chunk * count, count, pieces)
        for g in range(kv_cols // HEAD_SIZE):
            k_total, v_total = 0.0, 0.0
            for h in range(g * repeat, (g + 1) * repeat):
                q_head, k_head, grad = q_ref[:, head(h)], k_ref[:, head(g)], mixed[:, head(h)]
                weights = soft_weights(q_head, k_head, limit)
                grad_weights = dot(grad, v_ref[:, head(g)], NT)
                delta = jnp.sum(weights * grad_weights, axis=-1, keepdims=True)
                grad_scores = b16(weights * (grad_weights - delta))
                q_out[:, head(h)] = dot(grad_scores, k_head) * SCALE
                k_total = k_total + dot(grad_scores, q_head, TN)
                v_total = v_total + dot(b16(weights), grad, TN)
            k_out[:, head(g)] = k_total * SCALE
            v_out[:, head(g)] = v_total
        if old:
            k_out[:old, :] += olds[1][...]
            v_out[:old, :] += olds[2][...]

    flat = pl.BlockSpec((half, width), lambda i, s: (0, 0))
    keys = pl.BlockSpec((reach, kv_cols), lambda i, s: (0, 0))
    args = [own, other, w_o, query, key, value]
    specs = [flat, flat, whole(w_o), pl.BlockSpec((count, q_cols), lambda i, s: (chunk, 0)), keys, keys]
    alias = None
    if before is not None:
        args += list(before)
        specs += [pl.BlockSpec(memory_space=pl.ANY), whole(before[1]), whole(before[2])]
        alias = {7: 0}
    return call(
        body,
        [shape((tokens, q_cols), F32), shape((reach, kv_cols), F32), shape((reach, kv_cols), F32)],
        (1,),
        specs,
        [pl.BlockSpec((count, q_cols), lambda i, s: (chunk, 0)), keys, keys],
        args,
        "attend_backward",
        10 * count * reach * q_cols + 2 * count * width * q_cols,
        scalars,
        [pltpu.VMEM((count, q_cols), BF16)],
        alias,
    )


def rope_backward(scalars, grad_q, grad_k, grad_v, q_raw, kv_raw, q_gain, k_gain, cos, sin, w_q, w_k, w_v, rows):
    tokens, q_cols = q_raw.shape
    kv_cols, width = kv_raw.shape[2], w_q.shape[0]
    groups = tokens // (2 * rows)
    natural = lambda i, s: 2 * (i % groups) + (s[0] + 1 + i // groups) % 2

    def body(
        scalars, gq_ref, gk_ref, gv_ref, q_ref, kv_ref, qg_ref, kg_ref, cos_ref, sin_ref, wq_ref, wk_ref, wv_ref,
        q_out, kv_out, in_out, qg_out, kg_out,
    ):
        step = pl.program_id(0)

        @pl.when(step == 0)
        def _():
            qg_out[...] = jnp.zeros_like(qg_out)
            kg_out[...] = jnp.zeros_like(kg_out)

        cos_rows, sin_rows = cos_ref[...], sin_ref[...]
        for h in range(q_cols // HEAD_SIZE):
            grad = rotate_back(gq_ref[:, head(h)], cos_rows, sin_rows)
            back, gain = norm_back(q_ref[:, head(h)], qg_ref[...], grad)
            q_out[:, head(h)] = b16(back)
            qg_out[...] += gain
        for h in range(kv_cols // HEAD_SIZE):
            grad = rotate_back(gk_ref[:, head(h)], cos_rows, sin_rows)
            back, gain = norm_back(kv_ref[:, head(h)], kg_ref[...], grad)
            kv_out[0, :, head(h)] = b16(back)
            kg_out[...] += gain
        kv_out[1] = b16(gv_ref[...])
        total = dot(q_out[...], wq_ref[...], NT) + dot(kv_out[0], wk_ref[...], NT)
        in_out[...] = b16(total + dot(kv_out[1], wv_ref[...], NT))

    row = lambda cols: pl.BlockSpec((rows, cols), lambda i, s: (natural(i, s), 0))
    gain_spec = pl.BlockSpec((1, HEAD_SIZE), lambda i, s: (0, 0))
    return call(
        body,
        [
            shape((tokens, q_cols)),
            shape((2, tokens, kv_cols)),
            shape((tokens, width)),
            shape((1, HEAD_SIZE), F32),
            shape((1, HEAD_SIZE), F32),
        ],
        (tokens // rows,),
        [
            row(q_cols),
            row(kv_cols),
            row(kv_cols),
            row(q_cols),
            pl.BlockSpec((None, rows, kv_cols), lambda i, s: (0, natural(i, s), 0)),
            whole(q_gain),
            whole(k_gain),
            row(HEAD_SIZE),
            row(HEAD_SIZE),
            whole(w_q),
            whole(w_k),
            whole(w_v),
        ],
        [
            row(q_cols),
            pl.BlockSpec((2, rows, kv_cols), lambda i, s: (0, natural(i, s), 0)),
            pl.BlockSpec((rows, width), lambda i, s: (i, 0)),
            gain_spec,
            gain_spec,
        ],
        (grad_q, grad_k, grad_v, q_raw, kv_raw, q_gain, k_gain, cos, sin, w_q, w_k, w_v),
        "rope_backward",
        2 * tokens * width * (q_cols + 2 * kv_cols),
        scalars,
    )


def input_back(scalars, stream, kept, part, resids, gain):
    rows, width = kept.shape

    def body(scalars, stream_ref, kept_ref, part_ref, first_ref, second_ref, gain_ref, out, gain_out):
        grad = f32(kept_ref[...]) + f32(part_ref[...])
        back, gain_out[...] = norm_back(f32(stream_ref[...]), gain_ref[...], grad)
        resid = jnp.where(scalars[0] == 0, first_ref[...], second_ref[...])
        out[...] = b16(resid + back)

    flat = pl.BlockSpec((rows, width), lambda i, s: (0, 0))
    return call(
        body,
        [shape((rows, width)), shape((1, width), F32)],
        (1,),
        [pl.BlockSpec((rows, width), lambda i, s: (s[1], 0)), flat, flat, flat, flat, whole(gain)],
        [flat, pl.BlockSpec((1, width), lambda i, s: (0, 0))],
        (stream, kept, part, *resids, gain),
        "input_back",
        20 * rows * width,
        scalars,
    )


def split_pair(weights, rows):
    depth, _, cols = weights.shape

    def body(weights_ref, first_out, second_out):
        values = weights_ref[...]
        first_out[...] = values[:, 0, :]
        second_out[...] = values[:, 1, :]

    row = pl.BlockSpec((rows, cols), lambda i: (i, 0))
    return call(
        body,
        [shape((depth, cols)), shape((depth, cols))],
        (depth // rows,),
        [pl.BlockSpec((rows, 2, cols), lambda i: (i, 0, 0))],
        [row, row],
        (weights,),
        "split_pair",
        depth * cols,
    )


def block_order(bits):
    order = [0]
    for bit in reversed(bits[1:]):
        order = order + [k ^ bit for k in order]
    return order


def weight_grad(scalars, left, right, plane, col, cols, bits, ways):
    tokens, width = left.shape
    rows = width // ways
    own = block_order(bits)
    half = len(own) // 2
    order = [k ^ bits[0] for k in own] + own
    count = len(own)

    def source(i, s):
        k = jnp.int32(0)
        for index, value in enumerate(order):
            k = jnp.where(i == index, value, k)
        return k ^ s[0]

    def body(scalars, left_ref, right_ref, send_out, keep_out, next_out):
        step = pl.program_id(0)
        product = b16(dot(left_ref[...], right_ref[...], TN))

        @pl.when(step < count)
        def _():
            send_out[...] = product

        @pl.when((step >= count) & (step < count + half))
        def _():
            keep_out[...] = product

        @pl.when(step >= count + half)
        def _():
            next_out[...] = product

    if right.ndim == 3:
        right_spec = pl.BlockSpec((None, tokens, cols), lambda i, s: (plane, 0, col))
    else:
        right_spec = pl.BlockSpec((tokens, cols), lambda i, s: (0, col))
    return call(
        body,
        [shape((count * rows, cols)), shape((half * rows, cols)), shape((half * rows, cols))],
        (2 * count,),
        [pl.BlockSpec((tokens, rows), lambda i, s: (0, source(i, s))), right_spec],
        [
            pl.BlockSpec((rows, cols), lambda i, s: (jnp.minimum(i, count - 1), 0)),
            pl.BlockSpec((rows, cols), lambda i, s: (jnp.clip(i - count, 0, half - 1), 0)),
            pl.BlockSpec((rows, cols), lambda i, s: (jnp.clip(i - count - half, 0, half - 1), 0)),
        ],
        (left, right),
        "weight_grad",
        2 * tokens * width * cols,
        scalars,
    )


def swap(values, axis, bit):
    ways = lax.axis_size(axis)
    return lax.ppermute(values, axis, [(i, i ^ bit) for i in range(ways)])


def small_sum(values):
    for axis in ("dp", "tensor"):
        ways = lax.axis_size(axis)
        bit = 1
        while bit < ways:
            values = values + swap(values, axis, bit)
            bit *= 2
    return values


class Order:
    def __init__(self):
        self.last = None

    def __call__(self, function, first, *rest, **named):
        if self.last is not None:
            first, _ = lax.optimization_barrier((first, self.last))
        result = function(first, *rest, **named)
        self.last = jax.tree.leaves(result)[-1]
        return result


class Piece:
    def __init__(self, order, scalars, left, right, plane, col, cols, bits, ways):
        self.order, self.bits, self.ways = order, bits, ways
        run = lambda array: weight_grad(scalars, array, right, plane, col, cols, bits, ways)
        self.send, self.keep, self.next = order(run, left)
        self.arrived = swap(self.send, "dp", bits[0])

    def second(self):
        half = self.next.shape[0]
        add = lambda arrived: b16(f32(self.next) + f32(arrived[half:]))
        self.arrived2 = swap(self.order(add, self.arrived), "dp", self.bits[1])

    def third(self):
        half = self.keep.shape[0] // 2
        add = lambda arrived2: b16(
            f32(self.keep[half:]) + f32(self.arrived[half : 2 * half]) + f32(arrived2[half:])
        )
        self.arrived3 = swap(self.order(add, self.arrived2), "dp", self.bits[2])

    def last(self):
        half = self.keep.shape[0] // 2
        add = lambda arrived3: (
            f32(self.keep[:half]) + f32(self.arrived[:half]) + f32(self.arrived2[:half]) + f32(arrived3)
        )
        return self.order(add, self.arrived3)


def per_device(
    stream,
    cotangent,
    live_mask,
    piece_start,
    piece_len,
    norm1_gain,
    w_q,
    key_value_weight,
    q_gain,
    k_gain,
    w_o,
    norm2_gain,
    w_gu,
    w_down,
):
    tokens, width = stream.shape
    pieces = piece_start.shape[1]
    piece_span = SEQ_LEN // pieces
    tensor_ways, dp_ways = lax.axis_size("tensor"), lax.axis_size("dp")
    assert tensor_ways == 4 and tokens == SEQ_LEN and piece_start.shape[0] == 1
    tensor_index, dp_index = lax.axis_index("tensor"), lax.axis_index("dp")
    group, core = tensor_index // 2, tensor_index % 2
    share = tokens // tensor_ways
    kv_cols = key_value_weight.shape[2]
    ff_cols = w_down.shape[1]
    chunk_rows = 2 * share
    reach = [-(-(chunk_rows * (i + 1)) // piece_span) * piece_span for i in range(2)]
    cos, sin = rope_tables()

    live_count = jnp.sum(live_mask)
    ends = piece_start[0] + piece_len[0]
    spans = jnp.stack([piece_start[0], ends], axis=1).reshape(-1)
    scalars = jnp.concatenate([jnp.stack([core, live_count]), spans]).astype(jnp.int32)
    places = jnp.stack([group, tensor_index]).astype(jnp.int32)
    dp_scalar = jnp.stack([dp_index]).astype(jnp.int32)
    gain1, gain2 = norm1_gain[None], norm2_gain[None]
    gain_q, gain_k = q_gain[None], k_gain[None]

    order = Order()
    normed_in, q_raw = order(lambda s: norm_query(s, gain1, w_q, share), stream)
    kv_raw = order(
        lambda n: jnp.einsum("td,dcn->ctn", n, key_value_weight, preferred_element_type=F32), normed_in
    )
    query, key, value = order(
        lambda r: rope_forward(q_raw, r, gain_q, gain_k, cos, sin, share), kv_raw
    )
    attn_own, attn_arrived, mix_own, mix_other = [], [], [], []
    for chunk in range(2):
        own, other, own_mix, other_mix = order(
            lambda q: attend_forward(
                scalars, q, key, value, w_o, chunk, chunk_rows, reach[chunk], pieces
            ),
            query,
        )
        attn_own.append(own)
        mix_own.append(own_mix)
        mix_other.append(other_mix)
        attn_arrived.append(swap(other, "tensor", 1))
    add = lambda own, arrived: b16(f32(own) + f32(arrived))
    chip_attn, part_attn = [], []
    for chunk in range(2):
        chip_attn.append(order(add, attn_own[chunk], attn_arrived[chunk]))
        part_attn.append(swap(chip_attn[chunk], "tensor", 2))
    grad_hidden = order(lambda c: dot(c, w_down), cotangent)
    w_k, w_v = order(lambda w: split_pair(w, share), key_value_weight)
    mixed = order(lambda own: jnp.concatenate([own, mix_own[1]] + mix_other, axis=0), mix_own[0])
    resids, mids_own, mids_other = [], [], []
    for chunk in range(2):
        resid, mid = order(
            lambda part: middle(scalars, stream, chip_attn[chunk], part, gain2, chunk),
            part_attn[chunk],
        )
        resids.append(resid)
        mids_own.append(mid)
        mids_other.append(swap(mid, "tensor", 1))
    mids = order(lambda other: jnp.concatenate(mids_own + [mids_other[0], other], axis=0), mids_other[1])
    gate_up = order(
        lambda m: jnp.einsum("td,dcf->ctf", m, w_gu, preferred_element_type=F32), mids
    )
    hidden, grad_gu = order(lambda gu: gate_back(scalars, gu, grad_hidden, share), gate_up)
    half_ff = ff_cols // 2
    exchange = width // dp_ways % 128 == 0 and dp_ways == 8
    first, other_first = (1, 2, 4), (2, 1, 4)

    def piece(left, right, plane, col, cols, bits):
        return Piece(order, dp_scalar, left, right, plane, col, cols, bits, dp_ways)

    if exchange:
        gate0 = piece(mids, grad_gu, 0, 0, half_ff, first)
        gate1 = piece(mids, grad_gu, 0, 1, half_ff, other_first)
    mid_part = order(
        lambda g: b16(jnp.einsum("ctf,dcf->td", g, w_gu, preferred_element_type=F32)), grad_gu
    )
    half = tokens // 2
    arrived = swap(mid_part[half:], "tensor", 1)
    if exchange:
        up0 = piece(mids, grad_gu, 1, 0, half_ff, first)
    chip_mid = order(add, mid_part[:half], arrived)
    chip_mids = [chip_mid[:share], chip_mid[share:]]
    part_mids = [swap(chip, "tensor", 2) for chip in chip_mids]
    if exchange:
        up1 = piece(mids, grad_gu, 1, 1, half_ff, first)
        down0 = piece(cotangent, hidden, None, 0, half_ff, first)
        down1 = piece(cotangent, hidden, None, 1, half_ff, first)
        gate0.second()
        gate1.second()
    ffn_part = order(lambda h: project_other_first(scalars, h, w_down, share), hidden)
    ffn_arrived = swap(ffn_part[:half], "tensor", 1)

    grad_resids, grads_own, grads_other, gain2_term = [], [], [], 0.0
    for chunk in range(2):
        grad_resid, grad_attn, back_gain = order(
            lambda part: middle_back(
                scalars, resids[chunk], chip_mids[chunk], part, cotangent, gain2, chunk
            ),
            part_mids[chunk],
        )
        grad_resids.append(grad_resid)
        grads_own.append(grad_attn)
        grads_other.append(swap(grad_attn, "tensor", 1))
        gain2_term = gain2_term + back_gain * 0.5
        if exchange and chunk == 0:
            gate0.third()
            up0.second()
    backs = None
    for chunk in range(2):
        backs = order(
            lambda other: attend_backward(
                scalars, grads_own[chunk], other, w_o, query, key, value, backs,
                chunk, chunk_rows, reach[chunk], pieces,
            ),
            grads_other[chunk],
        )
    grad_q, grad_kv, in_part, gain_q_term, gain_k_term = order(
        lambda b: rope_backward(
            scalars, b, backs[1], backs[2], q_raw, kv_raw, gain_q, gain_k, cos, sin, w_q, w_k, w_v, share
        ),
        backs[0],
    )
    in_arrived = swap(in_part[:half], "tensor", 1)
    if exchange:
        gate1.third()
        up1.second()
        query_piece = piece(normed_in, grad_q, None, 0, grad_q.shape[1], first)
        key_piece = piece(normed_in, grad_kv, 0, 0, kv_cols, first)
        value_piece = piece(normed_in, grad_kv, 1, 0, kv_cols, first)

    def scatter(chip):
        kept = lax.dynamic_slice_in_dim(chip, group * share, share, 0)
        sent = lax.dynamic_slice_in_dim(chip, (1 - group) * share, share, 0)
        return kept, swap(sent, "tensor", 2)

    in_kept, in_sum = scatter(order(add, in_part[half:], in_arrived))
    ffn_kept, ffn_sum = scatter(order(add, ffn_part[half:], ffn_arrived))
    grad_attns = order(
        lambda own: jnp.concatenate([own, grads_own[1]] + grads_other, axis=0), grads_own[0]
    )
    if exchange:
        up0.third()
        down0.second()
        out_piece = piece(grad_attns, mixed, None, 0, mixed.shape[1], other_first)
        down1.second()
        up1.third()
        gate_first = gate0.last()
        gate_second = gate1.last()
    grad_stream, gain1_term = order(
        lambda part: input_back(places, stream, in_kept, part, grad_resids, gain1), in_sum
    )
    by_group = lambda pair: jnp.where(group == 0, pair[0], pair[1])

    def finish(part):
        ffn = f32(ffn_kept) + f32(part)
        attn = by_group([f32(chip_attn[i]) + f32(part_attn[i]) for i in range(2)])
        block_out = by_group(resids) + ffn
        live = lax.dynamic_slice_in_dim(live_mask, tensor_index * share, share, 0)
        live = f32(live)[:, None]
        terms = [jnp.sum(live * values * values) for values in (block_out, attn, ffn)]
        return b16(block_out), jnp.stack(terms + [jnp.sum(live)])

    block_out, stat_terms = order(finish, ffn_sum)
    packed = jnp.concatenate(
        [
            gain1_term[0],
            gain2_term[0],
            gain_q_term[0],
            gain_k_term[0],
            jnp.pad(stat_terms, (0, HEAD_SIZE - 4)),
        ]
    ).reshape(-1, HEAD_SIZE)
    totals = small_sum(packed).reshape(-1)
    cuts = (width, 2 * width, 2 * width + HEAD_SIZE, 2 * width + 2 * HEAD_SIZE)
    stat_total = totals[cuts[3] : cuts[3] + 4]
    stats = jnp.sqrt(stat_total[:3] / (stat_total[3] * MODEL_WIDTH))
    if exchange:
        down0.third()
        up_first = up0.last()
        query_piece.second()
        down1.third()
        up_second = up1.last()
        key_piece.second()
        value_piece.second()
        down_first = down0.last()
        query_piece.third()
        down_second = down1.last()
        key_piece.third()
        value_piece.third()
        out_piece.second()
        grad_w_q = query_piece.last()
        out_piece.third()
        grad_w_k, grad_w_v = key_piece.last(), value_piece.last()
        grad_w_o = out_piece.last()
        join = lambda a, b: jnp.concatenate([a, b], axis=1)
        grad_w_gu = jnp.stack([join(gate_first, gate_second), join(up_first, up_second)], axis=1)
        grad_w_down = join(down_first, down_second)
        grad_w_kv = jnp.stack([grad_w_k, grad_w_v], axis=1)
    else:
        reduced = [
            f32(lax.psum_scatter(b16(dot(left, right, TN)), "dp", scatter_dimension=0, tiled=True))
            for left, right in (
                (normed_in, grad_q),
                (normed_in, grad_kv[0]),
                (normed_in, grad_kv[1]),
                (grad_attns, mixed),
                (mids, grad_gu[0]),
                (mids, grad_gu[1]),
                (cotangent, hidden),
            )
        ]
        grad_w_q, grad_w_k, grad_w_v, grad_w_o, grad_gate, grad_up, grad_w_down = reduced
        grad_w_kv = jnp.stack([grad_w_k, grad_w_v], axis=1)
        grad_w_gu = jnp.stack([grad_gate, grad_up], axis=1)
    return (
        block_out,
        grad_stream,
        grad_w_q,
        grad_w_kv,
        grad_w_o,
        grad_w_gu,
        grad_w_down,
        totals[: cuts[0]],
        totals[cuts[0] : cuts[1]],
        totals[cuts[1] : cuts[2]],
        totals[cuts[2] : cuts[3]],
        stats,
    )


def solution(mesh):
    placed = (
        P("dp", None),
        P("dp", None),
        P("dp"),
        P("dp", None),
        P("dp", None),
        P(),
        P(None, "tensor"),
        P(None, None, "tensor"),
        P(),
        P(),
        P(None, "tensor"),
        P(),
        P(None, None, "tensor"),
        P(None, "tensor"),
    )
    return jax.shard_map(
        per_device,
        mesh=mesh,
        in_specs=placed,
        out_specs=(
            P(("dp", "tensor"), None),
            P(("dp", "tensor"), None),
            P("dp", "tensor"),
            P("dp", None, "tensor"),
            P("dp", "tensor"),
            P("dp", None, "tensor"),
            P("dp", "tensor"),
            P(),
            P(),
            P(),
            P(),
            P(),
        ),
        check_vma=False,
    )
```

```python
import math

import jax
import jax.numpy as jnp
import numpy as np
from jax import lax
from jax.experimental import pallas as pl
from jax.experimental.pallas import tpu as pltpu
from jax.sharding import PartitionSpec as P

MODEL_WIDTH = 2048
HEAD_SIZE = 128
SEQ_LEN = 1024
EPSILON = 1e-06
MASKED = -1e30
SCALE = HEAD_SIZE ** (-0.5)
F32 = jnp.float32
BF16 = jnp.bfloat16
VMEM_BYTES = 60 * 1024 * 1024
NN = (((1,), (0,)), ((), ()))
NT = (((1,), (1,)), ((), ()))
TN = (((0,), (0,)), ((), ()))


def dot(left, right, dims=NN):
    return lax.dot_general(left, right, dims, preferred_element_type=F32)


def f32(values):
    return values.astype(F32)


def b16(values):
    return values.astype(BF16)


def shape(dims, kind=BF16):
    return jax.ShapeDtypeStruct(dims, kind)


def call(body, outs, grid, in_specs, out_specs, args, name, scalars=None, scratch=(), alias=None):
    count = 0 if scalars is None else 1
    return pl.pallas_call(
        body,
        out_shape=outs,
        grid_spec=pltpu.PrefetchScalarGridSpec(
            num_scalar_prefetch=count,
            grid=grid,
            in_specs=in_specs,
            out_specs=out_specs,
            scratch_shapes=scratch,
        ),
        compiler_params=pltpu.CompilerParams(vmem_limit_bytes=VMEM_BYTES),
        cost_estimate=pl.CostEstimate(flops=1024, bytes_accessed=1024, transcendentals=0),
        input_output_aliases=alias or {},
        name=name,
    )(*(() if scalars is None else (scalars,)), *args)


def whole(array):
    dims = array.shape
    return pl.BlockSpec(dims, lambda *_: (0,) * len(dims))


def rms_scale(values):
    return lax.rsqrt(jnp.mean(values * values, axis=-1, keepdims=True) + EPSILON)


def norm_back(values, gain, grad):
    scale = rms_scale(values)
    weighted = grad * gain
    along = jnp.mean(weighted * values, axis=-1, keepdims=True)
    grad_values = scale * weighted - values * (scale * scale * scale * along)
    grad_gain = jnp.sum(grad * (values * scale), axis=0, keepdims=True)
    return grad_values, grad_gain


def rope_tables():
    half = HEAD_SIZE // 2
    inverse = np.exp(np.arange(half) * (-2.0 * math.log(1000000.0) / HEAD_SIZE))
    angles = np.arange(SEQ_LEN)[:, None] * inverse[None, :]
    cos, sin = np.cos(angles), np.sin(angles)
    wide_cos = np.concatenate([cos, cos], axis=1).astype(np.float32)
    wide_sin = np.concatenate([-sin, sin], axis=1).astype(np.float32)
    return wide_cos, wide_sin


def rotate(values, cos, sin):
    return values * cos + pltpu.roll(values, HEAD_SIZE // 2, 1) * sin


def rotate_back(values, cos, sin):
    return values * cos - pltpu.roll(values, HEAD_SIZE // 2, 1) * sin


def head(index):
    return slice(index * HEAD_SIZE, (index + 1) * HEAD_SIZE)


def norm_query(stream, gain, w_q, rows):
    tokens, width = stream.shape
    cols = w_q.shape[1]

    def body(stream_ref, gain_ref, w_ref, normed_ref, query_ref):
        values = f32(stream_ref[...])
        normed = b16(values * rms_scale(values) * gain_ref[...])
        normed_ref[...] = normed
        query_ref[...] = dot(normed, w_ref[...])

    return call(
        body,
        [shape((tokens, width)), shape((tokens, cols), F32)],
        (tokens // rows,),
        [pl.BlockSpec((rows, width), lambda i: (i, 0)), whole(gain), whole(w_q)],
        [pl.BlockSpec((rows, width), lambda i: (i, 0)), pl.BlockSpec((rows, cols), lambda i: (i, 0))],
        (stream, gain, w_q),
        "norm_query",
    )


def rope_forward(q_raw, kv_raw, q_gain, k_gain, cos, sin, rows):
    tokens, q_cols = q_raw.shape
    kv_cols = kv_raw.shape[2]

    def body(q_ref, kv_ref, qg_ref, kg_ref, cos_ref, sin_ref, q_out, k_out, v_out):
        cos_rows, sin_rows = cos_ref[...], sin_ref[...]
        for h in range(q_cols // HEAD_SIZE):
            values = q_ref[:, head(h)]
            q_out[:, head(h)] = b16(rotate(values * rms_scale(values) * qg_ref[...], cos_rows, sin_rows))
        for h in range(kv_cols // HEAD_SIZE):
            values = kv_ref[0, :, head(h)]
            k_out[:, head(h)] = b16(rotate(values * rms_scale(values) * kg_ref[...], cos_rows, sin_rows))
        v_out[...] = b16(kv_ref[1])

    row = lambda cols: pl.BlockSpec((rows, cols), lambda i: (i, 0))
    return call(
        body,
        [shape((tokens, q_cols)), shape((tokens, kv_cols)), shape((tokens, kv_cols))],
        (tokens // rows,),
        [
            row(q_cols),
            pl.BlockSpec((2, rows, kv_cols), lambda i: (0, i, 0)),
            whole(q_gain),
            whole(k_gain),
            row(HEAD_SIZE),
            row(HEAD_SIZE),
        ],
        [row(q_cols), row(kv_cols), row(kv_cols)],
        (q_raw, kv_raw, q_gain, k_gain, cos, sin),
        "rope_forward",
    )


def key_limit(scalars, start, count, pieces):
    position = start + lax.broadcasted_iota(jnp.int32, (count, 1), 0)
    limit = position + 1
    for piece in range(pieces):
        first, last = scalars[2 + 2 * piece], scalars[3 + 2 * piece]
        inside = (position >= first) & (position < last)
        limit = jnp.where(inside, jnp.maximum(limit, last), limit)
    return jnp.minimum(limit, scalars[1])


def soft_weights(query, keys, limit):
    scores = dot(query, keys, NT) * SCALE
    key_pos = lax.broadcasted_iota(jnp.int32, scores.shape, 1)
    scores = jnp.where(key_pos < limit, scores, MASKED)
    shifted = jnp.exp(scores - jnp.max(scores, axis=-1, keepdims=True))
    return shifted / jnp.sum(shifted, axis=-1, keepdims=True)


def attend_forward(scalars, query, key, value, w_o, chunk, count, reach, pieces):
    q_cols, kv_cols, width = query.shape[1], key.shape[1], w_o.shape[0]
    heads, half = q_cols // HEAD_SIZE, count // 2
    repeat = q_cols // kv_cols

    def body(scalars, q_ref, k_ref, v_ref, w_ref, own_out, other_out, own_mix, other_mix, mixed):
        limit = key_limit(scalars, chunk * count, count, pieces)
        for h in range(heads):
            weights = soft_weights(q_ref[:, head(h)], k_ref[:, head(h // repeat)], limit)
            mixed[:, head(h)] = b16(dot(b16(weights), v_ref[:, head(h // repeat)]))
        core = scalars[0]
        other = mixed[pl.ds(pl.multiple_of((1 - core) * half, half), half), :]
        own = mixed[pl.ds(pl.multiple_of(core * half, half), half), :]
        other_mix[...] = other
        own_mix[...] = own
        other_out[...] = b16(dot(other, w_ref[...], NT))
        own_out[...] = b16(dot(own, w_ref[...], NT))

    return call(
        body,
        [shape((half, width)), shape((half, width)), shape((half, q_cols)), shape((half, q_cols))],
        (1,),
        [
            pl.BlockSpec((count, q_cols), lambda i, s: (chunk, 0)),
            pl.BlockSpec((reach, kv_cols), lambda i, s: (0, 0)),
            pl.BlockSpec((reach, kv_cols), lambda i, s: (0, 0)),
            whole(w_o),
        ],
        [
            pl.BlockSpec((half, width), lambda i, s: (0, 0)),
            pl.BlockSpec((half, width), lambda i, s: (0, 0)),
            pl.BlockSpec((half, q_cols), lambda i, s: (0, 0)),
            pl.BlockSpec((half, q_cols), lambda i, s: (0, 0)),
        ],
        (query, key, value, w_o),
        "attend_forward",
        scalars,
        [pltpu.VMEM((count, q_cols), BF16)],
    )


def row_specs(rows, sub, width, chunk):
    steps = rows // sub
    picked = pl.BlockSpec((sub, width), lambda i, s: ((2 * chunk + s[0]) * steps + i, 0))
    return picked, pl.BlockSpec((sub, width), lambda i, s: (i, 0))


def middle(scalars, stream, chip, part, gain, chunk, sub):
    rows, width = chip.shape

    def body(scalars, stream_ref, chip_ref, part_ref, gain_ref, resid_out, normed_out):
        resid = f32(stream_ref[...]) + (f32(chip_ref[...]) + f32(part_ref[...]))
        resid_out[...] = resid
        normed_out[...] = b16(resid * rms_scale(resid) * gain_ref[...])

    picked, row = row_specs(rows, sub, width, chunk)
    return call(
        body,
        [shape((rows, width), F32), shape((rows, width))],
        (rows // sub,),
        [picked, row, row, whole(gain)],
        [row, row],
        (stream, chip, part, gain),
        "middle",
        scalars,
    )


def gate_back(scalars, gate_up, grad_hidden, before, chunk, rows, sub):
    planes, _, cols = gate_up.shape
    tokens = grad_hidden.shape[0]
    steps = rows // sub
    natural = lambda i, s: ((2 * chunk + (s[0] + i // steps) % 2) * steps + i % steps, 0)

    def body(scalars, gu_ref, gh_ref, *rest):
        hidden_out, own_out, other_out = rest[-3:]
        gate, up, grad = gu_ref[0], gu_ref[1], gh_ref[...]
        logistic = 1.0 / (1.0 + jnp.exp(-gate))
        silu = gate * logistic
        hidden_out[...] = b16(silu * up)
        grad_gate = b16(grad * up * logistic * (1.0 + gate * (1.0 - logistic)))
        grad_up = b16(grad * silu)

        @pl.when(pl.program_id(0) < steps)
        def _():
            own_out[0], own_out[1] = grad_gate, grad_up

        @pl.when(pl.program_id(0) >= steps)
        def _():
            other_out[0], other_out[1] = grad_gate, grad_up

    args = [gate_up, grad_hidden]
    specs = [
        pl.BlockSpec((planes, sub, cols), lambda i, s: (0, i, 0)),
        pl.BlockSpec((sub, cols), natural),
    ]
    alias = None
    if before is not None:
        args += list(before)
        specs += [pl.BlockSpec(memory_space=pl.ANY)] * 3
        alias = {3: 0, 4: 1, 5: 2}
    part = shape((planes, tokens // 2, cols))
    return call(
        body,
        [shape((tokens, cols)), part, part],
        (2 * steps,),
        specs,
        [
            pl.BlockSpec((sub, cols), natural),
            pl.BlockSpec((planes, sub, cols), lambda i, s: (0, chunk * steps + jnp.minimum(i, steps - 1), 0)),
            pl.BlockSpec((planes, sub, cols), lambda i, s: (0, chunk * steps + jnp.maximum(i - steps, 0), 0)),
        ],
        args,
        "gate_back",
        scalars,
        (),
        alias,
    )


def by_side(groups, product, other_out, own_out):
    @pl.when(pl.program_id(0) < groups)
    def _():
        other_out[...] = product

    @pl.when(pl.program_id(0) >= groups)
    def _():
        own_out[...] = product


def side_specs(groups, rows, width):
    return [
        pl.BlockSpec((rows, width), lambda i, s: (jnp.minimum(i, groups - 1), 0)),
        pl.BlockSpec((rows, width), lambda i, s: (jnp.maximum(i - groups, 0), 0)),
    ]


def project_other_first(scalars, values, weights, rows):
    tokens, depth = values.shape
    width = weights.shape[0]
    groups = tokens // (2 * rows)
    natural = lambda i, s: 2 * (i % groups) + (s[0] + 1 + i // groups) % 2

    def body(scalars, values_ref, weights_ref, other_out, own_out):
        product = b16(dot(values_ref[...], weights_ref[...], NT))
        by_side(groups, product, other_out, own_out)

    return call(
        body,
        [shape((tokens // 2, width)), shape((tokens // 2, width))],
        (tokens // rows,),
        [pl.BlockSpec((rows, depth), lambda i, s: (natural(i, s), 0)), whole(weights)],
        side_specs(groups, rows, width),
        (values, weights),
        "project",
        scalars,
    )


def add_gain(gain_out, gain):
    @pl.when(pl.program_id(0) == 0)
    def _():
        gain_out[...] = jnp.zeros_like(gain_out)

    gain_out[...] += gain


def middle_back(scalars, resid, chip, part, cotangent, gain, chunk, sub):
    rows, width = resid.shape

    def body(scalars, resid_ref, chip_ref, part_ref, cot_ref, gain_ref, resid_out, attn_out, gain_out):
        grad = f32(chip_ref[...]) + f32(part_ref[...])
        back, gain_part = norm_back(resid_ref[...], gain_ref[...], grad)
        add_gain(gain_out, gain_part)
        total = f32(cot_ref[...]) + back
        resid_out[...] = total
        attn_out[...] = b16(total)

    picked, row = row_specs(rows, sub, width, chunk)
    return call(
        body,
        [shape((rows, width), F32), shape((rows, width)), shape((1, width), F32)],
        (rows // sub,),
        [row, row, row, picked, whole(gain)],
        [row, row, pl.BlockSpec((1, width), lambda i, s: (0, 0))],
        (resid, chip, part, cotangent, gain),
        "middle_back",
        scalars,
    )


def attend_backward(scalars, own, other, w_o, query, key, value, before, chunk, count, reach, pieces):
    tokens, q_cols = query.shape
    kv_cols, width = key.shape[1], w_o.shape[0]
    heads, half = q_cols // HEAD_SIZE, count // 2
    repeat = q_cols // kv_cols
    old = 0 if before is None else before[1].shape[0]

    def body(scalars, own_ref, other_ref, w_ref, q_ref, k_ref, v_ref, *rest):
        olds = rest[: len(rest) - 4]
        q_out, k_out, v_out, mixed = rest[len(rest) - 4 :]
        core = scalars[0]
        w = w_ref[...]
        mixed[pl.ds(pl.multiple_of(core * half, half), half), :] = b16(dot(own_ref[...], w))
        mixed[pl.ds(pl.multiple_of((1 - core) * half, half), half), :] = b16(dot(other_ref[...], w))
        limit = key_limit(scalars, chunk * count, count, pieces)
        for g in range(kv_cols // HEAD_SIZE):
            k_total, v_total = 0.0, 0.0
            for h in range(g * repeat, (g + 1) * repeat):
                q_head, k_head, grad = q_ref[:, head(h)], k_ref[:, head(g)], mixed[:, head(h)]
                weights = soft_weights(q_head, k_head, limit)
                grad_weights = dot(grad, v_ref[:, head(g)], NT)
                delta = jnp.sum(weights * grad_weights, axis=-1, keepdims=True)
                grad_scores = b16(weights * (grad_weights - delta))
                q_out[:, head(h)] = dot(grad_scores, k_head) * SCALE
                k_total = k_total + dot(grad_scores, q_head, TN)
                v_total = v_total + dot(b16(weights), grad, TN)
            k_out[:, head(g)] = k_total * SCALE
            v_out[:, head(g)] = v_total
        if old:
            k_out[:old, :] += olds[1][...]
            v_out[:old, :] += olds[2][...]

    flat = pl.BlockSpec((half, width), lambda i, s: (0, 0))
    keys = pl.BlockSpec((reach, kv_cols), lambda i, s: (0, 0))
    args = [own, other, w_o, query, key, value]
    specs = [flat, flat, whole(w_o), pl.BlockSpec((count, q_cols), lambda i, s: (chunk, 0)), keys, keys]
    alias = None
    if before is not None:
        args += list(before)
        specs += [pl.BlockSpec(memory_space=pl.ANY), whole(before[1]), whole(before[2])]
        alias = {7: 0}
    return call(
        body,
        [shape((tokens, q_cols), F32), shape((reach, kv_cols), F32), shape((reach, kv_cols), F32)],
        (1,),
        specs,
        [pl.BlockSpec((count, q_cols), lambda i, s: (chunk, 0)), keys, keys],
        args,
        "attend_backward",
        scalars,
        [pltpu.VMEM((count, q_cols), BF16)],
        alias,
    )


def rope_backward(scalars, grad_q, grad_k, grad_v, q_raw, kv_raw, q_gain, k_gain, cos, sin, w_q, w_k, w_v, rows):
    tokens, q_cols = q_raw.shape
    kv_cols, width = kv_raw.shape[2], w_q.shape[0]
    all_cols, heads = q_cols + 2 * kv_cols, q_cols // HEAD_SIZE
    groups = tokens // (2 * rows)
    natural = lambda i, s: 2 * (i % groups) + (s[0] + 1 + i // groups) % 2

    def body(
        scalars, gq_ref, gk_ref, gv_ref, q_ref, kv_ref, qg_ref, kg_ref, cos_ref, sin_ref, wq_ref, wk_ref, wv_ref,
        qkv_out, other_out, own_out, qg_out, kg_out,
    ):
        step = pl.program_id(0)

        @pl.when(step == 0)
        def _():
            qg_out[...] = jnp.zeros_like(qg_out)
            kg_out[...] = jnp.zeros_like(kg_out)

        cos_rows, sin_rows = cos_ref[...], sin_ref[...]
        for h in range(q_cols // HEAD_SIZE):
            grad = rotate_back(gq_ref[:, head(h)], cos_rows, sin_rows)
            back, gain = norm_back(q_ref[:, head(h)], qg_ref[...], grad)
            qkv_out[:, head(h)] = b16(back)
            qg_out[...] += gain
        for h in range(kv_cols // HEAD_SIZE):
            grad = rotate_back(gk_ref[:, head(h)], cos_rows, sin_rows)
            back, gain = norm_back(kv_ref[:, head(h)], kg_ref[...], grad)
            qkv_out[:, head(heads + h)] = b16(back)
            kg_out[...] += gain
        qkv_out[:, q_cols + kv_cols :] = b16(gv_ref[...])
        total = dot(qkv_out[:, :q_cols], wq_ref[...], NT)
        total = total + dot(qkv_out[:, q_cols : q_cols + kv_cols], wk_ref[...], NT)
        total = total + dot(qkv_out[:, q_cols + kv_cols :], wv_ref[...], NT)
        by_side(groups, b16(total), other_out, own_out)

    row = lambda cols: pl.BlockSpec((rows, cols), lambda i, s: (natural(i, s), 0))
    gain_spec = pl.BlockSpec((1, HEAD_SIZE), lambda i, s: (0, 0))
    return call(
        body,
        [
            shape((tokens, all_cols)),
            shape((tokens // 2, width)),
            shape((tokens // 2, width)),
            shape((1, HEAD_SIZE), F32),
            shape((1, HEAD_SIZE), F32),
        ],
        (tokens // rows,),
        [
            row(q_cols),
            row(kv_cols),
            row(kv_cols),
            row(q_cols),
            pl.BlockSpec((None, rows, kv_cols), lambda i, s: (0, natural(i, s), 0)),
            whole(q_gain),
            whole(k_gain),
            row(HEAD_SIZE),
            row(HEAD_SIZE),
            whole(w_q),
            whole(w_k),
            whole(w_v),
        ],
        [
            row(all_cols),
            *side_specs(groups, rows, width),
            gain_spec,
            gain_spec,
        ],
        (grad_q, grad_k, grad_v, q_raw, kv_raw, q_gain, k_gain, cos, sin, w_q, w_k, w_v),
        "rope_backward",
        scalars,
    )


def input_back(places, stream, kept, part, resids, gain, sub):
    rows, width = kept.shape

    def body(places, stream_ref, kept_ref, part_ref, first_ref, second_ref, gain_ref, out, gain_out):
        grad = f32(kept_ref[...]) + f32(part_ref[...])
        back, gain_part = norm_back(f32(stream_ref[...]), gain_ref[...], grad)
        add_gain(gain_out, gain_part)
        resid = jnp.where(places[0] == 0, first_ref[...], second_ref[...])
        out[...] = b16(resid + back)

    steps = rows // sub
    row = pl.BlockSpec((sub, width), lambda i, s: (i, 0))
    return call(
        body,
        [shape((rows, width)), shape((1, width), F32)],
        (steps,),
        [pl.BlockSpec((sub, width), lambda i, s: (s[1] * steps + i, 0)), row, row, row, row, whole(gain)],
        [row, pl.BlockSpec((1, width), lambda i, s: (0, 0))],
        (stream, kept, part, *resids, gain),
        "input_back",
        places,
    )


def layer_out(places, kept, part, resids, chips, parts, sub):
    rows, width = kept.shape
    steps = rows // sub

    def body(places, kept_ref, part_ref, *rest):
        resid_refs, chip_refs, part_refs = rest[0:2], rest[2:4], rest[4:6]
        out, sums_out = rest[6:]
        first = places[0] == 0
        ffn = f32(kept_ref[...]) + f32(part_ref[...])
        attns = [f32(chip_refs[i][...]) + f32(part_refs[i][...]) for i in range(2)]
        attn = jnp.where(first, attns[0], attns[1])
        total = jnp.where(first, resid_refs[0][...], resid_refs[1][...]) + ffn
        out[...] = b16(total)
        position = places[1] * rows + pl.program_id(0) * sub + lax.broadcasted_iota(jnp.int32, (sub, 1), 0)
        live = position < places[2]
        for index, values in enumerate((total, attn, ffn)):
            rows_sum = jnp.sum(jnp.where(live, values * values, 0.0), axis=1, keepdims=True)
            one = jnp.sum(rows_sum, axis=0, keepdims=True)
            add_row(sums_out, index, one)
        add_row(sums_out, 3, jnp.sum(jnp.where(live, 1.0, 0.0), axis=0, keepdims=True))

    row = pl.BlockSpec((sub, width), lambda i, s: (i, 0))
    return call(
        body,
        [shape((rows, width)), shape((8, HEAD_SIZE), F32)],
        (steps,),
        [row] * 8,
        [row, pl.BlockSpec((8, HEAD_SIZE), lambda i, s: (0, 0))],
        (kept, part, *resids, *chips, *parts),
        "layer_out",
        places,
    )


def add_row(sums_out, index, one):
    wide = jnp.broadcast_to(one, (1, HEAD_SIZE))

    @pl.when(pl.program_id(0) == 0)
    def _():
        sums_out[index : index + 1, :] = wide

    @pl.when(pl.program_id(0) > 0)
    def _():
        sums_out[index : index + 1, :] += wide


def split_pair(weights, rows):
    depth, _, cols = weights.shape

    def body(weights_ref, first_out, second_out):
        values = weights_ref[...]
        first_out[...] = values[:, 0, :]
        second_out[...] = values[:, 1, :]

    row = pl.BlockSpec((rows, cols), lambda i: (i, 0))
    return call(
        body,
        [shape((depth, cols)), shape((depth, cols))],
        (depth // rows,),
        [pl.BlockSpec((rows, 2, cols), lambda i: (i, 0, 0))],
        [row, row],
        (weights,),
        "split_pair",
    )


def block_order(bits):
    order = [0]
    for bit in reversed(bits[1:]):
        order = order + [k ^ bit for k in order]
    return order


def weight_grad(scalars, pairs, col, cols, bits, ways):
    width = pairs[0][0].shape[1]
    rows = width // ways
    own = block_order(bits)
    count, half = len(own), len(own) // 2

    def source(index):
        def place(i, s):
            return (0, (own[index] ^ jnp.where(i == 0, bits[0], 0)) ^ s[0])

        return place

    args, specs = [], []
    for left, right, plane, block in pairs:
        depth = left.shape[0]
        args += [left] * count + [right]
        specs += [pl.BlockSpec((depth, rows), source(index)) for index in range(count)]
        if plane is None:
            specs.append(pl.BlockSpec((depth, cols), lambda i, s, b=block: (b, col)))
        else:
            specs.append(pl.BlockSpec((None, depth, cols), lambda i, s, p=plane, b=block: (p, b, col)))

    def body(scalars, *refs):
        send_out, keep_out, next_out = refs[-3:]
        total = 0.0
        for index in range(len(pairs)):
            part = refs[index * (count + 1) : (index + 1) * (count + 1)]
            left = jnp.concatenate([ref[...] for ref in part[:-1]], axis=1)
            total = total + dot(left, part[-1][...], TN)
        product = b16(total)

        @pl.when(pl.program_id(0) == 0)
        def _():
            send_out[...] = product

        @pl.when(pl.program_id(0) == 1)
        def _():
            keep_out[...] = product[: half * rows]
            next_out[...] = product[half * rows :]

    flat = lambda blocks: pl.BlockSpec((blocks * rows, cols), lambda i, s: (0, 0))
    return call(
        body,
        [shape((count * rows, cols)), shape((half * rows, cols)), shape((half * rows, cols))],
        (2,),
        specs,
        [flat(count), flat(half), flat(half)],
        args,
        "weight_grad",
        scalars,
    )


def swap(values, axis, bit):
    ways = lax.axis_size(axis)
    return lax.ppermute(values, axis, [(i, i ^ bit) for i in range(ways)])


class Order:
    def __init__(self):
        self.last = None

    def __call__(self, function, first, *rest, **named):
        if self.last is not None:
            first, _ = lax.optimization_barrier((first, self.last))
        result = function(first, *rest, **named)
        self.last = jax.tree.leaves(result)[-1]
        return result


class Piece:
    def __init__(self, order, scalars, pairs, col, cols, bits, ways):
        self.order, self.bits = order, bits
        run = lambda array: weight_grad(scalars, [(array, *pairs[0][1:])] + pairs[1:], col, cols, bits, ways)
        self.send, self.keep, self.next = order(run, pairs[0][0])
        self.arrived = swap(self.send, "dp", bits[0])

    def second(self):
        half = self.next.shape[0]
        add = lambda arrived: b16(f32(self.next) + f32(arrived[half:]))
        self.arrived2 = swap(self.order(add, self.arrived), "dp", self.bits[1])

    def third(self):
        half = self.keep.shape[0] // 2
        add = lambda arrived2: b16(
            f32(self.keep[half:]) + f32(self.arrived[half : 2 * half]) + f32(arrived2[half:])
        )
        self.arrived3 = swap(self.order(add, self.arrived2), "dp", self.bits[2])

    def last(self):
        half = self.keep.shape[0] // 2
        add = lambda arrived3: (
            f32(self.keep[:half]) + f32(self.arrived[:half]) + f32(self.arrived2[:half]) + f32(arrived3)
        )
        return self.order(add, self.arrived3)


def per_device(
    stream,
    cotangent,
    live_mask,
    piece_start,
    piece_len,
    norm1_gain,
    w_q,
    key_value_weight,
    q_gain,
    k_gain,
    w_o,
    norm2_gain,
    w_gu,
    w_down,
):
    tokens, width = stream.shape
    pieces = piece_start.shape[1]
    piece_span = SEQ_LEN // pieces
    tensor_ways, dp_ways = lax.axis_size("tensor"), lax.axis_size("dp")
    assert tensor_ways == 4 and tokens == SEQ_LEN and piece_start.shape[0] == 1
    tensor_index, dp_index = lax.axis_index("tensor"), lax.axis_index("dp")
    group, core = tensor_index // 2, tensor_index % 2
    share = tokens // tensor_ways
    sub = share // 4
    q_cols, kv_cols = w_q.shape[1], key_value_weight.shape[2]
    ff_cols = w_down.shape[1]
    chunk_rows = 2 * share
    reach = [-(-(chunk_rows * (i + 1)) // piece_span) * piece_span for i in range(2)]
    cos, sin = rope_tables()

    live_count = jnp.sum(live_mask)
    ends = piece_start[0] + piece_len[0]
    spans = jnp.stack([piece_start[0], ends], axis=1).reshape(-1)
    scalars = jnp.concatenate([jnp.stack([core, live_count]), spans]).astype(jnp.int32)
    places = jnp.stack([group, tensor_index, live_count]).astype(jnp.int32)
    dp_scalar = jnp.stack([dp_index]).astype(jnp.int32)
    gain1, gain2 = norm1_gain[None], norm2_gain[None]
    gain_q, gain_k = q_gain[None], k_gain[None]
    both = range(2)

    order = Order()
    normed_in, q_raw = order(lambda s: norm_query(s, gain1, w_q, share // 2), stream)
    kv_raw = order(
        lambda n: jnp.einsum("td,dcn->ctn", n, key_value_weight, preferred_element_type=F32), normed_in
    )
    query, key, value = order(
        lambda r: rope_forward(q_raw, r, gain_q, gain_k, cos, sin, share // 2), kv_raw
    )

    def attend(chunk):
        return order(
            lambda q: attend_forward(scalars, q, key, value, w_o, chunk, chunk_rows, reach[chunk], pieces),
            query,
        )

    add = lambda own, arrived: b16(f32(own) + f32(arrived))
    attn_own, attn_arrived, mix_own, mix_other = [None] * 2, [None] * 2, [None] * 2, [None] * 2
    chip_attn, part_attn = [None] * 2, [None] * 2
    for chunk in both:
        attn_own[chunk], other, mix_own[chunk], mix_other[chunk] = attend(chunk)
        attn_arrived[chunk] = swap(other, "tensor", 1)
        if chunk == 0:
            w_k, w_v = order(lambda w: split_pair(w, share), key_value_weight)
        else:
            grad_hidden = order(lambda c: dot(c, w_down), cotangent)
        chip_attn[chunk] = order(add, attn_own[chunk], attn_arrived[chunk])
        part_attn[chunk] = swap(chip_attn[chunk], "tensor", 2)

    resids, mids_own, mids_other, backs = [], [], [], None
    for chunk in both:
        resid, mid = order(
            lambda part: middle(scalars, stream, chip_attn[chunk], part, gain2, chunk, sub),
            part_attn[chunk],
        )
        other = swap(mid, "tensor", 1)
        resids.append(resid)
        mids_own.append(mid)
        mids_other.append(other)
        mids = order(lambda o: jnp.concatenate([mid, o], axis=0), other)
        gate_up = order(lambda m: jnp.einsum("td,dcf->ctf", m, w_gu, preferred_element_type=F32), mids)
        backs = order(lambda gu: gate_back(scalars, gu, grad_hidden, backs, chunk, share, share // 2), gate_up)
    hidden, gu_own, gu_other = backs

    exchange = width // dp_ways % 128 == 0 and dp_ways == 8
    x_first, z_first = (1, 2, 4), (2, 1, 4)
    half_ff = ff_cols // 2

    def piece(pairs, col, cols, bits):
        return Piece(order, dp_scalar, pairs, col, cols, bits, dp_ways)

    gu_pairs = [
        [
            (mids_own[0], gu_own, plane, 0),
            (mids_own[1], gu_own, plane, 1),
            (mids_other[0], gu_other, plane, 0),
            (mids_other[1], gu_other, plane, 1),
        ]
        for plane in both
    ]
    down_pairs = [(cotangent, hidden, None, 0)]

    def mid_part(grads):
        return order(
            lambda g: b16(jnp.einsum("ctf,dcf->td", g, w_gu, preferred_element_type=F32)), grads
        )

    if exchange:
        gate0 = piece(gu_pairs[0], 0, half_ff, x_first)
        gate1 = piece(gu_pairs[0], 1, half_ff, z_first)
    mid_arrived = swap(mid_part(gu_other), "tensor", 1)
    mid_own = mid_part(gu_own)
    chip_mid, part_mid = [], []
    for chunk in both:
        rows = slice(chunk * share, (chunk + 1) * share)
        chip_mid.append(order(lambda a: add(mid_own[rows], a[rows]), mid_arrived))
        part_mid.append(swap(chip_mid[chunk], "tensor", 2))
    if exchange:
        up0 = piece(gu_pairs[1], 0, half_ff, x_first)
        gate0.second()
        gate1.second()
        up1 = piece(gu_pairs[1], 1, half_ff, z_first)

    grad_resids, grads_own, grads_other, gain2_parts = [None] * 2, [None] * 2, [None] * 2, [None] * 2

    def back_middle(chunk):
        grad_resids[chunk], grads_own[chunk], gain2_parts[chunk] = order(
            lambda part: middle_back(
                scalars, resids[chunk], chip_mid[chunk], part, cotangent, gain2, chunk, sub
            ),
            part_mid[chunk],
        )
        grads_other[chunk] = swap(grads_own[chunk], "tensor", 1)

    def back_attend(chunk, before):
        return order(
            lambda other: attend_backward(
                scalars, grads_own[chunk], other, w_o, query, key, value, before,
                chunk, chunk_rows, reach[chunk], pieces,
            ),
            grads_other[chunk],
        )

    back_middle(0)
    if exchange:
        down0 = piece(down_pairs, 0, half_ff, x_first)
        gate0.third()
    backs = back_attend(0, None)
    back_middle(1)
    if exchange:
        up0.second()
        gate1.third()
    backs = back_attend(1, backs)
    if exchange:
        down1 = piece(down_pairs, 1, half_ff, x_first)
        up0.third()
    grad_qkv, in_other, in_own, gain_q_term, gain_k_term = order(
        lambda b: rope_backward(
            scalars, b, backs[1], backs[2], q_raw, kv_raw, gain_q, gain_k, cos, sin, w_q, w_k, w_v, share
        ),
        backs[0],
    )
    in_arrived = swap(in_other, "tensor", 1)
    if exchange:
        down0.second()
        up1.second()
        query_piece = piece([(normed_in, grad_qkv, None, 0)], 0, q_cols, x_first)

    def scatter(own, arrived):
        def rows(index):
            cut = lambda array: lax.dynamic_slice_in_dim(array, index * share, share, 0)
            return order(lambda a: add(cut(own), cut(a)), arrived)

        sent = swap(rows(1 - group), "tensor", 2)
        return rows(group), sent

    in_kept, in_sum = scatter(in_own, in_arrived)
    ffn_other, ffn_own = order(lambda h: project_other_first(scalars, h, w_down, share), hidden)
    ffn_arrived = swap(ffn_other, "tensor", 1)
    if exchange:
        key_piece = piece([(normed_in, grad_qkv, None, 0)], 1, 2 * kv_cols, x_first)
        up1.third()
        down0.third()
        gate_first = gate0.last()
    ffn_kept, ffn_sum = scatter(ffn_own, ffn_arrived)
    grad_stream, gain1_term = order(
        lambda part: input_back(places, stream, in_kept, part, grad_resids, gain1, sub), in_sum
    )
    if exchange:
        out_pairs = [
            (grads_own[0], mix_own[0], None, 0),
            (grads_own[1], mix_own[1], None, 0),
            (grads_other[0], mix_other[0], None, 0),
            (grads_other[1], mix_other[1], None, 0),
        ]
        out_piece = piece(out_pairs, 0, q_cols, x_first)
        gate_second = gate1.last()
        down1.second()
    block_out, stat_terms = order(
        lambda part: layer_out(places, ffn_kept, part, resids, chip_attn, part_attn, sub), ffn_sum
    )
    packed = order(
        lambda g: jnp.concatenate(
            [g[0], (gain2_parts[0][0] + gain2_parts[1][0]) * 0.5, gain_q_term[0], gain_k_term[0]]
            + [stat_terms[i] for i in range(4)]
        ).reshape(-1, HEAD_SIZE),
        gain1_term,
    )
    small_add = lambda mine, arrived: mine + arrived

    def small(values, axis, bit):
        return order(small_add, values, swap(values, axis, bit))

    packed = small(packed, "tensor", 1)
    packed = small(packed, "tensor", 2)
    if exchange:
        up_first = up0.last()
        down1.third()
        query_piece.second()
        arrived = swap(packed, "dp", 1)
        up_second = up1.last()
        down_first = down0.last()
        key_piece.second()
        query_piece.third()
        packed = order(small_add, packed, arrived)
        arrived = swap(packed, "dp", 2)
        down_second = down1.last()
        out_piece.second()
        key_piece.third()
        packed = order(small_add, packed, arrived)
        arrived = swap(packed, "dp", 4)
        grad_w_q = query_piece.last()
        join = lambda a, b: jnp.concatenate([a, b], axis=1)
        grad_w_gu = jnp.stack([join(gate_first, gate_second), join(up_first, up_second)], axis=1)
        grad_w_down = join(down_first, down_second)
        out_piece.third()
        packed = order(small_add, packed, arrived)
        grad_w_kv = key_piece.last()
        grad_w_o = out_piece.last()
        totals = packed.reshape(-1)
    else:
        bit = 1
        while bit < dp_ways:
            packed = small(packed, "dp", bit)
            bit *= 2
        totals = packed.reshape(-1)

        def reduced(pairs):
            total = sum(
                dot(left, (right if plane is None else right[plane])[block * left.shape[0] :][: left.shape[0]], TN)
                for left, right, plane, block in pairs
            )
            return f32(lax.psum_scatter(b16(total), "dp", scatter_dimension=0, tiled=True))

        qkv = reduced([(normed_in, grad_qkv, None, 0)])
        grad_w_q, grad_w_kv = qkv[:, :q_cols], qkv[:, q_cols:]
        grad_w_o = sum(
            dot(left, right, TN)
            for left, right in zip(grads_own + grads_other, mix_own + mix_other, strict=True)
        )
        grad_w_o = f32(lax.psum_scatter(b16(grad_w_o), "dp", scatter_dimension=0, tiled=True))
        grad_w_gu = jnp.stack([reduced(gu_pairs[0]), reduced(gu_pairs[1])], axis=1)
        grad_w_down = reduced(down_pairs)
    cuts = (width, 2 * width, 2 * width + HEAD_SIZE, 2 * width + 2 * HEAD_SIZE)
    stat_total = totals[cuts[3] :].reshape(4, HEAD_SIZE)[:, 0]
    stats = jnp.sqrt(stat_total[:3] / (stat_total[3] * MODEL_WIDTH))
    return (
        block_out,
        grad_stream,
        grad_w_q,
        grad_w_kv.reshape(-1, 2, kv_cols),
        grad_w_o,
        grad_w_gu,
        grad_w_down,
        totals[: cuts[0]],
        totals[cuts[0] : cuts[1]],
        totals[cuts[1] : cuts[2]],
        totals[cuts[2] : cuts[3]],
        stats,
    )


def solution(mesh):
    placed = (
        P("dp", None),
        P("dp", None),
        P("dp"),
        P("dp", None),
        P("dp", None),
        P(),
        P(None, "tensor"),
        P(None, None, "tensor"),
        P(),
        P(),
        P(None, "tensor"),
        P(),
        P(None, None, "tensor"),
        P(None, "tensor"),
    )
    return jax.shard_map(
        per_device,
        mesh=mesh,
        in_specs=placed,
        out_specs=(
            P(("dp", "tensor"), None),
            P(("dp", "tensor"), None),
            P("dp", "tensor"),
            P("dp", None, "tensor"),
            P("dp", "tensor"),
            P("dp", None, "tensor"),
            P("dp", "tensor"),
            P(),
            P(),
            P(),
            P(),
            P(),
        ),
        check_vma=False,
    )
```

```python
import math

import jax
import jax.numpy as jnp
import numpy as np
from jax import lax
from jax.experimental import pallas as pl
from jax.experimental.pallas import tpu as pltpu
from jax.sharding import PartitionSpec as P

MODEL_WIDTH = 2048
HEAD_SIZE = 128
SEQ_LEN = 1024
EPSILON = 1e-06
MASKED = -1e30
SCALE = HEAD_SIZE ** (-0.5)
F32 = jnp.float32
BF16 = jnp.bfloat16
VMEM_BYTES = 60 * 1024 * 1024
NN = (((1,), (0,)), ((), ()))
NT = (((1,), (1,)), ((), ()))
TN = (((0,), (0,)), ((), ()))
SPLIT = 1
FLIPPED = -1
GATE, UP, DOWN, QKV, ATTN = range(5)
LINE_FIRST = ()
RIDES = {GATE: ("core0",), UP: ("middle0",), DOWN: ("grads0", "middle1"), QKV: ("input0",)}


def dot(left, right, dims=NN):
    return lax.dot_general(left, right, dims, preferred_element_type=F32)


def f32(values):
    return values.astype(F32)


def b16(values):
    return values.astype(BF16)


def shape(dims, kind=BF16):
    return jax.ShapeDtypeStruct(dims, kind)


MESH_IDS = pl.DeviceIdType.MESH


def partner(bit):
    mine = lax.axis_index("tensor")
    return {"tensor": mine + bit * (1 - 2 * (mine // bit % 2))}


def exchange_copies(bits, sources, targets, sems):
    return [
        pltpu.make_async_remote_copy(
            src_ref=source,
            dst_ref=target,
            send_sem=sems.at[0, index],
            recv_sem=sems.at[1, index],
            device_id=partner(bit),
            device_id_type=MESH_IDS,
        )
        for index, (bit, source, target) in enumerate(zip(bits, sources, targets, strict=True))
    ]


def meet(bits):
    barrier = pltpu.get_barrier_semaphore()
    for bit in sorted(set(bits)):
        pl.semaphore_signal(barrier, inc=1, device_id=partner(bit), device_id_type=MESH_IDS)
    pl.semaphore_wait(barrier, len(set(bits)))


def call_with_riders(body, outs, grid, in_specs, out_specs, args, name, riders, ident):
    bits = [bit for _, bit in riders]
    count, inputs, results = len(riders), len(args), len(outs)

    def riding(*refs):
        own_in, sources = refs[:inputs], refs[inputs : inputs + count]
        rest = refs[inputs + count :]
        own_out, targets, sems = rest[:results], rest[results : results + count], rest[-1]

        @pl.when(pl.program_id(0) == 0)
        def _():
            meet(bits)
            for copy in exchange_copies(bits, sources, targets, sems):
                copy.start()

        body(*own_in, *own_out)

        @pl.when(pl.program_id(0) == grid[0] - 1)
        def _():
            for copy in exchange_copies(bits, sources, targets, sems):
                copy.wait()

    far = pl.BlockSpec(memory_space=pl.ANY)
    return pl.pallas_call(
        riding,
        out_shape=list(outs) + [shape(array.shape, array.dtype) for array, _ in riders],
        grid_spec=pltpu.PrefetchScalarGridSpec(
            num_scalar_prefetch=0,
            grid=grid,
            in_specs=list(in_specs) + [far] * count,
            out_specs=list(out_specs) + [far] * count,
            scratch_shapes=[pltpu.SemaphoreType.DMA((2, count))],
        ),
        compiler_params=pltpu.CompilerParams(
            vmem_limit_bytes=VMEM_BYTES, collective_id=ident, has_side_effects=True
        ),
        cost_estimate=pl.CostEstimate(flops=1024, bytes_accessed=1024, transcendentals=0),
        name=name,
    )(*args, *[array for array, _ in riders])


def call(body, outs, grid, in_specs, out_specs, args, name, scalars=None, scratch=(), alias=None):
    count = 0 if scalars is None else 1
    return pl.pallas_call(
        body,
        out_shape=outs,
        grid_spec=pltpu.PrefetchScalarGridSpec(
            num_scalar_prefetch=count,
            grid=grid,
            in_specs=in_specs,
            out_specs=out_specs,
            scratch_shapes=scratch,
        ),
        compiler_params=pltpu.CompilerParams(vmem_limit_bytes=VMEM_BYTES),
        cost_estimate=pl.CostEstimate(flops=1024, bytes_accessed=1024, transcendentals=0),
        input_output_aliases=alias or {},
        name=name,
    )(*(() if scalars is None else (scalars,)), *args)


def whole(array):
    dims = array.shape
    return pl.BlockSpec(dims, lambda *_: (0,) * len(dims))


def rms_scale(values):
    return lax.rsqrt(jnp.mean(values * values, axis=-1, keepdims=True) + EPSILON)


def norm_back(values, gain, grad):
    scale = rms_scale(values)
    weighted = grad * gain
    along = jnp.mean(weighted * values, axis=-1, keepdims=True)
    grad_values = scale * weighted - values * (scale * scale * scale * along)
    grad_gain = jnp.sum(grad * (values * scale), axis=0, keepdims=True)
    return grad_values, grad_gain


def rope_tables():
    half = HEAD_SIZE // 2
    inverse = np.exp(np.arange(half) * (-2.0 * math.log(1000000.0) / HEAD_SIZE))
    angles = np.arange(SEQ_LEN)[:, None] * inverse[None, :]
    cos, sin = np.cos(angles), np.sin(angles)
    wide_cos = np.concatenate([cos, cos], axis=1).astype(np.float32)
    wide_sin = np.concatenate([-sin, sin], axis=1).astype(np.float32)
    return wide_cos, wide_sin


def rotate(values, cos, sin):
    return values * cos + pltpu.roll(values, HEAD_SIZE // 2, 1) * sin


def rotate_back(values, cos, sin):
    return values * cos - pltpu.roll(values, HEAD_SIZE // 2, 1) * sin


def head(index):
    return slice(index * HEAD_SIZE, (index + 1) * HEAD_SIZE)


def norm_query(stream, gain, w_q, rows):
    tokens, width = stream.shape
    cols = w_q.shape[1]

    def body(stream_ref, gain_ref, w_ref, normed_ref, query_ref):
        values = f32(stream_ref[...])
        normed = b16(values * rms_scale(values) * gain_ref[...])
        normed_ref[...] = normed
        query_ref[...] = dot(normed, w_ref[...])

    return call(
        body,
        [shape((tokens, width)), shape((tokens, cols), F32)],
        (tokens // rows,),
        [pl.BlockSpec((rows, width), lambda i: (i, 0)), whole(gain), whole(w_q)],
        [pl.BlockSpec((rows, width), lambda i: (i, 0)), pl.BlockSpec((rows, cols), lambda i: (i, 0))],
        (stream, gain, w_q),
        "norm_query",
    )


def rope_forward(q_raw, kv_raw, q_gain, k_gain, cos, sin, rows):
    tokens, q_cols = q_raw.shape
    kv_cols = kv_raw.shape[2]

    def body(q_ref, kv_ref, qg_ref, kg_ref, cos_ref, sin_ref, q_out, k_out, v_out):
        cos_rows, sin_rows = cos_ref[...], sin_ref[...]
        for h in range(q_cols // HEAD_SIZE):
            values = q_ref[:, head(h)]
            q_out[:, head(h)] = b16(rotate(values * rms_scale(values) * qg_ref[...], cos_rows, sin_rows))
        for h in range(kv_cols // HEAD_SIZE):
            values = kv_ref[0, :, head(h)]
            k_out[:, head(h)] = b16(rotate(values * rms_scale(values) * kg_ref[...], cos_rows, sin_rows))
        v_out[...] = b16(kv_ref[1])

    row = lambda cols: pl.BlockSpec((rows, cols), lambda i: (i, 0))
    return call(
        body,
        [shape((tokens, q_cols)), shape((tokens, kv_cols)), shape((tokens, kv_cols))],
        (tokens // rows,),
        [
            row(q_cols),
            pl.BlockSpec((2, rows, kv_cols), lambda i: (0, i, 0)),
            whole(q_gain),
            whole(k_gain),
            row(HEAD_SIZE),
            row(HEAD_SIZE),
        ],
        [row(q_cols), row(kv_cols), row(kv_cols)],
        (q_raw, kv_raw, q_gain, k_gain, cos, sin),
        "rope_forward",
    )


def key_limit(scalars, start, count, pieces):
    position = start + lax.broadcasted_iota(jnp.int32, (count, 1), 0)
    limit = position + 1
    for piece in range(pieces):
        first, last = scalars[2 + 2 * piece], scalars[3 + 2 * piece]
        inside = (position >= first) & (position < last)
        limit = jnp.where(inside, jnp.maximum(limit, last), limit)
    return jnp.minimum(limit, scalars[1])


def soft_weights(query, keys, limit):
    scores = dot(query, keys, NT) * SCALE
    key_pos = lax.broadcasted_iota(jnp.int32, scores.shape, 1)
    scores = jnp.where(key_pos < limit, scores, MASKED)
    shifted = jnp.exp(scores - jnp.max(scores, axis=-1, keepdims=True))
    return shifted / jnp.sum(shifted, axis=-1, keepdims=True)


def attend_forward(scalars, query, key, value, w_o, chunk, count, reach, pieces):
    q_cols, kv_cols, width = query.shape[1], key.shape[1], w_o.shape[0]
    heads, half = q_cols // HEAD_SIZE, count // 2
    repeat = q_cols // kv_cols

    def body(scalars, q_ref, k_ref, v_ref, w_ref, own_out, other_out, own_mix, other_mix, mixed):
        limit = key_limit(scalars, chunk * count, count, pieces)
        for h in range(heads):
            weights = soft_weights(q_ref[:, head(h)], k_ref[:, head(h // repeat)], limit)
            mixed[:, head(h)] = b16(dot(b16(weights), v_ref[:, head(h // repeat)]))
        core = scalars[0]
        other = mixed[pl.ds(pl.multiple_of((1 - core) * half, half), half), :]
        own = mixed[pl.ds(pl.multiple_of(core * half, half), half), :]
        other_mix[...] = other
        own_mix[...] = own
        other_out[...] = b16(dot(other, w_ref[...], NT))
        own_out[...] = b16(dot(own, w_ref[...], NT))

    return call(
        body,
        [shape((half, width)), shape((half, width)), shape((half, q_cols)), shape((half, q_cols))],
        (1,),
        [
            pl.BlockSpec((count, q_cols), lambda i, s: (chunk, 0)),
            pl.BlockSpec((reach, kv_cols), lambda i, s: (0, 0)),
            pl.BlockSpec((reach, kv_cols), lambda i, s: (0, 0)),
            whole(w_o),
        ],
        [
            pl.BlockSpec((half, width), lambda i, s: (0, 0)),
            pl.BlockSpec((half, width), lambda i, s: (0, 0)),
            pl.BlockSpec((half, q_cols), lambda i, s: (0, 0)),
            pl.BlockSpec((half, q_cols), lambda i, s: (0, 0)),
        ],
        (query, key, value, w_o),
        "attend_forward",
        scalars,
        [pltpu.VMEM((count, q_cols), BF16)],
    )


def row_specs(rows, sub, width, chunk):
    steps = rows // sub
    picked = pl.BlockSpec((sub, width), lambda i, s: ((2 * chunk + s[0]) * steps + i, 0))
    return picked, pl.BlockSpec((sub, width), lambda i, s: (i, 0))


def middle(scalars, stream, chip, part, gain, chunk, sub):
    rows, width = chip.shape

    def body(scalars, stream_ref, chip_ref, part_ref, gain_ref, resid_out, normed_out):
        resid = f32(stream_ref[...]) + (f32(chip_ref[...]) + f32(part_ref[...]))
        resid_out[...] = resid
        normed_out[...] = b16(resid * rms_scale(resid) * gain_ref[...])

    picked, row = row_specs(rows, sub, width, chunk)
    return call(
        body,
        [shape((rows, width), F32), shape((rows, width))],
        (rows // sub,),
        [picked, row, row, whole(gain)],
        [row, row],
        (stream, chip, part, gain),
        "middle",
        scalars,
    )


def gate_back(scalars, gate_up, grad_hidden, before, chunk, rows, sub):
    planes, _, cols = gate_up.shape
    tokens = grad_hidden.shape[0]
    steps = rows // sub
    natural = lambda i, s: ((2 * chunk + (s[0] + i // steps) % 2) * steps + i % steps, 0)

    def body(scalars, gu_ref, gh_ref, *rest):
        hidden_out, own_out, other_out = rest[-3:]
        gate, up, grad = gu_ref[0], gu_ref[1], gh_ref[...]
        logistic = 1.0 / (1.0 + jnp.exp(-gate))
        silu = gate * logistic
        hidden_out[...] = b16(silu * up)
        grad_gate = b16(grad * up * logistic * (1.0 + gate * (1.0 - logistic)))
        grad_up = b16(grad * silu)

        @pl.when(pl.program_id(0) < steps)
        def _():
            own_out[0], own_out[1] = grad_gate, grad_up

        @pl.when(pl.program_id(0) >= steps)
        def _():
            other_out[0], other_out[1] = grad_gate, grad_up

    args = [gate_up, grad_hidden]
    specs = [
        pl.BlockSpec((planes, sub, cols), lambda i, s: (0, i, 0)),
        pl.BlockSpec((sub, cols), natural),
    ]
    alias = None
    if before is not None:
        args += list(before)
        specs += [pl.BlockSpec(memory_space=pl.ANY)] * 3
        alias = {3: 0, 4: 1, 5: 2}
    part = shape((planes, tokens // 2, cols))
    return call(
        body,
        [shape((tokens, cols)), part, part],
        (2 * steps,),
        specs,
        [
            pl.BlockSpec((sub, cols), natural),
            pl.BlockSpec((planes, sub, cols), lambda i, s: (0, chunk * steps + jnp.minimum(i, steps - 1), 0)),
            pl.BlockSpec((planes, sub, cols), lambda i, s: (0, chunk * steps + jnp.maximum(i - steps, 0), 0)),
        ],
        args,
        "gate_back",
        scalars,
        (),
        alias,
    )


def by_side(groups, product, other_outs, own_out):
    @pl.when(pl.program_id(0) < groups)
    def _():
        for index, other_out in enumerate(other_outs):
            cols = other_out.shape[1]
            other_out[...] = product[:, index * cols : (index + 1) * cols]

    @pl.when(pl.program_id(0) >= groups)
    def _():
        own_out[...] = product


def side_specs(groups, rows, width):
    part = pl.BlockSpec((rows, width // SPLIT), lambda i, s: (jnp.minimum(i, groups - 1), 0))
    return [part] * SPLIT + [pl.BlockSpec((rows, width), lambda i, s: (jnp.maximum(i - groups, 0), 0))]


def project_other_first(scalars, values, weights, rows):
    tokens, depth = values.shape
    width = weights.shape[0]
    groups = tokens // (2 * rows)
    natural = lambda i, s: 2 * (i % groups) + (s[0] + 1 + i // groups) % 2

    def body(scalars, values_ref, weights_ref, *outs):
        product = b16(dot(values_ref[...], weights_ref[...], NT))
        by_side(groups, product, outs[:-1], outs[-1])

    return call(
        body,
        [shape((tokens // 2, width // SPLIT))] * SPLIT + [shape((tokens // 2, width))],
        (tokens // rows,),
        [pl.BlockSpec((rows, depth), lambda i, s: (natural(i, s), 0)), whole(weights)],
        side_specs(groups, rows, width),
        (values, weights),
        "project",
        scalars,
    )


def add_gain(gain_out, gain):
    @pl.when(pl.program_id(0) == 0)
    def _():
        gain_out[...] = jnp.zeros_like(gain_out)

    gain_out[...] += gain


def middle_back(scalars, resid, chip, part, cotangent, gain, chunk, sub):
    rows, width = resid.shape

    def body(scalars, resid_ref, chip_ref, part_ref, cot_ref, gain_ref, resid_out, attn_out, gain_out):
        grad = f32(chip_ref[...]) + f32(part_ref[...])
        back, gain_part = norm_back(resid_ref[...], gain_ref[...], grad)
        add_gain(gain_out, gain_part)
        total = f32(cot_ref[...]) + back
        resid_out[...] = total
        attn_out[...] = b16(total)

    picked, row = row_specs(rows, sub, width, chunk)
    return call(
        body,
        [shape((rows, width), F32), shape((rows, width)), shape((1, width), F32)],
        (rows // sub,),
        [row, row, row, picked, whole(gain)],
        [row, row, pl.BlockSpec((1, width), lambda i, s: (0, 0))],
        (resid, chip, part, cotangent, gain),
        "middle_back",
        scalars,
    )


def attend_backward(scalars, own, other, w_o, query, key, value, before, chunk, count, reach, pieces):
    tokens, q_cols = query.shape
    kv_cols, width = key.shape[1], w_o.shape[0]
    heads, half = q_cols // HEAD_SIZE, count // 2
    repeat = q_cols // kv_cols
    old = 0 if before is None else before[1].shape[0]

    def body(scalars, own_ref, other_ref, w_ref, q_ref, k_ref, v_ref, *rest):
        olds = rest[: len(rest) - 4]
        q_out, k_out, v_out, mixed = rest[len(rest) - 4 :]
        core = scalars[0]
        w = w_ref[...]
        mixed[pl.ds(pl.multiple_of(core * half, half), half), :] = b16(dot(own_ref[...], w))
        mixed[pl.ds(pl.multiple_of((1 - core) * half, half), half), :] = b16(dot(other_ref[...], w))
        limit = key_limit(scalars, chunk * count, count, pieces)
        for g in range(kv_cols // HEAD_SIZE):
            k_total, v_total = 0.0, 0.0
            for h in range(g * repeat, (g + 1) * repeat):
                q_head, k_head, grad = q_ref[:, head(h)], k_ref[:, head(g)], mixed[:, head(h)]
                weights = soft_weights(q_head, k_head, limit)
                grad_weights = dot(grad, v_ref[:, head(g)], NT)
                delta = jnp.sum(weights * grad_weights, axis=-1, keepdims=True)
                grad_scores = b16(weights * (grad_weights - delta))
                q_out[:, head(h)] = dot(grad_scores, k_head) * SCALE
                k_total = k_total + dot(grad_scores, q_head, TN)
                v_total = v_total + dot(b16(weights), grad, TN)
            k_out[:, head(g)] = k_total * SCALE
            v_out[:, head(g)] = v_total
        if old:
            k_out[:old, :] += olds[1][...]
            v_out[:old, :] += olds[2][...]

    flat = pl.BlockSpec((half, width), lambda i, s: (0, 0))
    keys = pl.BlockSpec((reach, kv_cols), lambda i, s: (0, 0))
    args = [own, other, w_o, query, key, value]
    specs = [flat, flat, whole(w_o), pl.BlockSpec((count, q_cols), lambda i, s: (chunk, 0)), keys, keys]
    alias = None
    if before is not None:
        args += list(before)
        specs += [pl.BlockSpec(memory_space=pl.ANY), whole(before[1]), whole(before[2])]
        alias = {7: 0}
    return call(
        body,
        [shape((tokens, q_cols), F32), shape((reach, kv_cols), F32), shape((reach, kv_cols), F32)],
        (1,),
        specs,
        [pl.BlockSpec((count, q_cols), lambda i, s: (chunk, 0)), keys, keys],
        args,
        "attend_backward",
        scalars,
        [pltpu.VMEM((count, q_cols), BF16)],
        alias,
    )


def rope_backward(scalars, grad_q, grad_k, grad_v, q_raw, kv_raw, q_gain, k_gain, cos, sin, w_q, w_k, w_v, rows):
    tokens, q_cols = q_raw.shape
    kv_cols, width = kv_raw.shape[2], w_q.shape[0]
    all_cols, heads = q_cols + 2 * kv_cols, q_cols // HEAD_SIZE
    groups = tokens // (2 * rows)
    natural = lambda i, s: 2 * (i % groups) + (s[0] + 1 + i // groups) % 2

    def body(
        scalars, gq_ref, gk_ref, gv_ref, q_ref, kv_ref, qg_ref, kg_ref, cos_ref, sin_ref, wq_ref, wk_ref, wv_ref,
        qkv_out, *outs,
    ):
        *other_outs, own_out, qg_out, kg_out = outs
        step = pl.program_id(0)

        @pl.when(step == 0)
        def _():
            qg_out[...] = jnp.zeros_like(qg_out)
            kg_out[...] = jnp.zeros_like(kg_out)

        cos_rows, sin_rows = cos_ref[...], sin_ref[...]
        for h in range(q_cols // HEAD_SIZE):
            grad = rotate_back(gq_ref[:, head(h)], cos_rows, sin_rows)
            back, gain = norm_back(q_ref[:, head(h)], qg_ref[...], grad)
            qkv_out[:, head(h)] = b16(back)
            qg_out[...] += gain
        for h in range(kv_cols // HEAD_SIZE):
            grad = rotate_back(gk_ref[:, head(h)], cos_rows, sin_rows)
            back, gain = norm_back(kv_ref[:, head(h)], kg_ref[...], grad)
            qkv_out[:, head(heads + h)] = b16(back)
            kg_out[...] += gain
        qkv_out[:, q_cols + kv_cols :] = b16(gv_ref[...])
        total = dot(qkv_out[:, :q_cols], wq_ref[...], NT)
        total = total + dot(qkv_out[:, q_cols : q_cols + kv_cols], wk_ref[...], NT)
        total = total + dot(qkv_out[:, q_cols + kv_cols :], wv_ref[...], NT)
        by_side(groups, b16(total), other_outs, own_out)

    row = lambda cols: pl.BlockSpec((rows, cols), lambda i, s: (natural(i, s), 0))
    gain_spec = pl.BlockSpec((1, HEAD_SIZE), lambda i, s: (0, 0))
    return call(
        body,
        [
            shape((tokens, all_cols)),
            *[shape((tokens // 2, width // SPLIT))] * SPLIT,
            shape((tokens // 2, width)),
            shape((1, HEAD_SIZE), F32),
            shape((1, HEAD_SIZE), F32),
        ],
        (tokens // rows,),
        [
            row(q_cols),
            row(kv_cols),
            row(kv_cols),
            row(q_cols),
            pl.BlockSpec((None, rows, kv_cols), lambda i, s: (0, natural(i, s), 0)),
            whole(q_gain),
            whole(k_gain),
            row(HEAD_SIZE),
            row(HEAD_SIZE),
            whole(w_q),
            whole(w_k),
            whole(w_v),
        ],
        [
            row(all_cols),
            *side_specs(groups, rows, width),
            gain_spec,
            gain_spec,
        ],
        (grad_q, grad_k, grad_v, q_raw, kv_raw, q_gain, k_gain, cos, sin, w_q, w_k, w_v),
        "rope_backward",
        scalars,
    )


def input_back(places, stream, kept, part, resids, gain, sub):
    rows, width = kept.shape

    def body(places, stream_ref, kept_ref, part_ref, first_ref, second_ref, gain_ref, out, gain_out):
        grad = f32(kept_ref[...]) + f32(part_ref[...])
        back, gain_part = norm_back(f32(stream_ref[...]), gain_ref[...], grad)
        add_gain(gain_out, gain_part)
        resid = jnp.where(places[0] == 0, first_ref[...], second_ref[...])
        out[...] = b16(resid + back)

    steps = rows // sub
    row = pl.BlockSpec((sub, width), lambda i, s: (i, 0))
    return call(
        body,
        [shape((rows, width)), shape((1, width), F32)],
        (steps,),
        [pl.BlockSpec((sub, width), lambda i, s: (s[1] * steps + i, 0)), row, row, row, row, whole(gain)],
        [row, pl.BlockSpec((1, width), lambda i, s: (0, 0))],
        (stream, kept, part, *resids, gain),
        "input_back",
        places,
    )


def layer_out(places, kept, part, resids, chips, parts, sub):
    rows, width = kept.shape
    steps = rows // sub

    def body(places, kept_ref, part_ref, *rest):
        resid_refs, chip_refs, part_refs = rest[0:2], rest[2:4], rest[4:6]
        out, sums_out = rest[6:]
        first = places[0] == 0
        ffn = f32(kept_ref[...]) + f32(part_ref[...])
        attns = [f32(chip_refs[i][...]) + f32(part_refs[i][...]) for i in range(2)]
        attn = jnp.where(first, attns[0], attns[1])
        total = jnp.where(first, resid_refs[0][...], resid_refs[1][...]) + ffn
        out[...] = b16(total)
        position = places[1] * rows + pl.program_id(0) * sub + lax.broadcasted_iota(jnp.int32, (sub, 1), 0)
        live = position < places[2]
        for index, values in enumerate((total, attn, ffn)):
            rows_sum = jnp.sum(jnp.where(live, values * values, 0.0), axis=1, keepdims=True)
            one = jnp.sum(rows_sum, axis=0, keepdims=True)
            add_row(sums_out, index, one)
        add_row(sums_out, 3, jnp.sum(jnp.where(live, 1.0, 0.0), axis=0, keepdims=True))

    row = pl.BlockSpec((sub, width), lambda i, s: (i, 0))
    return call(
        body,
        [shape((rows, width)), shape((8, HEAD_SIZE), F32)],
        (steps,),
        [row] * 8,
        [row, pl.BlockSpec((8, HEAD_SIZE), lambda i, s: (0, 0))],
        (kept, part, *resids, *chips, *parts),
        "layer_out",
        places,
    )


def add_row(sums_out, index, one):
    wide = jnp.broadcast_to(one, (1, HEAD_SIZE))

    @pl.when(pl.program_id(0) == 0)
    def _():
        sums_out[index : index + 1, :] = wide

    @pl.when(pl.program_id(0) > 0)
    def _():
        sums_out[index : index + 1, :] += wide


def split_pair(weights, rows):
    depth, _, cols = weights.shape

    def body(weights_ref, first_out, second_out):
        values = weights_ref[...]
        first_out[...] = values[:, 0, :]
        second_out[...] = values[:, 1, :]

    row = pl.BlockSpec((rows, cols), lambda i: (i, 0))
    return call(
        body,
        [shape((depth, cols)), shape((depth, cols))],
        (depth // rows,),
        [pl.BlockSpec((rows, 2, cols), lambda i: (i, 0, 0))],
        [row, row],
        (weights,),
        "split_pair",
    )


def block_order(bits):
    order = [0]
    for bit in reversed(bits[1:]):
        order = order + [k ^ bit for k in order]
    return order


def flipped(index, value):
    bit = 1
    while bit <= value:
        if value & bit:
            index = index + bit * (1 - 2 * (index // bit % 2))
        bit *= 2
    return index


def weight_grad(pairs, col, cols, bits, ways, riders, ident):
    width = pairs[0][0].shape[1]
    rows = width // ways
    own = block_order(bits)
    count, half = len(own), len(own) // 2

    def source(index):
        def place(i):
            mine = flipped(lax.axis_index("dp"), own[index])
            return (0, i * mine + (1 - i) * flipped(mine, bits[0]))

        return place

    args, specs = [], []
    for left, right, plane, block in pairs:
        depth = left.shape[0]
        args += [left] * count + [right]
        specs += [pl.BlockSpec((depth, rows), source(index)) for index in range(count)]
        if plane is None:
            specs.append(pl.BlockSpec((depth, cols), lambda i, b=block: (b, col)))
        else:
            specs.append(pl.BlockSpec((None, depth, cols), lambda i, p=plane, b=block: (p, b, col)))

    def body(*refs):
        send_out, keep_out, next_out = refs[-3:]
        total = 0.0
        for index in range(len(pairs)):
            part = refs[index * (count + 1) : (index + 1) * (count + 1)]
            left = jnp.concatenate([ref[...] for ref in part[:-1]], axis=1)
            total = total + dot(left, part[-1][...], TN)
        product = b16(total)

        @pl.when(pl.program_id(0) == 0)
        def _():
            send_out[...] = product

        @pl.when(pl.program_id(0) == 1)
        def _():
            keep_out[...] = product[: half * rows]
            next_out[...] = product[half * rows :]

    flat = lambda blocks: pl.BlockSpec((blocks * rows, cols), lambda i: (0, 0))
    outs = [shape((count * rows, cols)), shape((half * rows, cols)), shape((half * rows, cols))]
    out_specs = [flat(count), flat(half), flat(half)]
    if riders:
        return call_with_riders(body, outs, (2,), specs, out_specs, args, "weight_grad", riders, ident)
    return call(body, outs, (2,), specs, out_specs, args, "weight_grad")


def add_parts(parts, rows, kind, scalars=None, steps=2):
    parts = [(array if isinstance(array, list) else [array], block) for array, block in parts]
    cols = sum(array.shape[1] for array in parts[0][0])
    sub = rows // steps

    def body(*refs):
        refs = list(refs if scalars is None else refs[1:])
        total = 0.0
        for arrays, _ in parts:
            values = [f32(refs.pop(0)[...]) for _ in arrays]
            total = total + (values[0] if len(values) == 1 else jnp.concatenate(values, axis=1))
        refs[0][...] = total.astype(kind)

    def spec(block, cols):
        if callable(block):
            return pl.BlockSpec((sub, cols), lambda i, s: (block(s) * steps + i, 0))
        if block is FLIPPED:
            return pl.BlockSpec((sub, cols), lambda i, *s: (steps - 1 - i, 0))
        return pl.BlockSpec((sub, cols), lambda i, *s: (block * steps + i, 0))

    return call(
        body,
        shape((rows, cols), kind),
        (steps,),
        [spec(block, array.shape[1]) for arrays, block in parts for array in arrays],
        pl.BlockSpec((sub, cols), lambda i, *s: (i, 0)),
        [array for arrays, _ in parts for array in arrays],
        "add_parts",
        scalars,
    )


def swap(values, axis, bit):
    ways = lax.axis_size(axis)
    return lax.ppermute(values, axis, [(i, i ^ bit) for i in range(ways)])


def core_swap(values, ident):
    def body(in_ref, out_ref, sems):
        meet([1])
        (copy,) = exchange_copies([1], [in_ref], [out_ref], sems)
        copy.start()
        copy.wait()

    return pl.pallas_call(
        body,
        out_shape=shape(values.shape, values.dtype),
        in_specs=[pl.BlockSpec(memory_space=pl.ANY)],
        out_specs=pl.BlockSpec(memory_space=pl.ANY),
        scratch_shapes=[pltpu.SemaphoreType.DMA((2, 1))],
        compiler_params=pltpu.CompilerParams(collective_id=ident, has_side_effects=True),
        cost_estimate=pl.CostEstimate(flops=1024, bytes_accessed=1024, transcendentals=0),
        name="core_swap",
    )(values)


class Order:
    def __init__(self):
        self.last = None

    def __call__(self, function, first, *rest, **named):
        if self.last is not None:
            first, _ = lax.optimization_barrier((first, self.last))
        result = function(first, *rest, **named)
        self.last = jax.tree.leaves(result)[-1]
        return result


class Piece:
    def __init__(self, order, pairs, col, cols, bits, ways, riders, ident):
        self.order, self.bits = order, bits
        run = lambda array: weight_grad(
            [(array, *pairs[0][1:])] + pairs[1:], col, cols, bits, ways, riders, ident
        )
        self.send, self.keep, self.next, *self.rode = order(run, pairs[0][0])
        self.start()

    def start(self):
        self.arrived = swap(self.send, "dp", self.bits[0])


class LinePiece(Piece):
    def second(self):
        add = lambda arrived: add_parts([(arrived, 1), (self.next, 0)], self.next.shape[0], BF16)
        self.far = self.order(add, self.arrived)
        self.arrived2 = lax.ppermute(self.far, "dp", [(0, 2), (1, 3), (6, 4), (7, 5)])

    def third(self):
        add = lambda arrived: add_parts([(arrived, FLIPPED), (self.far, 0)], self.far.shape[0], BF16)
        self.arrived3 = lax.ppermute(self.order(add, self.arrived2), "dp", [(2, 4), (4, 2), (3, 5), (5, 3)])

    def fourth(self):
        half = self.keep.shape[0] // 2
        add = lambda arrived: add_parts([(arrived, 0), (self.arrived, 1), (self.keep, 1)], half, BF16)
        self.arrived4 = swap(self.order(add, self.arrived3), "dp", 2)

    def last(self):
        half = self.keep.shape[0] // 2
        add = lambda arrived: add_parts(
            [(arrived, 0), (self.arrived3, 1), (self.arrived, 0), (self.keep, 0)], half, F32
        )
        return self.order(add, self.arrived4)


class LineFirstPiece(Piece):
    def start(self):
        self.arrived = lax.ppermute(self.send, "dp", [(0, 2), (1, 3), (6, 4), (7, 5)])

    def second(self):
        add = lambda arrived: add_parts([(arrived, FLIPPED), (self.send, 0)], self.send.shape[0], BF16)
        self.arrived2 = lax.ppermute(self.order(add, self.arrived), "dp", [(2, 4), (4, 2), (3, 5), (5, 3)])

    def third(self):
        add = lambda arrived: add_parts([(arrived, 0), (self.next, 0)], self.next.shape[0], BF16)
        self.arrived3 = swap(self.order(add, self.arrived2), "dp", 2)

    def fourth(self):
        half = self.keep.shape[0] // 2
        add = lambda arrived: add_parts([(arrived, 1), (self.arrived2, 3), (self.keep, 1)], half, BF16)
        self.arrived4 = swap(self.order(add, self.arrived3), "dp", 1)

    def last(self):
        half = self.keep.shape[0] // 2
        add = lambda arrived: add_parts(
            [(arrived, 0), (self.arrived3, 0), (self.arrived2, 2), (self.keep, 0)], half, F32
        )
        return self.order(add, self.arrived4)


def per_device(
    stream,
    cotangent,
    live_mask,
    piece_start,
    piece_len,
    norm1_gain,
    w_q,
    key_value_weight,
    q_gain,
    k_gain,
    w_o,
    norm2_gain,
    w_gu,
    w_down,
):
    tokens, width = stream.shape
    pieces = piece_start.shape[1]
    piece_span = SEQ_LEN // pieces
    tensor_ways, dp_ways = lax.axis_size("tensor"), lax.axis_size("dp")
    assert tensor_ways == 4 and tokens == SEQ_LEN and piece_start.shape[0] == 1
    tensor_index = lax.axis_index("tensor")
    group, core = tensor_index // 2, tensor_index % 2
    share = tokens // tensor_ways
    sub = share // 4
    q_cols, kv_cols = w_q.shape[1], key_value_weight.shape[2]
    ff_cols = w_down.shape[1]
    chunk_rows = 2 * share
    reach = [-(-(chunk_rows * (i + 1)) // piece_span) * piece_span for i in range(2)]
    cos, sin = rope_tables()

    live_count = jnp.sum(live_mask)
    ends = piece_start[0] + piece_len[0]
    spans = jnp.stack([piece_start[0], ends], axis=1).reshape(-1)
    scalars = jnp.concatenate([jnp.stack([core, live_count]), spans]).astype(jnp.int32)
    places = jnp.stack([group, tensor_index, live_count]).astype(jnp.int32)
    gain1, gain2 = norm1_gain[None], norm2_gain[None]
    gain_q, gain_k = q_gain[None], k_gain[None]
    both = range(2)

    order = Order()
    normed_in, q_raw = order(lambda s: norm_query(s, gain1, w_q, share // 2), stream)
    kv_raw = order(
        lambda n: jnp.einsum("td,dcn->ctn", n, key_value_weight, preferred_element_type=F32), normed_in
    )
    query, key, value = order(
        lambda r: rope_forward(q_raw, r, gain_q, gain_k, cos, sin, share // 2), kv_raw
    )

    def attend(chunk):
        return order(
            lambda q: attend_forward(scalars, q, key, value, w_o, chunk, chunk_rows, reach[chunk], pieces),
            query,
        )

    def add(arrived, own, block=0):
        return add_parts([(arrived, block), (own, block)], share, BF16, places)

    attn_own, attn_arrived, mix_own, mix_other = [None] * 2, [None] * 2, [None] * 2, [None] * 2
    chip_attn, part_attn = [None] * 2, [None] * 2
    for chunk in both:
        attn_own[chunk], other, mix_own[chunk], mix_other[chunk] = attend(chunk)
        attn_arrived[chunk] = swap(other, "tensor", 1)
        if chunk == 0:
            w_k, w_v = order(lambda w: split_pair(w, share), key_value_weight)
        else:
            grad_hidden = order(lambda c: dot(c, w_down), cotangent)
        chip_attn[chunk] = order(add, attn_arrived[chunk], attn_own[chunk])
        part_attn[chunk] = swap(chip_attn[chunk], "tensor", 2)

    resids, mids_own, mids_other, backs = [], [], [], None
    for chunk in both:
        resid, mid = order(
            lambda part: middle(scalars, stream, chip_attn[chunk], part, gain2, chunk, sub),
            part_attn[chunk],
        )
        other = swap(mid, "tensor", 1)
        resids.append(resid)
        mids_own.append(mid)
        mids_other.append(other)
        mids = order(lambda o: jnp.concatenate([mid, o], axis=0), other)
        gate_up = order(lambda m: jnp.einsum("td,dcf->ctf", m, w_gu, preferred_element_type=F32), mids)
        backs = order(lambda gu: gate_back(scalars, gu, grad_hidden, backs, chunk, share, share // 2), gate_up)
    hidden, gu_own, gu_other = backs

    exchange = width // dp_ways % 128 == 0 and dp_ways == 8
    line, line_first = (1, 4, 2), (4, 2, 1)

    def piece(pairs, col, cols, bits, riders, ident):
        kind = LinePiece if bits == line else LineFirstPiece
        return kind(order, pairs, col, cols, bits, dp_ways, riders, ident)

    gu_pairs = [
        [
            (mids_own[0], gu_own, plane, 0),
            (mids_own[1], gu_own, plane, 1),
            (mids_other[0], gu_other, plane, 0),
            (mids_other[1], gu_other, plane, 1),
        ]
        for plane in both
    ]
    down_pairs = [(cotangent, hidden, None, 0)]

    def mid_part(grads):
        return order(
            lambda g: b16(jnp.einsum("ctf,dcf->td", g, w_gu, preferred_element_type=F32)), grads
        )

    riding = sum(RIDES.values(), ())
    grad_resids, grads_own, grads_other, gain2_parts = [None] * 2, [None] * 2, [None] * 2, [None] * 2
    chip_mid, part_mid, made, pieces_of, done = [None] * 2, [None] * 2, {}, {}, {}

    def start_piece(name):
        if not exchange:
            for ride in RIDES.get(name, ()):
                array, bit = rider(ride)
                landed(ride, swap(array, "tensor", bit))
            return
        pairs, col, cols = {
            GATE: (gu_pairs[0], 0, ff_cols),
            UP: (gu_pairs[1], 0, ff_cols),
            DOWN: (down_pairs, 0, ff_cols),
            QKV: ([(normed_in, made.get("qkv"), None, 0)], 0, q_cols + 2 * kv_cols),
            ATTN: (
                [
                    (grads_own[0], mix_own[0], None, 0),
                    (grads_own[1], mix_own[1], None, 0),
                    (grads_other[0], mix_other[0], None, 0),
                    (grads_other[1], mix_other[1], None, 0),
                ],
                0,
                q_cols,
            ),
        }[name]
        names = RIDES.get(name, ())
        bits = line_first if name in LINE_FIRST else line
        pieces_of[name] = piece(pairs, col, cols, bits, [rider(n) for n in names], 8 + len(pieces_of))
        for rode, arrived in zip(names, pieces_of[name].rode, strict=True):
            landed(rode, arrived)

    def rider(name):
        kind, chunk = name[:-1], int(name[-1])
        if kind == "core":
            return made["mid_part"], 1
        if kind == "input":
            return made["in_other"], 1
        return (chip_mid[chunk], 2) if kind == "middle" else (grads_own[chunk], 1)

    def landed(name, arrived):
        kind, chunk = name[:-1], int(name[-1])
        if kind == "core":
            made["mid_arrived"] = arrived
        elif kind == "input":
            made["in_arrived"] = [arrived]
        elif kind == "middle":
            part_mid[chunk] = arrived
        else:
            grads_other[chunk] = arrived

    def mid_other():
        made["mid_part"] = mid_part(gu_other)
        if "core0" not in riding:
            made["mid_arrived"] = order(lambda part: core_swap(part, 0), made["mid_part"])

    def mid_own():
        made["mid_own"] = mid_part(gu_own)

    def chip_middle(chunk):
        chip_mid[chunk] = order(lambda a: add(a, made["mid_own"], chunk), made["mid_arrived"])
        if f"middle{chunk}" not in riding:
            part_mid[chunk] = swap(chip_mid[chunk], "tensor", 2)

    def back_middle(chunk):
        grad_resids[chunk], grads_own[chunk], gain2_parts[chunk] = order(
            lambda part: middle_back(
                scalars, resids[chunk], chip_mid[chunk], part, cotangent, gain2, chunk, sub
            ),
            part_mid[chunk],
        )
        if f"grads{chunk}" not in riding:
            grads_other[chunk] = order(lambda own: core_swap(own, 1 + chunk), grads_own[chunk])

    def back_attend(chunk):
        made["backs"] = order(
            lambda other: attend_backward(
                scalars, grads_own[chunk], other, w_o, query, key, value, made.get("backs"),
                chunk, chunk_rows, reach[chunk], pieces,
            ),
            grads_other[chunk],
        )

    def rope():
        backs = made["backs"]
        made["qkv"], made["in_other"], made["in_own"], made["gain_q"], made["gain_k"] = order(
            lambda b: rope_backward(
                scalars, b, backs[1], backs[2], q_raw, kv_raw, gain_q, gain_k, cos, sin, w_q, w_k, w_v, share
            ),
            backs[0],
        )

    def scatter(own, arrived):
        def half_sum(block):
            return order(lambda first: add([first] + arrived[1:], own, block), arrived[0])

        sent = swap(half_sum(lambda s: 1 - s[0]), "tensor", 2)
        return half_sum(lambda s: s[0]), sent

    def in_scatter():
        made["in_kept"], made["in_sum"] = scatter(made["in_own"], made["in_arrived"])

    def project():
        *ffn_other, made["ffn_own"] = order(lambda h: project_other_first(scalars, h, w_down, share), hidden)
        made["ffn_arrived"] = [order(lambda part: core_swap(part, 4), part) for part in ffn_other]

    def ffn_scatter():
        made["ffn_kept"], made["ffn_sum"] = scatter(made["ffn_own"], made["ffn_arrived"])

    def stream_back():
        made["grad_stream"], made["gain1"] = order(
            lambda part: input_back(places, stream, made["in_kept"], part, grad_resids, gain1, sub),
            made["in_sum"],
        )

    def block_out():
        made["out"], made["stats"] = order(
            lambda part: layer_out(places, made["ffn_kept"], part, resids, chip_attn, part_attn, sub),
            made["ffn_sum"],
        )

    small_add = lambda mine, arrived: mine + arrived

    def small(axis, bit):
        made["packed"] = order(small_add, made["packed"], swap(made["packed"], axis, bit))

    def pack():
        made["packed"] = order(
            lambda g: jnp.concatenate(
                [g[0], (gain2_parts[0][0] + gain2_parts[1][0]) * 0.5, made["gain_q"][0], made["gain_k"][0]]
                + [made["stats"][i] for i in range(4)]
            ).reshape(-1, HEAD_SIZE),
            made["gain1"],
        )
        small("tensor", 1)
        small("tensor", 2)

    def second(name):
        if exchange:
            pieces_of[name].second()

    def third(name):
        if exchange:
            pieces_of[name].third()

    def fourth(name):
        if exchange:
            pieces_of[name].fourth()

    def last(name):
        if exchange:
            done[name] = pieces_of[name].last()

    def send_small(bit):
        if exchange:
            made["small"] = swap(made["packed"], "dp", bit)

    def add_small():
        if exchange:
            made["packed"] = order(small_add, made["packed"], made["small"])

    mid_other()
    start_piece(GATE)
    mid_own()
    chip_middle(0)
    chip_middle(1)
    start_piece(UP)
    back_middle(0)
    start_piece(DOWN)
    second(GATE)
    back_attend(0)
    back_middle(1)
    back_attend(1)
    third(GATE)
    rope()
    second(UP)
    start_piece(QKV)
    in_scatter()
    fourth(GATE)
    project()
    ffn_scatter()
    stream_back()
    third(UP)
    last(GATE)
    start_piece(ATTN)
    second(DOWN)
    block_out()
    fourth(UP)
    third(DOWN)
    second(QKV)
    last(UP)
    pack()
    send_small(1)
    second(ATTN)
    add_small()
    send_small(2)
    third(QKV)
    add_small()
    send_small(4)
    third(ATTN)
    fourth(DOWN)
    last(DOWN)
    fourth(QKV)
    fourth(ATTN)
    add_small()
    last(QKV)
    last(ATTN)
    if exchange:
        grad_w_o = done[ATTN]
        grad_w_q, grad_w_kv = done[QKV][:, :q_cols], done[QKV][:, q_cols:]
        grad_w_gu = jnp.stack([done[GATE], done[UP]], axis=1)
        grad_w_down = done[DOWN]
        totals = made["packed"].reshape(-1)
    else:
        bit = 1
        while bit < dp_ways:
            small("dp", bit)
            bit *= 2
        totals = made["packed"].reshape(-1)

        def reduced(pairs):
            total = sum(
                dot(left, (right if plane is None else right[plane])[block * left.shape[0] :][: left.shape[0]], TN)
                for left, right, plane, block in pairs
            )
            return f32(lax.psum_scatter(b16(total), "dp", scatter_dimension=0, tiled=True))

        qkv = reduced([(normed_in, made["qkv"], None, 0)])
        grad_w_q, grad_w_kv = qkv[:, :q_cols], qkv[:, q_cols:]
        grad_w_o = sum(
            dot(left, right, TN)
            for left, right in zip(grads_own + grads_other, mix_own + mix_other, strict=True)
        )
        grad_w_o = f32(lax.psum_scatter(b16(grad_w_o), "dp", scatter_dimension=0, tiled=True))
        grad_w_gu = jnp.stack([reduced(gu_pairs[0]), reduced(gu_pairs[1])], axis=1)
        grad_w_down = reduced(down_pairs)
    cuts = (width, 2 * width, 2 * width + HEAD_SIZE, 2 * width + 2 * HEAD_SIZE)
    stat_total = totals[cuts[3] :].reshape(4, HEAD_SIZE)[:, 0]
    stats = jnp.sqrt(stat_total[:3] / (stat_total[3] * MODEL_WIDTH))
    return (
        made["out"],
        made["grad_stream"],
        grad_w_q,
        grad_w_kv.reshape(-1, 2, kv_cols),
        grad_w_o,
        grad_w_gu,
        grad_w_down,
        totals[: cuts[0]],
        totals[cuts[0] : cuts[1]],
        totals[cuts[1] : cuts[2]],
        totals[cuts[2] : cuts[3]],
        stats,
    )


def solution(mesh):
    placed = (
        P("dp", None),
        P("dp", None),
        P("dp"),
        P("dp", None),
        P("dp", None),
        P(),
        P(None, "tensor"),
        P(None, None, "tensor"),
        P(),
        P(),
        P(None, "tensor"),
        P(),
        P(None, None, "tensor"),
        P(None, "tensor"),
    )
    return jax.shard_map(
        per_device,
        mesh=mesh,
        in_specs=placed,
        out_specs=(
            P(("dp", "tensor"), None),
            P(("dp", "tensor"), None),
            P("dp", "tensor"),
            P("dp", None, "tensor"),
            P("dp", "tensor"),
            P("dp", None, "tensor"),
            P("dp", "tensor"),
            P(),
            P(),
            P(),
            P(),
            P(),
        ),
        check_vma=False,
    )
```

```python
import math

import jax
import jax.numpy as jnp
import numpy as np
from jax import lax
from jax.experimental import pallas as pl
from jax.experimental.pallas import tpu as pltpu
from jax.sharding import PartitionSpec as P

MODEL_WIDTH = 2048
HEAD_SIZE = 128
SEQ_LEN = 1024
EPSILON = 1e-06
MASKED = -1e30
SCALE = HEAD_SIZE ** (-0.5)
F32 = jnp.float32
BF16 = jnp.bfloat16
VMEM_BYTES = 60 * 1024 * 1024
NN = (((1,), (0,)), ((), ()))
NT = (((1,), (1,)), ((), ()))
TN = (((0,), (0,)), ((), ()))
SPLIT = 1
FLIPPED = -1
GATE, UP, DOWN, QKV, ATTN = range(5)
LINE_FIRST = (GATE,)
RIDES = {GATE: ("core0",), QKV: ("input0",)}


def dot(left, right, dims=NN):
    return lax.dot_general(left, right, dims, preferred_element_type=F32)


def f32(values):
    return values.astype(F32)


def b16(values):
    return values.astype(BF16)


def shape(dims, kind=BF16):
    return jax.ShapeDtypeStruct(dims, kind)


MESH_IDS = pl.DeviceIdType.MESH


def partner(bit):
    mine = lax.axis_index("tensor")
    return {"tensor": mine + bit * (1 - 2 * (mine // bit % 2))}


def exchange_copies(bits, sources, targets, sems):
    return [
        pltpu.make_async_remote_copy(
            src_ref=source,
            dst_ref=target,
            send_sem=sems.at[0, index],
            recv_sem=sems.at[1, index],
            device_id=partner(bit),
            device_id_type=MESH_IDS,
        )
        for index, (bit, source, target) in enumerate(zip(bits, sources, targets, strict=True))
    ]


def meet(bits):
    barrier = pltpu.get_barrier_semaphore()
    for bit in sorted(set(bits)):
        pl.semaphore_signal(barrier, inc=1, device_id=partner(bit), device_id_type=MESH_IDS)
    pl.semaphore_wait(barrier, len(set(bits)))


def call_with_riders(body, outs, grid, in_specs, out_specs, args, name, riders, ident):
    bits = [bit for _, bit in riders]
    count, inputs, results = len(riders), len(args), len(outs)

    def riding(*refs):
        own_in, sources = refs[:inputs], refs[inputs : inputs + count]
        rest = refs[inputs + count :]
        own_out, targets, sems = rest[:results], rest[results : results + count], rest[-1]

        @pl.when(pl.program_id(0) == 0)
        def _():
            meet(bits)
            for copy in exchange_copies(bits, sources, targets, sems):
                copy.start()

        body(*own_in, *own_out)

        @pl.when(pl.program_id(0) == grid[0] - 1)
        def _():
            for copy in exchange_copies(bits, sources, targets, sems):
                copy.wait()

    far = pl.BlockSpec(memory_space=pl.ANY)
    return pl.pallas_call(
        riding,
        out_shape=list(outs) + [shape(array.shape, array.dtype) for array, _ in riders],
        grid_spec=pltpu.PrefetchScalarGridSpec(
            num_scalar_prefetch=0,
            grid=grid,
            in_specs=list(in_specs) + [far] * count,
            out_specs=list(out_specs) + [far] * count,
            scratch_shapes=[pltpu.SemaphoreType.DMA((2, count))],
        ),
        compiler_params=pltpu.CompilerParams(
            vmem_limit_bytes=VMEM_BYTES, collective_id=ident, has_side_effects=True
        ),
        cost_estimate=pl.CostEstimate(flops=1024, bytes_accessed=1024, transcendentals=0),
        name=name,
    )(*args, *[array for array, _ in riders])


def call(body, outs, grid, in_specs, out_specs, args, name, scalars=None, scratch=(), alias=None):
    count = 0 if scalars is None else 1
    return pl.pallas_call(
        body,
        out_shape=outs,
        grid_spec=pltpu.PrefetchScalarGridSpec(
            num_scalar_prefetch=count,
            grid=grid,
            in_specs=in_specs,
            out_specs=out_specs,
            scratch_shapes=scratch,
        ),
        compiler_params=pltpu.CompilerParams(vmem_limit_bytes=VMEM_BYTES),
        cost_estimate=pl.CostEstimate(flops=1024, bytes_accessed=1024, transcendentals=0),
        input_output_aliases=alias or {},
        name=name,
    )(*(() if scalars is None else (scalars,)), *args)


def whole(array):
    dims = array.shape
    return pl.BlockSpec(dims, lambda *_: (0,) * len(dims))


def rms_scale(values):
    return lax.rsqrt(jnp.mean(values * values, axis=-1, keepdims=True) + EPSILON)


def norm_back(values, gain, grad):
    scale = rms_scale(values)
    weighted = grad * gain
    along = jnp.mean(weighted * values, axis=-1, keepdims=True)
    grad_values = scale * weighted - values * (scale * scale * scale * along)
    grad_gain = jnp.sum(grad * (values * scale), axis=0, keepdims=True)
    return grad_values, grad_gain


def rope_tables():
    half = HEAD_SIZE // 2
    inverse = np.exp(np.arange(half) * (-2.0 * math.log(1000000.0) / HEAD_SIZE))
    angles = np.arange(SEQ_LEN)[:, None] * inverse[None, :]
    cos, sin = np.cos(angles), np.sin(angles)
    wide_cos = np.concatenate([cos, cos], axis=1).astype(np.float32)
    wide_sin = np.concatenate([-sin, sin], axis=1).astype(np.float32)
    return wide_cos, wide_sin


def rotate(values, cos, sin):
    return values * cos + pltpu.roll(values, HEAD_SIZE // 2, 1) * sin


def rotate_back(values, cos, sin):
    return values * cos - pltpu.roll(values, HEAD_SIZE // 2, 1) * sin


def head(index):
    return slice(index * HEAD_SIZE, (index + 1) * HEAD_SIZE)


def norm_query(stream, gain, w_q, rows):
    tokens, width = stream.shape
    cols = w_q.shape[1]

    def body(stream_ref, gain_ref, w_ref, normed_ref, query_ref):
        values = f32(stream_ref[...])
        normed = b16(values * rms_scale(values) * gain_ref[...])
        normed_ref[...] = normed
        query_ref[...] = dot(normed, w_ref[...])

    return call(
        body,
        [shape((tokens, width)), shape((tokens, cols), F32)],
        (tokens // rows,),
        [pl.BlockSpec((rows, width), lambda i: (i, 0)), whole(gain), whole(w_q)],
        [pl.BlockSpec((rows, width), lambda i: (i, 0)), pl.BlockSpec((rows, cols), lambda i: (i, 0))],
        (stream, gain, w_q),
        "norm_query",
    )


def rope_forward(q_raw, kv_raw, q_gain, k_gain, cos, sin, rows):
    tokens, q_cols = q_raw.shape
    kv_cols = kv_raw.shape[2]

    def body(q_ref, kv_ref, qg_ref, kg_ref, cos_ref, sin_ref, q_out, k_out, v_out):
        cos_rows, sin_rows = cos_ref[...], sin_ref[...]
        for h in range(q_cols // HEAD_SIZE):
            values = q_ref[:, head(h)]
            q_out[:, head(h)] = b16(rotate(values * rms_scale(values) * qg_ref[...], cos_rows, sin_rows))
        for h in range(kv_cols // HEAD_SIZE):
            values = kv_ref[0, :, head(h)]
            k_out[:, head(h)] = b16(rotate(values * rms_scale(values) * kg_ref[...], cos_rows, sin_rows))
        v_out[...] = b16(kv_ref[1])

    row = lambda cols: pl.BlockSpec((rows, cols), lambda i: (i, 0))
    return call(
        body,
        [shape((tokens, q_cols)), shape((tokens, kv_cols)), shape((tokens, kv_cols))],
        (tokens // rows,),
        [
            row(q_cols),
            pl.BlockSpec((2, rows, kv_cols), lambda i: (0, i, 0)),
            whole(q_gain),
            whole(k_gain),
            row(HEAD_SIZE),
            row(HEAD_SIZE),
        ],
        [row(q_cols), row(kv_cols), row(kv_cols)],
        (q_raw, kv_raw, q_gain, k_gain, cos, sin),
        "rope_forward",
    )


def key_limit(scalars, start, count, pieces):
    position = start + lax.broadcasted_iota(jnp.int32, (count, 1), 0)
    limit = position + 1
    for piece in range(pieces):
        first, last = scalars[2 + 2 * piece], scalars[3 + 2 * piece]
        inside = (position >= first) & (position < last)
        limit = jnp.where(inside, jnp.maximum(limit, last), limit)
    return jnp.minimum(limit, scalars[1])


def soft_weights(query, keys, limit):
    scores = dot(query, keys, NT) * SCALE
    key_pos = lax.broadcasted_iota(jnp.int32, scores.shape, 1)
    scores = jnp.where(key_pos < limit, scores, MASKED)
    shifted = jnp.exp(scores - jnp.max(scores, axis=-1, keepdims=True))
    return shifted / jnp.sum(shifted, axis=-1, keepdims=True)


def attend_forward(scalars, query, key, value, w_o, chunk, count, reach, pieces):
    q_cols, kv_cols, width = query.shape[1], key.shape[1], w_o.shape[0]
    heads, half = q_cols // HEAD_SIZE, count // 2
    repeat = q_cols // kv_cols

    def body(scalars, q_ref, k_ref, v_ref, w_ref, own_out, other_out, own_mix, other_mix, mixed):
        limit = key_limit(scalars, chunk * count, count, pieces)
        for h in range(heads):
            weights = soft_weights(q_ref[:, head(h)], k_ref[:, head(h // repeat)], limit)
            mixed[:, head(h)] = b16(dot(b16(weights), v_ref[:, head(h // repeat)]))
        core = scalars[0]
        other = mixed[pl.ds(pl.multiple_of((1 - core) * half, half), half), :]
        own = mixed[pl.ds(pl.multiple_of(core * half, half), half), :]
        other_mix[...] = other
        own_mix[...] = own
        other_out[...] = b16(dot(other, w_ref[...], NT))
        own_out[...] = b16(dot(own, w_ref[...], NT))

    return call(
        body,
        [shape((half, width)), shape((half, width)), shape((half, q_cols)), shape((half, q_cols))],
        (1,),
        [
            pl.BlockSpec((count, q_cols), lambda i, s: (chunk, 0)),
            pl.BlockSpec((reach, kv_cols), lambda i, s: (0, 0)),
            pl.BlockSpec((reach, kv_cols), lambda i, s: (0, 0)),
            whole(w_o),
        ],
        [
            pl.BlockSpec((half, width), lambda i, s: (0, 0)),
            pl.BlockSpec((half, width), lambda i, s: (0, 0)),
            pl.BlockSpec((half, q_cols), lambda i, s: (0, 0)),
            pl.BlockSpec((half, q_cols), lambda i, s: (0, 0)),
        ],
        (query, key, value, w_o),
        "attend_forward",
        scalars,
        [pltpu.VMEM((count, q_cols), BF16)],
    )


def row_specs(rows, sub, width, chunk):
    steps = rows // sub
    picked = pl.BlockSpec((sub, width), lambda i, s: ((2 * chunk + s[0]) * steps + i, 0))
    return picked, pl.BlockSpec((sub, width), lambda i, s: (i, 0))


def middle(scalars, stream, chip, part, gain, chunk, sub):
    rows, width = chip.shape

    def body(scalars, stream_ref, chip_ref, part_ref, gain_ref, resid_out, normed_out):
        resid = f32(stream_ref[...]) + (f32(chip_ref[...]) + f32(part_ref[...]))
        resid_out[...] = resid
        normed_out[...] = b16(resid * rms_scale(resid) * gain_ref[...])

    picked, row = row_specs(rows, sub, width, chunk)
    return call(
        body,
        [shape((rows, width), F32), shape((rows, width))],
        (rows // sub,),
        [picked, row, row, whole(gain)],
        [row, row],
        (stream, chip, part, gain),
        "middle",
        scalars,
    )


def gate_back(scalars, gate_up, grad_hidden, before, chunk, rows, sub):
    planes, _, cols = gate_up.shape
    tokens = grad_hidden.shape[0]
    steps = rows // sub
    natural = lambda i, s: ((2 * chunk + (s[0] + i // steps) % 2) * steps + i % steps, 0)

    def body(scalars, gu_ref, gh_ref, *rest):
        hidden_out, own_out, other_out = rest[-3:]
        gate, up, grad = gu_ref[0], gu_ref[1], gh_ref[...]
        logistic = 1.0 / (1.0 + jnp.exp(-gate))
        silu = gate * logistic
        hidden_out[...] = b16(silu * up)
        grad_gate = b16(grad * up * logistic * (1.0 + gate * (1.0 - logistic)))
        grad_up = b16(grad * silu)

        @pl.when(pl.program_id(0) < steps)
        def _():
            own_out[0], own_out[1] = grad_gate, grad_up

        @pl.when(pl.program_id(0) >= steps)
        def _():
            other_out[0], other_out[1] = grad_gate, grad_up

    args = [gate_up, grad_hidden]
    specs = [
        pl.BlockSpec((planes, sub, cols), lambda i, s: (0, i, 0)),
        pl.BlockSpec((sub, cols), natural),
    ]
    alias = None
    if before is not None:
        args += list(before)
        specs += [pl.BlockSpec(memory_space=pl.ANY)] * 3
        alias = {3: 0, 4: 1, 5: 2}
    part = shape((planes, tokens // 2, cols))
    return call(
        body,
        [shape((tokens, cols)), part, part],
        (2 * steps,),
        specs,
        [
            pl.BlockSpec((sub, cols), natural),
            pl.BlockSpec((planes, sub, cols), lambda i, s: (0, chunk * steps + jnp.minimum(i, steps - 1), 0)),
            pl.BlockSpec((planes, sub, cols), lambda i, s: (0, chunk * steps + jnp.maximum(i - steps, 0), 0)),
        ],
        args,
        "gate_back",
        scalars,
        (),
        alias,
    )


def by_side(groups, product, other_outs, own_out):
    @pl.when(pl.program_id(0) < groups)
    def _():
        for index, other_out in enumerate(other_outs):
            cols = other_out.shape[1]
            other_out[...] = product[:, index * cols : (index + 1) * cols]

    @pl.when(pl.program_id(0) >= groups)
    def _():
        own_out[...] = product


def side_specs(groups, rows, width):
    part = pl.BlockSpec((rows, width // SPLIT), lambda i, s: (jnp.minimum(i, groups - 1), 0))
    return [part] * SPLIT + [pl.BlockSpec((rows, width), lambda i, s: (jnp.maximum(i - groups, 0), 0))]


def project_other_first(scalars, values, weights, rows):
    tokens, depth = values.shape
    width = weights.shape[0]
    groups = tokens // (2 * rows)
    natural = lambda i, s: 2 * (i % groups) + (s[0] + 1 + i // groups) % 2

    def body(scalars, values_ref, weights_ref, *outs):
        product = b16(dot(values_ref[...], weights_ref[...], NT))
        by_side(groups, product, outs[:-1], outs[-1])

    return call(
        body,
        [shape((tokens // 2, width // SPLIT))] * SPLIT + [shape((tokens // 2, width))],
        (tokens // rows,),
        [pl.BlockSpec((rows, depth), lambda i, s: (natural(i, s), 0)), whole(weights)],
        side_specs(groups, rows, width),
        (values, weights),
        "project",
        scalars,
    )


def add_gain(gain_out, gain):
    @pl.when(pl.program_id(0) == 0)
    def _():
        gain_out[...] = jnp.zeros_like(gain_out)

    gain_out[...] += gain


def middle_back(scalars, resid, chip, part, cotangent, gain, chunk, sub):
    rows, width = resid.shape

    def body(scalars, resid_ref, chip_ref, part_ref, cot_ref, gain_ref, resid_out, attn_out, gain_out):
        grad = f32(chip_ref[...]) + f32(part_ref[...])
        back, gain_part = norm_back(resid_ref[...], gain_ref[...], grad)
        add_gain(gain_out, gain_part)
        total = f32(cot_ref[...]) + back
        resid_out[...] = total
        attn_out[...] = b16(total)

    picked, row = row_specs(rows, sub, width, chunk)
    return call(
        body,
        [shape((rows, width), F32), shape((rows, width)), shape((1, width), F32)],
        (rows // sub,),
        [row, row, row, picked, whole(gain)],
        [row, row, pl.BlockSpec((1, width), lambda i, s: (0, 0))],
        (resid, chip, part, cotangent, gain),
        "middle_back",
        scalars,
    )


def attend_backward(scalars, own, other, w_o, query, key, value, before, chunk, count, reach, pieces):
    tokens, q_cols = query.shape
    kv_cols, width = key.shape[1], w_o.shape[0]
    heads, half = q_cols // HEAD_SIZE, count // 2
    repeat = q_cols // kv_cols
    old = 0 if before is None else before[1].shape[0]

    def body(scalars, own_ref, other_ref, w_ref, q_ref, k_ref, v_ref, *rest):
        olds = rest[: len(rest) - 4]
        q_out, k_out, v_out, mixed = rest[len(rest) - 4 :]
        core = scalars[0]
        w = w_ref[...]
        mixed[pl.ds(pl.multiple_of(core * half, half), half), :] = b16(dot(own_ref[...], w))
        mixed[pl.ds(pl.multiple_of((1 - core) * half, half), half), :] = b16(dot(other_ref[...], w))
        limit = key_limit(scalars, chunk * count, count, pieces)
        for g in range(kv_cols // HEAD_SIZE):
            k_total, v_total = 0.0, 0.0
            for h in range(g * repeat, (g + 1) * repeat):
                q_head, k_head, grad = q_ref[:, head(h)], k_ref[:, head(g)], mixed[:, head(h)]
                weights = soft_weights(q_head, k_head, limit)
                grad_weights = dot(grad, v_ref[:, head(g)], NT)
                delta = jnp.sum(weights * grad_weights, axis=-1, keepdims=True)
                grad_scores = b16(weights * (grad_weights - delta))
                q_out[:, head(h)] = dot(grad_scores, k_head) * SCALE
                k_total = k_total + dot(grad_scores, q_head, TN)
                v_total = v_total + dot(b16(weights), grad, TN)
            k_out[:, head(g)] = k_total * SCALE
            v_out[:, head(g)] = v_total
        if old:
            k_out[:old, :] += olds[1][...]
            v_out[:old, :] += olds[2][...]

    flat = pl.BlockSpec((half, width), lambda i, s: (0, 0))
    keys = pl.BlockSpec((reach, kv_cols), lambda i, s: (0, 0))
    args = [own, other, w_o, query, key, value]
    specs = [flat, flat, whole(w_o), pl.BlockSpec((count, q_cols), lambda i, s: (chunk, 0)), keys, keys]
    alias = None
    if before is not None:
        args += list(before)
        specs += [pl.BlockSpec(memory_space=pl.ANY), whole(before[1]), whole(before[2])]
        alias = {7: 0}
    return call(
        body,
        [shape((tokens, q_cols), F32), shape((reach, kv_cols), F32), shape((reach, kv_cols), F32)],
        (1,),
        specs,
        [pl.BlockSpec((count, q_cols), lambda i, s: (chunk, 0)), keys, keys],
        args,
        "attend_backward",
        scalars,
        [pltpu.VMEM((count, q_cols), BF16)],
        alias,
    )


def rope_backward(scalars, grad_q, grad_k, grad_v, q_raw, kv_raw, q_gain, k_gain, cos, sin, w_q, w_k, w_v, rows):
    tokens, q_cols = q_raw.shape
    kv_cols, width = kv_raw.shape[2], w_q.shape[0]
    all_cols, heads = q_cols + 2 * kv_cols, q_cols // HEAD_SIZE
    groups = tokens // (2 * rows)
    natural = lambda i, s: 2 * (i % groups) + (s[0] + 1 + i // groups) % 2

    def body(
        scalars, gq_ref, gk_ref, gv_ref, q_ref, kv_ref, qg_ref, kg_ref, cos_ref, sin_ref, wq_ref, wk_ref, wv_ref,
        qkv_out, *outs,
    ):
        *other_outs, own_out, qg_out, kg_out = outs
        step = pl.program_id(0)

        @pl.when(step == 0)
        def _():
            qg_out[...] = jnp.zeros_like(qg_out)
            kg_out[...] = jnp.zeros_like(kg_out)

        cos_rows, sin_rows = cos_ref[...], sin_ref[...]
        for h in range(q_cols // HEAD_SIZE):
            grad = rotate_back(gq_ref[:, head(h)], cos_rows, sin_rows)
            back, gain = norm_back(q_ref[:, head(h)], qg_ref[...], grad)
            qkv_out[:, head(h)] = b16(back)
            qg_out[...] += gain
        for h in range(kv_cols // HEAD_SIZE):
            grad = rotate_back(gk_ref[:, head(h)], cos_rows, sin_rows)
            back, gain = norm_back(kv_ref[:, head(h)], kg_ref[...], grad)
            qkv_out[:, head(heads + h)] = b16(back)
            kg_out[...] += gain
        qkv_out[:, q_cols + kv_cols :] = b16(gv_ref[...])
        total = dot(qkv_out[:, :q_cols], wq_ref[...], NT)
        total = total + dot(qkv_out[:, q_cols : q_cols + kv_cols], wk_ref[...], NT)
        total = total + dot(qkv_out[:, q_cols + kv_cols :], wv_ref[...], NT)
        by_side(groups, b16(total), other_outs, own_out)

    row = lambda cols: pl.BlockSpec((rows, cols), lambda i, s: (natural(i, s), 0))
    gain_spec = pl.BlockSpec((1, HEAD_SIZE), lambda i, s: (0, 0))
    return call(
        body,
        [
            shape((tokens, all_cols)),
            *[shape((tokens // 2, width // SPLIT))] * SPLIT,
            shape((tokens // 2, width)),
            shape((1, HEAD_SIZE), F32),
            shape((1, HEAD_SIZE), F32),
        ],
        (tokens // rows,),
        [
            row(q_cols),
            row(kv_cols),
            row(kv_cols),
            row(q_cols),
            pl.BlockSpec((None, rows, kv_cols), lambda i, s: (0, natural(i, s), 0)),
            whole(q_gain),
            whole(k_gain),
            row(HEAD_SIZE),
            row(HEAD_SIZE),
            whole(w_q),
            whole(w_k),
            whole(w_v),
        ],
        [
            row(all_cols),
            *side_specs(groups, rows, width),
            gain_spec,
            gain_spec,
        ],
        (grad_q, grad_k, grad_v, q_raw, kv_raw, q_gain, k_gain, cos, sin, w_q, w_k, w_v),
        "rope_backward",
        scalars,
    )


def input_back(places, stream, kept, part, resids, gain, sub):
    rows, width = kept.shape

    def body(places, stream_ref, kept_ref, part_ref, first_ref, second_ref, gain_ref, out, gain_out):
        grad = f32(kept_ref[...]) + f32(part_ref[...])
        back, gain_part = norm_back(f32(stream_ref[...]), gain_ref[...], grad)
        add_gain(gain_out, gain_part)
        resid = jnp.where(places[0] == 0, first_ref[...], second_ref[...])
        out[...] = b16(resid + back)

    steps = rows // sub
    row = pl.BlockSpec((sub, width), lambda i, s: (i, 0))
    return call(
        body,
        [shape((rows, width)), shape((1, width), F32)],
        (steps,),
        [pl.BlockSpec((sub, width), lambda i, s: (s[1] * steps + i, 0)), row, row, row, row, whole(gain)],
        [row, pl.BlockSpec((1, width), lambda i, s: (0, 0))],
        (stream, kept, part, *resids, gain),
        "input_back",
        places,
    )


def layer_out(places, kept, part, resids, chips, parts, sub):
    rows, width = kept.shape
    steps = rows // sub

    def body(places, kept_ref, part_ref, *rest):
        resid_refs, chip_refs, part_refs = rest[0:2], rest[2:4], rest[4:6]
        out, sums_out = rest[6:]
        first = places[0] == 0
        ffn = f32(kept_ref[...]) + f32(part_ref[...])
        attns = [f32(chip_refs[i][...]) + f32(part_refs[i][...]) for i in range(2)]
        attn = jnp.where(first, attns[0], attns[1])
        total = jnp.where(first, resid_refs[0][...], resid_refs[1][...]) + ffn
        out[...] = b16(total)
        position = places[1] * rows + pl.program_id(0) * sub + lax.broadcasted_iota(jnp.int32, (sub, 1), 0)
        live = position < places[2]
        for index, values in enumerate((total, attn, ffn)):
            rows_sum = jnp.sum(jnp.where(live, values * values, 0.0), axis=1, keepdims=True)
            one = jnp.sum(rows_sum, axis=0, keepdims=True)
            add_row(sums_out, index, one)
        add_row(sums_out, 3, jnp.sum(jnp.where(live, 1.0, 0.0), axis=0, keepdims=True))

    row = pl.BlockSpec((sub, width), lambda i, s: (i, 0))
    return call(
        body,
        [shape((rows, width)), shape((8, HEAD_SIZE), F32)],
        (steps,),
        [row] * 8,
        [row, pl.BlockSpec((8, HEAD_SIZE), lambda i, s: (0, 0))],
        (kept, part, *resids, *chips, *parts),
        "layer_out",
        places,
    )


def add_row(sums_out, index, one):
    wide = jnp.broadcast_to(one, (1, HEAD_SIZE))

    @pl.when(pl.program_id(0) == 0)
    def _():
        sums_out[index : index + 1, :] = wide

    @pl.when(pl.program_id(0) > 0)
    def _():
        sums_out[index : index + 1, :] += wide


def split_pair(weights, rows):
    depth, _, cols = weights.shape

    def body(weights_ref, first_out, second_out):
        values = weights_ref[...]
        first_out[...] = values[:, 0, :]
        second_out[...] = values[:, 1, :]

    row = pl.BlockSpec((rows, cols), lambda i: (i, 0))
    return call(
        body,
        [shape((depth, cols)), shape((depth, cols))],
        (depth // rows,),
        [pl.BlockSpec((rows, 2, cols), lambda i: (i, 0, 0))],
        [row, row],
        (weights,),
        "split_pair",
    )


def block_order(bits):
    order = [0]
    for bit in reversed(bits[1:]):
        order = order + [k ^ bit for k in order]
    return order


def flipped(index, value):
    bit = 1
    while bit <= value:
        if value & bit:
            index = index + bit * (1 - 2 * (index // bit % 2))
        bit *= 2
    return index


def weight_grad(pairs, col, cols, bits, ways, riders, ident):
    width = pairs[0][0].shape[1]
    rows = width // ways
    own = block_order(bits)
    count, half = len(own), len(own) // 2

    def source(index):
        def place(i):
            mine = flipped(lax.axis_index("dp"), own[index])
            return (0, i * mine + (1 - i) * flipped(mine, bits[0]))

        return place

    args, specs = [], []
    for left, right, plane, block in pairs:
        depth = left.shape[0]
        args += [left] * count + [right]
        specs += [pl.BlockSpec((depth, rows), source(index)) for index in range(count)]
        if plane is None:
            specs.append(pl.BlockSpec((depth, cols), lambda i, b=block: (b, col)))
        else:
            specs.append(pl.BlockSpec((None, depth, cols), lambda i, p=plane, b=block: (p, b, col)))

    def body(*refs):
        send_out, keep_out, next_out = refs[-3:]
        total = 0.0
        for index in range(len(pairs)):
            part = refs[index * (count + 1) : (index + 1) * (count + 1)]
            left = jnp.concatenate([ref[...] for ref in part[:-1]], axis=1)
            total = total + dot(left, part[-1][...], TN)
        product = b16(total)

        @pl.when(pl.program_id(0) == 0)
        def _():
            send_out[...] = product

        @pl.when(pl.program_id(0) == 1)
        def _():
            keep_out[...] = product[: half * rows]
            next_out[...] = product[half * rows :]

    flat = lambda blocks: pl.BlockSpec((blocks * rows, cols), lambda i: (0, 0))
    outs = [shape((count * rows, cols)), shape((half * rows, cols)), shape((half * rows, cols))]
    out_specs = [flat(count), flat(half), flat(half)]
    if riders:
        return call_with_riders(body, outs, (2,), specs, out_specs, args, "weight_grad", riders, ident)
    return call(body, outs, (2,), specs, out_specs, args, "weight_grad")


def add_parts(parts, rows, kind, scalars=None, steps=2):
    parts = [(array if isinstance(array, list) else [array], block) for array, block in parts]
    cols = sum(array.shape[1] for array in parts[0][0])
    sub = rows // steps

    def body(*refs):
        refs = list(refs if scalars is None else refs[1:])
        total = 0.0
        for arrays, _ in parts:
            values = [f32(refs.pop(0)[...]) for _ in arrays]
            total = total + (values[0] if len(values) == 1 else jnp.concatenate(values, axis=1))
        refs[0][...] = total.astype(kind)

    def spec(block, cols):
        if callable(block):
            return pl.BlockSpec((sub, cols), lambda i, s: (block(s) * steps + i, 0))
        if block is FLIPPED:
            return pl.BlockSpec((sub, cols), lambda i, *s: (steps - 1 - i, 0))
        return pl.BlockSpec((sub, cols), lambda i, *s: (block * steps + i, 0))

    return call(
        body,
        shape((rows, cols), kind),
        (steps,),
        [spec(block, array.shape[1]) for arrays, block in parts for array in arrays],
        pl.BlockSpec((sub, cols), lambda i, *s: (i, 0)),
        [array for arrays, _ in parts for array in arrays],
        "add_parts",
        scalars,
    )


def swap(values, axis, bit):
    ways = lax.axis_size(axis)
    return lax.ppermute(values, axis, [(i, i ^ bit) for i in range(ways)])


def core_swap(values, ident):
    def body(in_ref, out_ref, sems):
        meet([1])
        (copy,) = exchange_copies([1], [in_ref], [out_ref], sems)
        copy.start()
        copy.wait()

    return pl.pallas_call(
        body,
        out_shape=shape(values.shape, values.dtype),
        in_specs=[pl.BlockSpec(memory_space=pl.ANY)],
        out_specs=pl.BlockSpec(memory_space=pl.ANY),
        scratch_shapes=[pltpu.SemaphoreType.DMA((2, 1))],
        compiler_params=pltpu.CompilerParams(collective_id=ident, has_side_effects=True),
        cost_estimate=pl.CostEstimate(flops=1024, bytes_accessed=1024, transcendentals=0),
        name="core_swap",
    )(values)


class Order:
    def __init__(self):
        self.last = None

    def __call__(self, function, first, *rest, **named):
        if self.last is not None:
            first, _ = lax.optimization_barrier((first, self.last))
        result = function(first, *rest, **named)
        self.last = jax.tree.leaves(result)[-1]
        return result


class Piece:
    def __init__(self, order, pairs, col, cols, bits, ways, riders, ident):
        self.order, self.bits = order, bits
        run = lambda array: weight_grad(
            [(array, *pairs[0][1:])] + pairs[1:], col, cols, bits, ways, riders, ident
        )
        self.send, self.keep, self.next, *self.rode = order(run, pairs[0][0])
        self.start()

    def start(self):
        self.arrived = swap(self.send, "dp", self.bits[0])


class LinePiece(Piece):
    def second(self):
        add = lambda arrived: add_parts([(arrived, 1), (self.next, 0)], self.next.shape[0], BF16)
        self.far = self.order(add, self.arrived)
        self.arrived2 = lax.ppermute(self.far, "dp", [(0, 2), (1, 3), (6, 4), (7, 5)])

    def third(self):
        add = lambda arrived: add_parts([(arrived, FLIPPED), (self.far, 0)], self.far.shape[0], BF16)
        self.arrived3 = lax.ppermute(self.order(add, self.arrived2), "dp", [(2, 4), (4, 2), (3, 5), (5, 3)])

    def fourth(self):
        half = self.keep.shape[0] // 2
        add = lambda arrived: add_parts([(arrived, 0), (self.arrived, 1), (self.keep, 1)], half, BF16)
        self.arrived4 = swap(self.order(add, self.arrived3), "dp", 2)

    def last(self):
        half = self.keep.shape[0] // 2
        add = lambda arrived: add_parts(
            [(arrived, 0), (self.arrived3, 1), (self.arrived, 0), (self.keep, 0)], half, F32
        )
        return self.order(add, self.arrived4)


class LineFirstPiece(Piece):
    def start(self):
        self.arrived = lax.ppermute(self.send, "dp", [(0, 2), (1, 3), (6, 4), (7, 5)])

    def second(self):
        add = lambda arrived: add_parts([(arrived, FLIPPED), (self.send, 0)], self.send.shape[0], BF16)
        self.arrived2 = lax.ppermute(self.order(add, self.arrived), "dp", [(2, 4), (4, 2), (3, 5), (5, 3)])

    def third(self):
        add = lambda arrived: add_parts([(arrived, 0), (self.next, 0)], self.next.shape[0], BF16)
        self.arrived3 = swap(self.order(add, self.arrived2), "dp", 2)

    def fourth(self):
        half = self.keep.shape[0] // 2
        add = lambda arrived: add_parts([(arrived, 1), (self.arrived2, 3), (self.keep, 1)], half, BF16)
        self.arrived4 = swap(self.order(add, self.arrived3), "dp", 1)

    def last(self):
        half = self.keep.shape[0] // 2
        add = lambda arrived: add_parts(
            [(arrived, 0), (self.arrived3, 0), (self.arrived2, 2), (self.keep, 0)], half, F32
        )
        return self.order(add, self.arrived4)


def per_device(
    stream,
    cotangent,
    live_mask,
    piece_start,
    piece_len,
    norm1_gain,
    w_q,
    key_value_weight,
    q_gain,
    k_gain,
    w_o,
    norm2_gain,
    w_gu,
    w_down,
):
    tokens, width = stream.shape
    pieces = piece_start.shape[1]
    piece_span = SEQ_LEN // pieces
    tensor_ways, dp_ways = lax.axis_size("tensor"), lax.axis_size("dp")
    assert tensor_ways == 4 and tokens == SEQ_LEN and piece_start.shape[0] == 1
    tensor_index = lax.axis_index("tensor")
    group, core = tensor_index // 2, tensor_index % 2
    share = tokens // tensor_ways
    sub = share // 4
    q_cols, kv_cols = w_q.shape[1], key_value_weight.shape[2]
    ff_cols = w_down.shape[1]
    chunk_rows = 2 * share
    reach = [-(-(chunk_rows * (i + 1)) // piece_span) * piece_span for i in range(2)]
    cos, sin = rope_tables()

    live_count = jnp.sum(live_mask)
    ends = piece_start[0] + piece_len[0]
    spans = jnp.stack([piece_start[0], ends], axis=1).reshape(-1)
    scalars = jnp.concatenate([jnp.stack([core, live_count]), spans]).astype(jnp.int32)
    places = jnp.stack([group, tensor_index, live_count]).astype(jnp.int32)
    gain1, gain2 = norm1_gain[None], norm2_gain[None]
    gain_q, gain_k = q_gain[None], k_gain[None]
    both = range(2)

    order = Order()
    normed_in, q_raw = order(lambda s: norm_query(s, gain1, w_q, share // 2), stream)
    kv_raw = order(
        lambda n: jnp.einsum("td,dcn->ctn", n, key_value_weight, preferred_element_type=F32), normed_in
    )
    query, key, value = order(
        lambda r: rope_forward(q_raw, r, gain_q, gain_k, cos, sin, share // 2), kv_raw
    )

    def attend(chunk):
        return order(
            lambda q: attend_forward(scalars, q, key, value, w_o, chunk, chunk_rows, reach[chunk], pieces),
            query,
        )

    def add(arrived, own, block=0):
        return add_parts([(arrived, block), (own, block)], share, BF16, places)

    attn_own, attn_arrived, mix_own, mix_other = [None] * 2, [None] * 2, [None] * 2, [None] * 2
    chip_attn, part_attn = [None] * 2, [None] * 2
    for chunk in both:
        attn_own[chunk], other, mix_own[chunk], mix_other[chunk] = attend(chunk)
        attn_arrived[chunk] = swap(other, "tensor", 1)
        if chunk == 0:
            w_k, w_v = order(lambda w: split_pair(w, share), key_value_weight)
        else:
            grad_hidden = order(lambda c: dot(c, w_down), cotangent)
        chip_attn[chunk] = order(add, attn_arrived[chunk], attn_own[chunk])
        part_attn[chunk] = swap(chip_attn[chunk], "tensor", 2)

    resids, mids_own, mids_other, backs = [], [], [], None
    for chunk in both:
        resid, mid = order(
            lambda part: middle(scalars, stream, chip_attn[chunk], part, gain2, chunk, sub),
            part_attn[chunk],
        )
        other = swap(mid, "tensor", 1)
        resids.append(resid)
        mids_own.append(mid)
        mids_other.append(other)
        mids = order(lambda o: jnp.concatenate([mid, o], axis=0), other)
        gate_up = order(lambda m: jnp.einsum("td,dcf->ctf", m, w_gu, preferred_element_type=F32), mids)
        backs = order(lambda gu: gate_back(scalars, gu, grad_hidden, backs, chunk, share, share // 2), gate_up)
    hidden, gu_own, gu_other = backs

    exchange = width // dp_ways % 128 == 0 and dp_ways == 8
    line, line_first = (1, 4, 2), (4, 2, 1)

    def piece(pairs, col, cols, bits, riders, ident):
        kind = LinePiece if bits == line else LineFirstPiece
        return kind(order, pairs, col, cols, bits, dp_ways, riders, ident)

    gu_pairs = [
        [
            (mids_own[0], gu_own, plane, 0),
            (mids_own[1], gu_own, plane, 1),
            (mids_other[0], gu_other, plane, 0),
            (mids_other[1], gu_other, plane, 1),
        ]
        for plane in both
    ]
    down_pairs = [(cotangent, hidden, None, 0)]

    def mid_part(grads):
        return order(
            lambda g: b16(jnp.einsum("ctf,dcf->td", g, w_gu, preferred_element_type=F32)), grads
        )

    riding = sum(RIDES.values(), ())
    grad_resids, grads_own, grads_other, gain2_parts = [None] * 2, [None] * 2, [None] * 2, [None] * 2
    chip_mid, part_mid, made, pieces_of, done = [None] * 2, [None] * 2, {}, {}, {}

    def start_piece(name):
        if not exchange:
            for ride in RIDES.get(name, ()):
                array, bit = rider(ride)
                landed(ride, swap(array, "tensor", bit))
            return
        pairs, col, cols = {
            GATE: (gu_pairs[0], 0, ff_cols),
            UP: (gu_pairs[1], 0, ff_cols),
            DOWN: (down_pairs, 0, ff_cols),
            QKV: ([(normed_in, made.get("qkv"), None, 0)], 0, q_cols + 2 * kv_cols),
            ATTN: (
                [
                    (grads_own[0], mix_own[0], None, 0),
                    (grads_own[1], mix_own[1], None, 0),
                    (grads_other[0], mix_other[0], None, 0),
                    (grads_other[1], mix_other[1], None, 0),
                ],
                0,
                q_cols,
            ),
        }[name]
        names = RIDES.get(name, ())
        bits = line_first if name in LINE_FIRST else line
        pieces_of[name] = piece(pairs, col, cols, bits, [rider(n) for n in names], 8 + len(pieces_of))
        for rode, arrived in zip(names, pieces_of[name].rode, strict=True):
            landed(rode, arrived)

    def rider(name):
        kind, chunk = name[:-1], int(name[-1])
        if kind == "core":
            return made["mid_part"], 1
        if kind == "input":
            return made["in_other"], 1
        return (chip_mid[chunk], 2) if kind == "middle" else (grads_own[chunk], 1)

    def landed(name, arrived):
        kind, chunk = name[:-1], int(name[-1])
        if kind == "core":
            made["mid_arrived"] = arrived
        elif kind == "input":
            made["in_arrived"] = [arrived]
        elif kind == "middle":
            part_mid[chunk] = arrived
        else:
            grads_other[chunk] = arrived

    def mid_other():
        made["mid_part"] = mid_part(gu_other)
        if "core0" not in riding:
            made["mid_arrived"] = order(lambda part: core_swap(part, 0), made["mid_part"])

    def mid_own():
        made["mid_own"] = mid_part(gu_own)

    def chip_middle(chunk):
        chip_mid[chunk] = order(lambda a: add(a, made["mid_own"], chunk), made["mid_arrived"])
        if f"middle{chunk}" not in riding:
            part_mid[chunk] = swap(chip_mid[chunk], "tensor", 2)

    def back_middle(chunk):
        grad_resids[chunk], grads_own[chunk], gain2_parts[chunk] = order(
            lambda part: middle_back(
                scalars, resids[chunk], chip_mid[chunk], part, cotangent, gain2, chunk, sub
            ),
            part_mid[chunk],
        )
        if f"grads{chunk}" not in riding:
            grads_other[chunk] = order(lambda own: core_swap(own, 1 + chunk), grads_own[chunk])

    def back_attend(chunk):
        made["backs"] = order(
            lambda other: attend_backward(
                scalars, grads_own[chunk], other, w_o, query, key, value, made.get("backs"),
                chunk, chunk_rows, reach[chunk], pieces,
            ),
            grads_other[chunk],
        )

    def rope():
        backs = made["backs"]
        made["qkv"], made["in_other"], made["in_own"], made["gain_q"], made["gain_k"] = order(
            lambda b: rope_backward(
                scalars, b, backs[1], backs[2], q_raw, kv_raw, gain_q, gain_k, cos, sin, w_q, w_k, w_v, share
            ),
            backs[0],
        )

    def scatter(own, arrived):
        def half_sum(block):
            return order(lambda first: add([first] + arrived[1:], own, block), arrived[0])

        sent = swap(half_sum(lambda s: 1 - s[0]), "tensor", 2)
        return half_sum(lambda s: s[0]), sent

    def in_scatter():
        made["in_kept"], made["in_sum"] = scatter(made["in_own"], made["in_arrived"])

    def project():
        *ffn_other, made["ffn_own"] = order(lambda h: project_other_first(scalars, h, w_down, share), hidden)
        made["ffn_arrived"] = [order(lambda part: core_swap(part, 4), part) for part in ffn_other]

    def ffn_scatter():
        made["ffn_kept"], made["ffn_sum"] = scatter(made["ffn_own"], made["ffn_arrived"])

    def stream_back():
        made["grad_stream"], made["gain1"] = order(
            lambda part: input_back(places, stream, made["in_kept"], part, grad_resids, gain1, sub),
            made["in_sum"],
        )

    def block_out():
        made["out"], made["stats"] = order(
            lambda part: layer_out(places, made["ffn_kept"], part, resids, chip_attn, part_attn, sub),
            made["ffn_sum"],
        )

    small_add = lambda mine, arrived: mine + arrived

    def small(axis, bit):
        made["packed"] = order(small_add, made["packed"], swap(made["packed"], axis, bit))

    def pack():
        made["packed"] = order(
            lambda g: jnp.concatenate(
                [g[0], (gain2_parts[0][0] + gain2_parts[1][0]) * 0.5, made["gain_q"][0], made["gain_k"][0]]
                + [made["stats"][i] for i in range(4)]
            ).reshape(-1, HEAD_SIZE),
            made["gain1"],
        )
        small("tensor", 1)
        small("tensor", 2)

    def second(name):
        if exchange:
            pieces_of[name].second()

    def third(name):
        if exchange:
            pieces_of[name].third()

    def fourth(name):
        if exchange:
            pieces_of[name].fourth()

    def last(name):
        if exchange:
            done[name] = pieces_of[name].last()

    def send_small(bit):
        if exchange:
            made["small"] = swap(made["packed"], "dp", bit)

    def add_small():
        if exchange:
            made["packed"] = order(small_add, made["packed"], made["small"])

    mid_other()
    start_piece(GATE)
    mid_own()
    chip_middle(0)
    chip_middle(1)
    start_piece(UP)
    start_piece(DOWN)
    back_middle(0)
    back_attend(0)
    second(GATE)
    back_middle(1)
    second(UP)
    back_attend(1)
    rope()
    third(GATE)
    start_piece(QKV)
    in_scatter()
    start_piece(ATTN)
    second(DOWN)
    project()
    third(UP)
    ffn_scatter()
    stream_back()
    fourth(GATE)
    second(QKV)
    block_out()
    third(DOWN)
    fourth(UP)
    second(ATTN)
    pack()
    send_small(1)
    last(GATE)
    add_small()
    send_small(2)
    third(QKV)
    last(UP)
    add_small()
    send_small(4)
    fourth(DOWN)
    third(ATTN)
    fourth(QKV)
    last(DOWN)
    fourth(ATTN)
    add_small()
    last(QKV)
    last(ATTN)
    if exchange:
        grad_w_o = done[ATTN]
        grad_w_q, grad_w_kv = done[QKV][:, :q_cols], done[QKV][:, q_cols:]
        grad_w_gu = jnp.stack([done[GATE], done[UP]], axis=1)
        grad_w_down = done[DOWN]
        totals = made["packed"].reshape(-1)
    else:
        bit = 1
        while bit < dp_ways:
            small("dp", bit)
            bit *= 2
        totals = made["packed"].reshape(-1)

        def reduced(pairs):
            total = sum(
                dot(left, (right if plane is None else right[plane])[block * left.shape[0] :][: left.shape[0]], TN)
                for left, right, plane, block in pairs
            )
            return f32(lax.psum_scatter(b16(total), "dp", scatter_dimension=0, tiled=True))

        qkv = reduced([(normed_in, made["qkv"], None, 0)])
        grad_w_q, grad_w_kv = qkv[:, :q_cols], qkv[:, q_cols:]
        grad_w_o = sum(
            dot(left, right, TN)
            for left, right in zip(grads_own + grads_other, mix_own + mix_other, strict=True)
        )
        grad_w_o = f32(lax.psum_scatter(b16(grad_w_o), "dp", scatter_dimension=0, tiled=True))
        grad_w_gu = jnp.stack([reduced(gu_pairs[0]), reduced(gu_pairs[1])], axis=1)
        grad_w_down = reduced(down_pairs)
    cuts = (width, 2 * width, 2 * width + HEAD_SIZE, 2 * width + 2 * HEAD_SIZE)
    stat_total = totals[cuts[3] :].reshape(4, HEAD_SIZE)[:, 0]
    stats = jnp.sqrt(stat_total[:3] / (stat_total[3] * MODEL_WIDTH))
    return (
        made["out"],
        made["grad_stream"],
        grad_w_q,
        grad_w_kv.reshape(-1, 2, kv_cols),
        grad_w_o,
        grad_w_gu,
        grad_w_down,
        totals[: cuts[0]],
        totals[cuts[0] : cuts[1]],
        totals[cuts[1] : cuts[2]],
        totals[cuts[2] : cuts[3]],
        stats,
    )


def solution(mesh):
    placed = (
        P("dp", None),
        P("dp", None),
        P("dp"),
        P("dp", None),
        P("dp", None),
        P(),
        P(None, "tensor"),
        P(None, None, "tensor"),
        P(),
        P(),
        P(None, "tensor"),
        P(),
        P(None, None, "tensor"),
        P(None, "tensor"),
    )
    return jax.shard_map(
        per_device,
        mesh=mesh,
        in_specs=placed,
        out_specs=(
            P(("dp", "tensor"), None),
            P(("dp", "tensor"), None),
            P("dp", "tensor"),
            P("dp", None, "tensor"),
            P("dp", "tensor"),
            P("dp", None, "tensor"),
            P("dp", "tensor"),
            P(),
            P(),
            P(),
            P(),
            P(),
        ),
        check_vma=False,
    )
```

```python
import math

import jax
import jax.numpy as jnp
import numpy as np
from jax import lax
from jax.experimental import pallas as pl
from jax.experimental.pallas import tpu as pltpu
from jax.sharding import PartitionSpec as P

MODEL_WIDTH = 2048
HEAD_SIZE = 128
SEQ_LEN = 1024
EPSILON = 1e-06
MASKED = -1e30
SCALE = HEAD_SIZE ** (-0.5)
F32 = jnp.float32
BF16 = jnp.bfloat16
VMEM_BYTES = 60 * 1024 * 1024
NN = (((1,), (0,)), ((), ()))
NT = (((1,), (1,)), ((), ()))
TN = (((0,), (0,)), ((), ()))
SPLIT = 1
FLIPPED = -1
GATE, UP, DOWN, QKV, ATTN = range(5)
LINE_FIRST = (GATE,)
RIDES = {GATE: ("core0",), QKV: ("input0",)}


def dot(left, right, dims=NN):
    return lax.dot_general(left, right, dims, preferred_element_type=F32)


def f32(values):
    return values.astype(F32)


def b16(values):
    return values.astype(BF16)


def shape(dims, kind=BF16):
    return jax.ShapeDtypeStruct(dims, kind)


MESH_IDS = pl.DeviceIdType.MESH


def partner(bit):
    mine = lax.axis_index("tensor")
    return {"tensor": mine + bit * (1 - 2 * (mine // bit % 2))}


def exchange_copies(bits, sources, targets, sems):
    return [
        pltpu.make_async_remote_copy(
            src_ref=source,
            dst_ref=target,
            send_sem=sems.at[0, index],
            recv_sem=sems.at[1, index],
            device_id=partner(bit),
            device_id_type=MESH_IDS,
        )
        for index, (bit, source, target) in enumerate(zip(bits, sources, targets, strict=True))
    ]


def meet(bits):
    barrier = pltpu.get_barrier_semaphore()
    for bit in sorted(set(bits)):
        pl.semaphore_signal(barrier, inc=1, device_id=partner(bit), device_id_type=MESH_IDS)
    pl.semaphore_wait(barrier, len(set(bits)))


def call_with_riders(body, outs, grid, in_specs, out_specs, args, name, riders, ident):
    bits = [bit for _, bit in riders]
    count, inputs, results = len(riders), len(args), len(outs)

    def riding(*refs):
        own_in, sources = refs[:inputs], refs[inputs : inputs + count]
        rest = refs[inputs + count :]
        own_out, targets, sems = rest[:results], rest[results : results + count], rest[-1]

        @pl.when(pl.program_id(0) == 0)
        def _():
            meet(bits)
            for copy in exchange_copies(bits, sources, targets, sems):
                copy.start()

        body(*own_in, *own_out)

        @pl.when(pl.program_id(0) == grid[0] - 1)
        def _():
            for copy in exchange_copies(bits, sources, targets, sems):
                copy.wait()

    far = pl.BlockSpec(memory_space=pl.ANY)
    return pl.pallas_call(
        riding,
        out_shape=list(outs) + [shape(array.shape, array.dtype) for array, _ in riders],
        grid_spec=pltpu.PrefetchScalarGridSpec(
            num_scalar_prefetch=0,
            grid=grid,
            in_specs=list(in_specs) + [far] * count,
            out_specs=list(out_specs) + [far] * count,
            scratch_shapes=[pltpu.SemaphoreType.DMA((2, count))],
        ),
        compiler_params=pltpu.CompilerParams(
            vmem_limit_bytes=VMEM_BYTES, collective_id=ident, has_side_effects=True
        ),
        cost_estimate=pl.CostEstimate(flops=1024, bytes_accessed=1024, transcendentals=0),
        name=name,
    )(*args, *[array for array, _ in riders])


def call(body, outs, grid, in_specs, out_specs, args, name, scalars=None, scratch=(), alias=None):
    count = 0 if scalars is None else 1
    return pl.pallas_call(
        body,
        out_shape=outs,
        grid_spec=pltpu.PrefetchScalarGridSpec(
            num_scalar_prefetch=count,
            grid=grid,
            in_specs=in_specs,
            out_specs=out_specs,
            scratch_shapes=scratch,
        ),
        compiler_params=pltpu.CompilerParams(vmem_limit_bytes=VMEM_BYTES),
        cost_estimate=pl.CostEstimate(flops=1024, bytes_accessed=1024, transcendentals=0),
        input_output_aliases=alias or {},
        name=name,
    )(*(() if scalars is None else (scalars,)), *args)


def whole(array):
    dims = array.shape
    return pl.BlockSpec(dims, lambda *_: (0,) * len(dims))


def rms_scale(values):
    return lax.rsqrt(jnp.mean(values * values, axis=-1, keepdims=True) + EPSILON)


def norm_back(values, gain, grad):
    scale = rms_scale(values)
    weighted = grad * gain
    along = jnp.mean(weighted * values, axis=-1, keepdims=True)
    grad_values = scale * weighted - values * (scale * scale * scale * along)
    grad_gain = jnp.sum(grad * (values * scale), axis=0, keepdims=True)
    return grad_values, grad_gain


def rope_tables():
    half = HEAD_SIZE // 2
    inverse = np.exp(np.arange(half) * (-2.0 * math.log(1000000.0) / HEAD_SIZE))
    angles = np.arange(SEQ_LEN)[:, None] * inverse[None, :]
    cos, sin = np.cos(angles), np.sin(angles)
    wide_cos = np.concatenate([cos, cos], axis=1).astype(np.float32)
    wide_sin = np.concatenate([-sin, sin], axis=1).astype(np.float32)
    return wide_cos, wide_sin


def rotate(values, cos, sin):
    return values * cos + pltpu.roll(values, HEAD_SIZE // 2, 1) * sin


def rotate_back(values, cos, sin):
    return values * cos - pltpu.roll(values, HEAD_SIZE // 2, 1) * sin


def head(index):
    return slice(index * HEAD_SIZE, (index + 1) * HEAD_SIZE)


def norm_query(stream, gain, w_q, rows):
    tokens, width = stream.shape
    cols = w_q.shape[1]

    def body(stream_ref, gain_ref, w_ref, normed_ref, query_ref):
        values = f32(stream_ref[...])
        normed = b16(values * rms_scale(values) * gain_ref[...])
        normed_ref[...] = normed
        query_ref[...] = dot(normed, w_ref[...])

    return call(
        body,
        [shape((tokens, width)), shape((tokens, cols), F32)],
        (tokens // rows,),
        [pl.BlockSpec((rows, width), lambda i: (i, 0)), whole(gain), whole(w_q)],
        [pl.BlockSpec((rows, width), lambda i: (i, 0)), pl.BlockSpec((rows, cols), lambda i: (i, 0))],
        (stream, gain, w_q),
        "norm_query",
    )


def rope_forward(q_raw, kv_raw, q_gain, k_gain, cos, sin, rows):
    tokens, q_cols = q_raw.shape
    kv_cols = kv_raw.shape[2]

    def body(q_ref, kv_ref, qg_ref, kg_ref, cos_ref, sin_ref, q_out, k_out, v_out):
        cos_rows, sin_rows = cos_ref[...], sin_ref[...]
        for h in range(q_cols // HEAD_SIZE):
            values = q_ref[:, head(h)]
            q_out[:, head(h)] = b16(rotate(values * rms_scale(values) * qg_ref[...], cos_rows, sin_rows))
        for h in range(kv_cols // HEAD_SIZE):
            values = kv_ref[0, :, head(h)]
            k_out[:, head(h)] = b16(rotate(values * rms_scale(values) * kg_ref[...], cos_rows, sin_rows))
        v_out[...] = b16(kv_ref[1])

    row = lambda cols: pl.BlockSpec((rows, cols), lambda i: (i, 0))
    return call(
        body,
        [shape((tokens, q_cols)), shape((tokens, kv_cols)), shape((tokens, kv_cols))],
        (tokens // rows,),
        [
            row(q_cols),
            pl.BlockSpec((2, rows, kv_cols), lambda i: (0, i, 0)),
            whole(q_gain),
            whole(k_gain),
            row(HEAD_SIZE),
            row(HEAD_SIZE),
        ],
        [row(q_cols), row(kv_cols), row(kv_cols)],
        (q_raw, kv_raw, q_gain, k_gain, cos, sin),
        "rope_forward",
    )


def key_limit(scalars, start, count, pieces):
    position = start + lax.broadcasted_iota(jnp.int32, (count, 1), 0)
    limit = position + 1
    for piece in range(pieces):
        first, last = scalars[2 + 2 * piece], scalars[3 + 2 * piece]
        inside = (position >= first) & (position < last)
        limit = jnp.where(inside, jnp.maximum(limit, last), limit)
    return jnp.minimum(limit, scalars[1])


def soft_weights(query, keys, limit):
    scores = dot(query, keys, NT) * SCALE
    key_pos = lax.broadcasted_iota(jnp.int32, scores.shape, 1)
    scores = jnp.where(key_pos < limit, scores, MASKED)
    shifted = jnp.exp(scores - jnp.max(scores, axis=-1, keepdims=True))
    return shifted / jnp.sum(shifted, axis=-1, keepdims=True)


def attend_forward(scalars, query, key, value, w_o, chunk, count, reach, pieces):
    q_cols, kv_cols, width = query.shape[1], key.shape[1], w_o.shape[0]
    heads, half = q_cols // HEAD_SIZE, count // 2
    repeat = q_cols // kv_cols

    def body(scalars, q_ref, k_ref, v_ref, w_ref, own_out, other_out, own_mix, other_mix, mixed):
        limit = key_limit(scalars, chunk * count, count, pieces)
        for h in range(heads):
            weights = soft_weights(q_ref[:, head(h)], k_ref[:, head(h // repeat)], limit)
            mixed[:, head(h)] = b16(dot(b16(weights), v_ref[:, head(h // repeat)]))
        core = scalars[0]
        other = mixed[pl.ds(pl.multiple_of((1 - core) * half, half), half), :]
        own = mixed[pl.ds(pl.multiple_of(core * half, half), half), :]
        other_mix[...] = other
        own_mix[...] = own
        other_out[...] = b16(dot(other, w_ref[...], NT))
        own_out[...] = b16(dot(own, w_ref[...], NT))

    return call(
        body,
        [shape((half, width)), shape((half, width)), shape((half, q_cols)), shape((half, q_cols))],
        (1,),
        [
            pl.BlockSpec((count, q_cols), lambda i, s: (chunk, 0)),
            pl.BlockSpec((reach, kv_cols), lambda i, s: (0, 0)),
            pl.BlockSpec((reach, kv_cols), lambda i, s: (0, 0)),
            whole(w_o),
        ],
        [
            pl.BlockSpec((half, width), lambda i, s: (0, 0)),
            pl.BlockSpec((half, width), lambda i, s: (0, 0)),
            pl.BlockSpec((half, q_cols), lambda i, s: (0, 0)),
            pl.BlockSpec((half, q_cols), lambda i, s: (0, 0)),
        ],
        (query, key, value, w_o),
        "attend_forward",
        scalars,
        [pltpu.VMEM((count, q_cols), BF16)],
    )


def row_specs(rows, sub, width, chunk):
    steps = rows // sub
    picked = pl.BlockSpec((sub, width), lambda i, s: ((2 * chunk + s[0]) * steps + i, 0))
    return picked, pl.BlockSpec((sub, width), lambda i, s: (i, 0))


def middle(scalars, stream, chip, part, gain, chunk, sub):
    rows, width = chip.shape

    def body(scalars, stream_ref, chip_ref, part_ref, gain_ref, resid_out, normed_out):
        resid = f32(stream_ref[...]) + (f32(chip_ref[...]) + f32(part_ref[...]))
        resid_out[...] = resid
        normed_out[...] = b16(resid * rms_scale(resid) * gain_ref[...])

    picked, row = row_specs(rows, sub, width, chunk)
    return call(
        body,
        [shape((rows, width), F32), shape((rows, width))],
        (rows // sub,),
        [picked, row, row, whole(gain)],
        [row, row],
        (stream, chip, part, gain),
        "middle",
        scalars,
    )


def gate_back(scalars, gate_up, grad_hidden, before, chunk, rows, sub):
    planes, _, cols = gate_up.shape
    tokens = grad_hidden.shape[0]
    steps = rows // sub
    natural = lambda i, s: ((2 * chunk + (s[0] + i // steps) % 2) * steps + i % steps, 0)

    def body(scalars, gu_ref, gh_ref, *rest):
        hidden_out, own_out, other_out = rest[-3:]
        gate, up, grad = gu_ref[0], gu_ref[1], gh_ref[...]
        logistic = 1.0 / (1.0 + jnp.exp(-gate))
        silu = gate * logistic
        hidden_out[...] = b16(silu * up)
        grad_gate = b16(grad * up * logistic * (1.0 + gate * (1.0 - logistic)))
        grad_up = b16(grad * silu)

        @pl.when(pl.program_id(0) < steps)
        def _():
            own_out[0], own_out[1] = grad_gate, grad_up

        @pl.when(pl.program_id(0) >= steps)
        def _():
            other_out[0], other_out[1] = grad_gate, grad_up

    args = [gate_up, grad_hidden]
    specs = [
        pl.BlockSpec((planes, sub, cols), lambda i, s: (0, i, 0)),
        pl.BlockSpec((sub, cols), natural),
    ]
    alias = None
    if before is not None:
        args += list(before)
        specs += [pl.BlockSpec(memory_space=pl.ANY)] * 3
        alias = {3: 0, 4: 1, 5: 2}
    part = shape((planes, tokens // 2, cols))
    return call(
        body,
        [shape((tokens, cols)), part, part],
        (2 * steps,),
        specs,
        [
            pl.BlockSpec((sub, cols), natural),
            pl.BlockSpec((planes, sub, cols), lambda i, s: (0, chunk * steps + jnp.minimum(i, steps - 1), 0)),
            pl.BlockSpec((planes, sub, cols), lambda i, s: (0, chunk * steps + jnp.maximum(i - steps, 0), 0)),
        ],
        args,
        "gate_back",
        scalars,
        (),
        alias,
    )


def by_side(groups, product, other_outs, own_out):
    @pl.when(pl.program_id(0) < groups)
    def _():
        for index, other_out in enumerate(other_outs):
            cols = other_out.shape[1]
            other_out[...] = product[:, index * cols : (index + 1) * cols]

    @pl.when(pl.program_id(0) >= groups)
    def _():
        own_out[...] = product


def side_specs(groups, rows, width):
    part = pl.BlockSpec((rows, width // SPLIT), lambda i, s: (jnp.minimum(i, groups - 1), 0))
    return [part] * SPLIT + [pl.BlockSpec((rows, width), lambda i, s: (jnp.maximum(i - groups, 0), 0))]


def project_other_first(scalars, values, weights, rows):
    tokens, depth = values.shape
    width = weights.shape[0]
    groups = tokens // (2 * rows)
    natural = lambda i, s: 2 * (i % groups) + (s[0] + 1 + i // groups) % 2

    def body(scalars, values_ref, weights_ref, *outs):
        product = b16(dot(values_ref[...], weights_ref[...], NT))
        by_side(groups, product, outs[:-1], outs[-1])

    return call(
        body,
        [shape((tokens // 2, width // SPLIT))] * SPLIT + [shape((tokens // 2, width))],
        (tokens // rows,),
        [pl.BlockSpec((rows, depth), lambda i, s: (natural(i, s), 0)), whole(weights)],
        side_specs(groups, rows, width),
        (values, weights),
        "project",
        scalars,
    )


def add_gain(gain_out, gain):
    @pl.when(pl.program_id(0) == 0)
    def _():
        gain_out[...] = jnp.zeros_like(gain_out)

    gain_out[...] += gain


def middle_back(scalars, resid, chip, part, cotangent, gain, chunk, sub):
    rows, width = resid.shape

    def body(scalars, resid_ref, chip_ref, part_ref, cot_ref, gain_ref, resid_out, attn_out, gain_out):
        grad = f32(chip_ref[...]) + f32(part_ref[...])
        back, gain_part = norm_back(resid_ref[...], gain_ref[...], grad)
        add_gain(gain_out, gain_part)
        total = f32(cot_ref[...]) + back
        resid_out[...] = total
        attn_out[...] = b16(total)

    picked, row = row_specs(rows, sub, width, chunk)
    return call(
        body,
        [shape((rows, width), F32), shape((rows, width)), shape((1, width), F32)],
        (rows // sub,),
        [row, row, row, picked, whole(gain)],
        [row, row, pl.BlockSpec((1, width), lambda i, s: (0, 0))],
        (resid, chip, part, cotangent, gain),
        "middle_back",
        scalars,
    )


def attend_backward(scalars, own, other, w_o, query, key, value, before, chunk, count, reach, pieces):
    tokens, q_cols = query.shape
    kv_cols, width = key.shape[1], w_o.shape[0]
    heads, half = q_cols // HEAD_SIZE, count // 2
    repeat = q_cols // kv_cols
    old = 0 if before is None else before[1].shape[0]

    def body(scalars, own_ref, other_ref, w_ref, q_ref, k_ref, v_ref, *rest):
        olds = rest[: len(rest) - 4]
        q_out, k_out, v_out, mixed = rest[len(rest) - 4 :]
        core = scalars[0]
        w = w_ref[...]
        mixed[pl.ds(pl.multiple_of(core * half, half), half), :] = b16(dot(own_ref[...], w))
        mixed[pl.ds(pl.multiple_of((1 - core) * half, half), half), :] = b16(dot(other_ref[...], w))
        limit = key_limit(scalars, chunk * count, count, pieces)
        for g in range(kv_cols // HEAD_SIZE):
            k_total, v_total = 0.0, 0.0
            for h in range(g * repeat, (g + 1) * repeat):
                q_head, k_head, grad = q_ref[:, head(h)], k_ref[:, head(g)], mixed[:, head(h)]
                weights = soft_weights(q_head, k_head, limit)
                grad_weights = dot(grad, v_ref[:, head(g)], NT)
                delta = jnp.sum(weights * grad_weights, axis=-1, keepdims=True)
                grad_scores = b16(weights * (grad_weights - delta))
                q_out[:, head(h)] = dot(grad_scores, k_head) * SCALE
                k_total = k_total + dot(grad_scores, q_head, TN)
                v_total = v_total + dot(b16(weights), grad, TN)
            k_out[:, head(g)] = k_total * SCALE
            v_out[:, head(g)] = v_total
        if old:
            k_out[:old, :] += olds[1][...]
            v_out[:old, :] += olds[2][...]

    flat = pl.BlockSpec((half, width), lambda i, s: (0, 0))
    keys = pl.BlockSpec((reach, kv_cols), lambda i, s: (0, 0))
    args = [own, other, w_o, query, key, value]
    specs = [flat, flat, whole(w_o), pl.BlockSpec((count, q_cols), lambda i, s: (chunk, 0)), keys, keys]
    alias = None
    if before is not None:
        args += list(before)
        specs += [pl.BlockSpec(memory_space=pl.ANY), whole(before[1]), whole(before[2])]
        alias = {7: 0}
    return call(
        body,
        [shape((tokens, q_cols), F32), shape((reach, kv_cols), F32), shape((reach, kv_cols), F32)],
        (1,),
        specs,
        [pl.BlockSpec((count, q_cols), lambda i, s: (chunk, 0)), keys, keys],
        args,
        "attend_backward",
        scalars,
        [pltpu.VMEM((count, q_cols), BF16)],
        alias,
    )


def rope_backward(scalars, grad_q, grad_k, grad_v, q_raw, kv_raw, q_gain, k_gain, cos, sin, w_q, w_k, w_v, rows):
    tokens, q_cols = q_raw.shape
    kv_cols, width = kv_raw.shape[2], w_q.shape[0]
    all_cols, heads = q_cols + 2 * kv_cols, q_cols // HEAD_SIZE
    groups = tokens // (2 * rows)
    natural = lambda i, s: 2 * (i % groups) + (s[0] + 1 + i // groups) % 2

    def body(
        scalars, gq_ref, gk_ref, gv_ref, q_ref, kv_ref, qg_ref, kg_ref, cos_ref, sin_ref, wq_ref, wk_ref, wv_ref,
        qkv_out, *outs,
    ):
        *other_outs, own_out, qg_out, kg_out = outs
        step = pl.program_id(0)

        @pl.when(step == 0)
        def _():
            qg_out[...] = jnp.zeros_like(qg_out)
            kg_out[...] = jnp.zeros_like(kg_out)

        cos_rows, sin_rows = cos_ref[...], sin_ref[...]
        for h in range(q_cols // HEAD_SIZE):
            grad = rotate_back(gq_ref[:, head(h)], cos_rows, sin_rows)
            back, gain = norm_back(q_ref[:, head(h)], qg_ref[...], grad)
            qkv_out[:, head(h)] = b16(back)
            qg_out[...] += gain
        for h in range(kv_cols // HEAD_SIZE):
            grad = rotate_back(gk_ref[:, head(h)], cos_rows, sin_rows)
            back, gain = norm_back(kv_ref[:, head(h)], kg_ref[...], grad)
            qkv_out[:, head(heads + h)] = b16(back)
            kg_out[...] += gain
        qkv_out[:, q_cols + kv_cols :] = b16(gv_ref[...])
        total = dot(qkv_out[:, :q_cols], wq_ref[...], NT)
        total = total + dot(qkv_out[:, q_cols : q_cols + kv_cols], wk_ref[...], NT)
        total = total + dot(qkv_out[:, q_cols + kv_cols :], wv_ref[...], NT)
        by_side(groups, b16(total), other_outs, own_out)

    row = lambda cols: pl.BlockSpec((rows, cols), lambda i, s: (natural(i, s), 0))
    gain_spec = pl.BlockSpec((1, HEAD_SIZE), lambda i, s: (0, 0))
    return call(
        body,
        [
            shape((tokens, all_cols)),
            *[shape((tokens // 2, width // SPLIT))] * SPLIT,
            shape((tokens // 2, width)),
            shape((1, HEAD_SIZE), F32),
            shape((1, HEAD_SIZE), F32),
        ],
        (tokens // rows,),
        [
            row(q_cols),
            row(kv_cols),
            row(kv_cols),
            row(q_cols),
            pl.BlockSpec((None, rows, kv_cols), lambda i, s: (0, natural(i, s), 0)),
            whole(q_gain),
            whole(k_gain),
            row(HEAD_SIZE),
            row(HEAD_SIZE),
            whole(w_q),
            whole(w_k),
            whole(w_v),
        ],
        [
            row(all_cols),
            *side_specs(groups, rows, width),
            gain_spec,
            gain_spec,
        ],
        (grad_q, grad_k, grad_v, q_raw, kv_raw, q_gain, k_gain, cos, sin, w_q, w_k, w_v),
        "rope_backward",
        scalars,
    )


def input_back(places, stream, kept, part, resids, gain, sub):
    rows, width = kept.shape

    def body(places, stream_ref, kept_ref, part_ref, first_ref, second_ref, gain_ref, out, gain_out):
        grad = f32(kept_ref[...]) + f32(part_ref[...])
        back, gain_part = norm_back(f32(stream_ref[...]), gain_ref[...], grad)
        add_gain(gain_out, gain_part)
        resid = jnp.where(places[0] == 0, first_ref[...], second_ref[...])
        out[...] = b16(resid + back)

    steps = rows // sub
    row = pl.BlockSpec((sub, width), lambda i, s: (i, 0))
    return call(
        body,
        [shape((rows, width)), shape((1, width), F32)],
        (steps,),
        [pl.BlockSpec((sub, width), lambda i, s: (s[1] * steps + i, 0)), row, row, row, row, whole(gain)],
        [row, pl.BlockSpec((1, width), lambda i, s: (0, 0))],
        (stream, kept, part, *resids, gain),
        "input_back",
        places,
    )


def layer_out(places, kept, part, resids, chips, parts, sub):
    rows, width = kept.shape
    steps = rows // sub

    def body(places, kept_ref, part_ref, *rest):
        resid_refs, chip_refs, part_refs = rest[0:2], rest[2:4], rest[4:6]
        out, sums_out = rest[6:]
        first = places[0] == 0
        ffn = f32(kept_ref[...]) + f32(part_ref[...])
        attns = [f32(chip_refs[i][...]) + f32(part_refs[i][...]) for i in range(2)]
        attn = jnp.where(first, attns[0], attns[1])
        total = jnp.where(first, resid_refs[0][...], resid_refs[1][...]) + ffn
        out[...] = b16(total)
        position = places[1] * rows + pl.program_id(0) * sub + lax.broadcasted_iota(jnp.int32, (sub, 1), 0)
        live = position < places[2]
        for index, values in enumerate((total, attn, ffn)):
            rows_sum = jnp.sum(jnp.where(live, values * values, 0.0), axis=1, keepdims=True)
            one = jnp.sum(rows_sum, axis=0, keepdims=True)
            add_row(sums_out, index, one)
        add_row(sums_out, 3, jnp.sum(jnp.where(live, 1.0, 0.0), axis=0, keepdims=True))

    row = pl.BlockSpec((sub, width), lambda i, s: (i, 0))
    return call(
        body,
        [shape((rows, width)), shape((8, HEAD_SIZE), F32)],
        (steps,),
        [row] * 8,
        [row, pl.BlockSpec((8, HEAD_SIZE), lambda i, s: (0, 0))],
        (kept, part, *resids, *chips, *parts),
        "layer_out",
        places,
    )


def add_row(sums_out, index, one):
    wide = jnp.broadcast_to(one, (1, HEAD_SIZE))

    @pl.when(pl.program_id(0) == 0)
    def _():
        sums_out[index : index + 1, :] = wide

    @pl.when(pl.program_id(0) > 0)
    def _():
        sums_out[index : index + 1, :] += wide


def split_pair(weights, rows):
    depth, _, cols = weights.shape

    def body(weights_ref, first_out, second_out):
        values = weights_ref[...]
        first_out[...] = values[:, 0, :]
        second_out[...] = values[:, 1, :]

    row = pl.BlockSpec((rows, cols), lambda i: (i, 0))
    return call(
        body,
        [shape((depth, cols)), shape((depth, cols))],
        (depth // rows,),
        [pl.BlockSpec((rows, 2, cols), lambda i: (i, 0, 0))],
        [row, row],
        (weights,),
        "split_pair",
    )


def block_order(bits):
    order = [0]
    for bit in reversed(bits[1:]):
        order = order + [k ^ bit for k in order]
    return order


def flipped(index, value):
    bit = 1
    while bit <= value:
        if value & bit:
            index = index + bit * (1 - 2 * (index // bit % 2))
        bit *= 2
    return index


def weight_grad(pairs, col, cols, bits, ways, riders, ident):
    width = pairs[0][0].shape[1]
    rows = width // ways
    own = block_order(bits)
    count, half = len(own), len(own) // 2

    def source(index):
        def place(i):
            mine = flipped(lax.axis_index("dp"), own[index])
            return (0, i * mine + (1 - i) * flipped(mine, bits[0]))

        return place

    args, specs = [], []
    for left, right, plane, block in pairs:
        depth = left.shape[0]
        args += [left] * count + [right]
        specs += [pl.BlockSpec((depth, rows), source(index)) for index in range(count)]
        if plane is None:
            specs.append(pl.BlockSpec((depth, cols), lambda i, b=block: (b, col)))
        else:
            specs.append(pl.BlockSpec((None, depth, cols), lambda i, p=plane, b=block: (p, b, col)))

    def body(*refs):
        send_out, keep_out, next_out = refs[-3:]
        total = 0.0
        for index in range(len(pairs)):
            part = refs[index * (count + 1) : (index + 1) * (count + 1)]
            left = jnp.concatenate([ref[...] for ref in part[:-1]], axis=1)
            total = total + dot(left, part[-1][...], TN)
        product = b16(total)

        @pl.when(pl.program_id(0) == 0)
        def _():
            send_out[...] = product

        @pl.when(pl.program_id(0) == 1)
        def _():
            keep_out[...] = product[: half * rows]
            next_out[...] = product[half * rows :]

    flat = lambda blocks: pl.BlockSpec((blocks * rows, cols), lambda i: (0, 0))
    outs = [shape((count * rows, cols)), shape((half * rows, cols)), shape((half * rows, cols))]
    out_specs = [flat(count), flat(half), flat(half)]
    if riders:
        return call_with_riders(body, outs, (2,), specs, out_specs, args, "weight_grad", riders, ident)
    return call(body, outs, (2,), specs, out_specs, args, "weight_grad")


def add_parts(parts, rows, kind, scalars=None, steps=2):
    parts = [(array if isinstance(array, list) else [array], block) for array, block in parts]
    cols = sum(array.shape[1] for array in parts[0][0])
    sub = rows // steps

    def body(*refs):
        refs = list(refs if scalars is None else refs[1:])
        total = 0.0
        for arrays, _ in parts:
            values = [f32(refs.pop(0)[...]) for _ in arrays]
            total = total + (values[0] if len(values) == 1 else jnp.concatenate(values, axis=1))
        refs[0][...] = total.astype(kind)

    def spec(block, cols):
        if callable(block):
            return pl.BlockSpec((sub, cols), lambda i, s: (block(s) * steps + i, 0))
        if block is FLIPPED:
            return pl.BlockSpec((sub, cols), lambda i, *s: (steps - 1 - i, 0))
        return pl.BlockSpec((sub, cols), lambda i, *s: (block * steps + i, 0))

    return call(
        body,
        shape((rows, cols), kind),
        (steps,),
        [spec(block, array.shape[1]) for arrays, block in parts for array in arrays],
        pl.BlockSpec((sub, cols), lambda i, *s: (i, 0)),
        [array for arrays, _ in parts for array in arrays],
        "add_parts",
        scalars,
    )


def swap(values, axis, bit):
    ways = lax.axis_size(axis)
    return lax.ppermute(values, axis, [(i, i ^ bit) for i in range(ways)])


def core_swap(values, ident):
    def body(in_ref, out_ref, sems):
        meet([1])
        (copy,) = exchange_copies([1], [in_ref], [out_ref], sems)
        copy.start()
        copy.wait()

    return pl.pallas_call(
        body,
        out_shape=shape(values.shape, values.dtype),
        in_specs=[pl.BlockSpec(memory_space=pl.ANY)],
        out_specs=pl.BlockSpec(memory_space=pl.ANY),
        scratch_shapes=[pltpu.SemaphoreType.DMA((2, 1))],
        compiler_params=pltpu.CompilerParams(collective_id=ident, has_side_effects=True),
        cost_estimate=pl.CostEstimate(flops=1024, bytes_accessed=1024, transcendentals=0),
        name="core_swap",
    )(values)


class Order:
    def __init__(self):
        self.last = None

    def __call__(self, function, first, *rest, **named):
        if self.last is not None:
            first, _ = lax.optimization_barrier((first, self.last))
        result = function(first, *rest, **named)
        self.last = jax.tree.leaves(result)[-1]
        return result


class Piece:
    def __init__(self, order, pairs, col, cols, bits, ways, riders, ident):
        self.order, self.bits = order, bits
        run = lambda array: weight_grad(
            [(array, *pairs[0][1:])] + pairs[1:], col, cols, bits, ways, riders, ident
        )
        self.send, self.keep, self.next, *self.rode = order(run, pairs[0][0])
        self.start()

    def start(self):
        self.arrived = swap(self.send, "dp", self.bits[0])


class LinePiece(Piece):
    def second(self):
        add = lambda arrived: add_parts([(arrived, 1), (self.next, 0)], self.next.shape[0], BF16)
        self.far = self.order(add, self.arrived)
        self.arrived2 = lax.ppermute(self.far, "dp", [(0, 2), (1, 3), (6, 4), (7, 5)])

    def third(self):
        add = lambda arrived: add_parts([(arrived, FLIPPED), (self.far, 0)], self.far.shape[0], BF16)
        self.arrived3 = lax.ppermute(self.order(add, self.arrived2), "dp", [(2, 4), (4, 2), (3, 5), (5, 3)])

    def fourth(self):
        half = self.keep.shape[0] // 2
        add = lambda arrived: add_parts([(arrived, 0), (self.arrived, 1), (self.keep, 1)], half, BF16)
        self.arrived4 = swap(self.order(add, self.arrived3), "dp", 2)

    def last(self):
        half = self.keep.shape[0] // 2
        add = lambda arrived: add_parts(
            [(arrived, 0), (self.arrived3, 1), (self.arrived, 0), (self.keep, 0)], half, F32
        )
        return self.order(add, self.arrived4)


class LineFirstPiece(Piece):
    def start(self):
        self.arrived = lax.ppermute(self.send, "dp", [(0, 2), (1, 3), (6, 4), (7, 5)])

    def second(self):
        add = lambda arrived: add_parts([(arrived, FLIPPED), (self.send, 0)], self.send.shape[0], BF16)
        self.arrived2 = lax.ppermute(self.order(add, self.arrived), "dp", [(2, 4), (4, 2), (3, 5), (5, 3)])

    def third(self):
        add = lambda arrived: add_parts([(arrived, 0), (self.next, 0)], self.next.shape[0], BF16)
        self.arrived3 = swap(self.order(add, self.arrived2), "dp", 2)

    def fourth(self):
        half = self.keep.shape[0] // 2
        add = lambda arrived: add_parts([(arrived, 1), (self.arrived2, 3), (self.keep, 1)], half, BF16)
        self.arrived4 = swap(self.order(add, self.arrived3), "dp", 1)

    def last(self):
        half = self.keep.shape[0] // 2
        add = lambda arrived: add_parts(
            [(arrived, 0), (self.arrived3, 0), (self.arrived2, 2), (self.keep, 0)], half, F32
        )
        return self.order(add, self.arrived4)


def per_device(
    stream,
    cotangent,
    live_mask,
    piece_start,
    piece_len,
    norm1_gain,
    w_q,
    key_value_weight,
    q_gain,
    k_gain,
    w_o,
    norm2_gain,
    w_gu,
    w_down,
):
    tokens, width = stream.shape
    pieces = piece_start.shape[1]
    piece_span = SEQ_LEN // pieces
    tensor_ways, dp_ways = lax.axis_size("tensor"), lax.axis_size("dp")
    assert tensor_ways == 4 and tokens == SEQ_LEN and piece_start.shape[0] == 1
    tensor_index = lax.axis_index("tensor")
    group, core = tensor_index // 2, tensor_index % 2
    share = tokens // tensor_ways
    sub = share // 4
    q_cols, kv_cols = w_q.shape[1], key_value_weight.shape[2]
    ff_cols = w_down.shape[1]
    chunk_rows = 2 * share
    reach = [-(-(chunk_rows * (i + 1)) // piece_span) * piece_span for i in range(2)]
    cos, sin = rope_tables()

    live_count = jnp.sum(live_mask)
    ends = piece_start[0] + piece_len[0]
    spans = jnp.stack([piece_start[0], ends], axis=1).reshape(-1)
    scalars = jnp.concatenate([jnp.stack([core, live_count]), spans]).astype(jnp.int32)
    places = jnp.stack([group, tensor_index, live_count]).astype(jnp.int32)
    gain1, gain2 = norm1_gain[None], norm2_gain[None]
    gain_q, gain_k = q_gain[None], k_gain[None]
    both = range(2)

    order = Order()
    normed_in, q_raw = order(lambda s: norm_query(s, gain1, w_q, share // 2), stream)
    kv_raw = order(
        lambda n: jnp.einsum("td,dcn->ctn", n, key_value_weight, preferred_element_type=F32), normed_in
    )
    query, key, value = order(
        lambda r: rope_forward(q_raw, r, gain_q, gain_k, cos, sin, share // 2), kv_raw
    )

    def attend(chunk):
        return order(
            lambda q: attend_forward(scalars, q, key, value, w_o, chunk, chunk_rows, reach[chunk], pieces),
            query,
        )

    def add(arrived, own, block=0):
        return add_parts([(arrived, block), (own, block)], share, BF16, places)

    attn_own, attn_arrived, mix_own, mix_other = [None] * 2, [None] * 2, [None] * 2, [None] * 2
    chip_attn, part_attn = [None] * 2, [None] * 2
    for chunk in both:
        attn_own[chunk], other, mix_own[chunk], mix_other[chunk] = attend(chunk)
        attn_arrived[chunk] = swap(other, "tensor", 1)
        if chunk == 0:
            w_k, w_v = order(lambda w: split_pair(w, share), key_value_weight)
        else:
            grad_hidden = order(lambda c: dot(c, w_down), cotangent)
        chip_attn[chunk] = order(add, attn_arrived[chunk], attn_own[chunk])
        part_attn[chunk] = swap(chip_attn[chunk], "tensor", 2)

    resids, mids_own, mids_other, backs = [], [], [], None
    for chunk in both:
        resid, mid = order(
            lambda part: middle(scalars, stream, chip_attn[chunk], part, gain2, chunk, sub),
            part_attn[chunk],
        )
        other = swap(mid, "tensor", 1)
        resids.append(resid)
        mids_own.append(mid)
        mids_other.append(other)
        mids = order(lambda o: jnp.concatenate([mid, o], axis=0), other)
        gate_up = order(lambda m: jnp.einsum("td,dcf->ctf", m, w_gu, preferred_element_type=F32), mids)
        backs = order(lambda gu: gate_back(scalars, gu, grad_hidden, backs, chunk, share, share // 2), gate_up)
    hidden, gu_own, gu_other = backs

    exchange = width // dp_ways % 128 == 0 and dp_ways == 8
    line, line_first = (1, 4, 2), (4, 2, 1)

    def piece(pairs, col, cols, bits, riders, ident):
        kind = LinePiece if bits == line else LineFirstPiece
        return kind(order, pairs, col, cols, bits, dp_ways, riders, ident)

    gu_pairs = [
        [
            (mids_own[0], gu_own, plane, 0),
            (mids_own[1], gu_own, plane, 1),
            (mids_other[0], gu_other, plane, 0),
            (mids_other[1], gu_other, plane, 1),
        ]
        for plane in both
    ]
    down_pairs = [(cotangent, hidden, None, 0)]

    def mid_part(grads):
        return order(
            lambda g: b16(jnp.einsum("ctf,dcf->td", g, w_gu, preferred_element_type=F32)), grads
        )

    riding = sum(RIDES.values(), ())
    grad_resids, grads_own, grads_other, gain2_parts = [None] * 2, [None] * 2, [None] * 2, [None] * 2
    chip_mid, part_mid, made, pieces_of, done = [None] * 2, [None] * 2, {}, {}, {}

    def start_piece(name):
        if not exchange:
            for ride in RIDES.get(name, ()):
                array, bit = rider(ride)
                landed(ride, swap(array, "tensor", bit))
            return
        pairs, col, cols = {
            GATE: (gu_pairs[0], 0, ff_cols),
            UP: (gu_pairs[1], 0, ff_cols),
            DOWN: (down_pairs, 0, ff_cols),
            QKV: ([(normed_in, made.get("qkv"), None, 0)], 0, q_cols + 2 * kv_cols),
            ATTN: (
                [
                    (grads_own[0], mix_own[0], None, 0),
                    (grads_own[1], mix_own[1], None, 0),
                    (grads_other[0], mix_other[0], None, 0),
                    (grads_other[1], mix_other[1], None, 0),
                ],
                0,
                q_cols,
            ),
        }[name]
        names = RIDES.get(name, ())
        bits = line_first if name in LINE_FIRST else line
        pieces_of[name] = piece(pairs, col, cols, bits, [rider(n) for n in names], 8 + len(pieces_of))
        for rode, arrived in zip(names, pieces_of[name].rode, strict=True):
            landed(rode, arrived)

    def rider(name):
        kind, chunk = name[:-1], int(name[-1])
        if kind == "core":
            return made["mid_part"], 1
        if kind == "input":
            return made["in_other"], 1
        return (chip_mid[chunk], 2) if kind == "middle" else (grads_own[chunk], 1)

    def landed(name, arrived):
        kind, chunk = name[:-1], int(name[-1])
        if kind == "core":
            made["mid_arrived"] = arrived
        elif kind == "input":
            made["in_arrived"] = [arrived]
        elif kind == "middle":
            part_mid[chunk] = arrived
        else:
            grads_other[chunk] = arrived

    def mid_other():
        made["mid_part"] = mid_part(gu_other)
        if "core0" not in riding:
            made["mid_arrived"] = order(lambda part: core_swap(part, 0), made["mid_part"])

    def mid_own():
        made["mid_own"] = mid_part(gu_own)

    def chip_middle(chunk):
        chip_mid[chunk] = order(lambda a: add(a, made["mid_own"], chunk), made["mid_arrived"])
        if f"middle{chunk}" not in riding:
            part_mid[chunk] = swap(chip_mid[chunk], "tensor", 2)

    def back_middle(chunk):
        grad_resids[chunk], grads_own[chunk], gain2_parts[chunk] = order(
            lambda part: middle_back(
                scalars, resids[chunk], chip_mid[chunk], part, cotangent, gain2, chunk, sub
            ),
            part_mid[chunk],
        )
        if f"grads{chunk}" not in riding:
            grads_other[chunk] = order(lambda own: core_swap(own, 1 + chunk), grads_own[chunk])

    def back_attend(chunk):
        made["backs"] = order(
            lambda other: attend_backward(
                scalars, grads_own[chunk], other, w_o, query, key, value, made.get("backs"),
                chunk, chunk_rows, reach[chunk], pieces,
            ),
            grads_other[chunk],
        )

    def rope():
        backs = made["backs"]
        made["qkv"], made["in_other"], made["in_own"], made["gain_q"], made["gain_k"] = order(
            lambda b: rope_backward(
                scalars, b, backs[1], backs[2], q_raw, kv_raw, gain_q, gain_k, cos, sin, w_q, w_k, w_v, share
            ),
            backs[0],
        )

    def scatter(own, arrived):
        def half_sum(block):
            return order(lambda first: add([first] + arrived[1:], own, block), arrived[0])

        sent = swap(half_sum(lambda s: 1 - s[0]), "tensor", 2)
        return half_sum(lambda s: s[0]), sent

    def in_scatter():
        made["in_kept"], made["in_sum"] = scatter(made["in_own"], made["in_arrived"])

    def project():
        *ffn_other, made["ffn_own"] = order(lambda h: project_other_first(scalars, h, w_down, share), hidden)
        made["ffn_arrived"] = [order(lambda part: core_swap(part, 4), part) for part in ffn_other]

    def ffn_scatter():
        made["ffn_kept"], made["ffn_sum"] = scatter(made["ffn_own"], made["ffn_arrived"])

    def stream_back():
        made["grad_stream"], made["gain1"] = order(
            lambda part: input_back(places, stream, made["in_kept"], part, grad_resids, gain1, sub),
            made["in_sum"],
        )

    def block_out():
        made["out"], made["stats"] = order(
            lambda part: layer_out(places, made["ffn_kept"], part, resids, chip_attn, part_attn, sub),
            made["ffn_sum"],
        )

    small_add = lambda mine, arrived: mine + arrived

    def small(axis, bit):
        made["packed"] = order(small_add, made["packed"], swap(made["packed"], axis, bit))

    def pack():
        made["packed"] = order(
            lambda g: jnp.concatenate(
                [g[0], (gain2_parts[0][0] + gain2_parts[1][0]) * 0.5, made["gain_q"][0], made["gain_k"][0]]
                + [made["stats"][i] for i in range(4)]
            ).reshape(-1, HEAD_SIZE),
            made["gain1"],
        )
        small("tensor", 1)
        small("tensor", 2)

    def second(name):
        if exchange:
            pieces_of[name].second()

    def third(name):
        if exchange:
            pieces_of[name].third()

    def fourth(name):
        if exchange:
            pieces_of[name].fourth()

    def last(name):
        if exchange:
            done[name] = pieces_of[name].last()

    def send_small(bit):
        if exchange:
            made["small"] = swap(made["packed"], "dp", bit)

    def add_small():
        if exchange:
            made["packed"] = order(small_add, made["packed"], made["small"])

    mid_other()
    start_piece(GATE)
    mid_own()
    chip_middle(0)
    chip_middle(1)
    start_piece(UP)
    start_piece(DOWN)
    back_middle(0)
    back_attend(0)
    back_middle(1)
    second(GATE)
    back_attend(1)
    second(UP)
    start_piece(ATTN)
    rope()
    start_piece(QKV)
    in_scatter()
    third(GATE)
    second(DOWN)
    project()
    third(UP)
    ffn_scatter()
    stream_back()
    fourth(GATE)
    second(QKV)
    block_out()
    third(DOWN)
    fourth(UP)
    second(ATTN)
    pack()
    send_small(1)
    last(GATE)
    add_small()
    send_small(2)
    third(QKV)
    last(UP)
    add_small()
    send_small(4)
    fourth(DOWN)
    fourth(QKV)
    add_small()
    third(ATTN)
    last(DOWN)
    fourth(ATTN)
    last(QKV)
    last(ATTN)
    if exchange:
        grad_w_o = done[ATTN]
        grad_w_q, grad_w_kv = done[QKV][:, :q_cols], done[QKV][:, q_cols:]
        grad_w_gu = jnp.stack([done[GATE], done[UP]], axis=1)
        grad_w_down = done[DOWN]
        totals = made["packed"].reshape(-1)
    else:
        bit = 1
        while bit < dp_ways:
            small("dp", bit)
            bit *= 2
        totals = made["packed"].reshape(-1)

        def reduced(pairs):
            total = sum(
                dot(left, (right if plane is None else right[plane])[block * left.shape[0] :][: left.shape[0]], TN)
                for left, right, plane, block in pairs
            )
            return f32(lax.psum_scatter(b16(total), "dp", scatter_dimension=0, tiled=True))

        qkv = reduced([(normed_in, made["qkv"], None, 0)])
        grad_w_q, grad_w_kv = qkv[:, :q_cols], qkv[:, q_cols:]
        grad_w_o = sum(
            dot(left, right, TN)
            for left, right in zip(grads_own + grads_other, mix_own + mix_other, strict=True)
        )
        grad_w_o = f32(lax.psum_scatter(b16(grad_w_o), "dp", scatter_dimension=0, tiled=True))
        grad_w_gu = jnp.stack([reduced(gu_pairs[0]), reduced(gu_pairs[1])], axis=1)
        grad_w_down = reduced(down_pairs)
    cuts = (width, 2 * width, 2 * width + HEAD_SIZE, 2 * width + 2 * HEAD_SIZE)
    stat_total = totals[cuts[3] :].reshape(4, HEAD_SIZE)[:, 0]
    stats = jnp.sqrt(stat_total[:3] / (stat_total[3] * MODEL_WIDTH))
    return (
        made["out"],
        made["grad_stream"],
        grad_w_q,
        grad_w_kv.reshape(-1, 2, kv_cols),
        grad_w_o,
        grad_w_gu,
        grad_w_down,
        totals[: cuts[0]],
        totals[cuts[0] : cuts[1]],
        totals[cuts[1] : cuts[2]],
        totals[cuts[2] : cuts[3]],
        stats,
    )


def solution(mesh):
    placed = (
        P("dp", None),
        P("dp", None),
        P("dp"),
        P("dp", None),
        P("dp", None),
        P(),
        P(None, "tensor"),
        P(None, None, "tensor"),
        P(),
        P(),
        P(None, "tensor"),
        P(),
        P(None, None, "tensor"),
        P(None, "tensor"),
    )
    return jax.shard_map(
        per_device,
        mesh=mesh,
        in_specs=placed,
        out_specs=(
            P(("dp", "tensor"), None),
            P(("dp", "tensor"), None),
            P("dp", "tensor"),
            P("dp", None, "tensor"),
            P("dp", "tensor"),
            P("dp", None, "tensor"),
            P("dp", "tensor"),
            P(),
            P(),
            P(),
            P(),
            P(),
        ),
        check_vma=False,
    )
```

```python
import math

import jax
import jax.numpy as jnp
import numpy as np
from jax import lax
from jax.experimental import pallas as pl
from jax.experimental.pallas import tpu as pltpu
from jax.sharding import PartitionSpec as P

MODEL_WIDTH = 2048
HEAD_SIZE = 128
SEQ_LEN = 1024
EPSILON = 1e-06
MASKED = -1e30
SCALE = HEAD_SIZE ** (-0.5)
F32 = jnp.float32
BF16 = jnp.bfloat16
VMEM_BYTES = 60 * 1024 * 1024
NN = (((1,), (0,)), ((), ()))
NT = (((1,), (1,)), ((), ()))
TN = (((0,), (0,)), ((), ()))
SPLIT = 1
FLIPPED = -1
GATE, UP, DOWN, QKV, ATTN = range(5)
LINE_FIRST = (GATE,)
RIDES = {GATE: ("core0",), QKV: ("input0",)}


def dot(left, right, dims=NN):
    return lax.dot_general(left, right, dims, preferred_element_type=F32)


def f32(values):
    return values.astype(F32)


def b16(values):
    return values.astype(BF16)


def shape(dims, kind=BF16):
    return jax.ShapeDtypeStruct(dims, kind)


MESH_IDS = pl.DeviceIdType.MESH


def partner(bit):
    mine = lax.axis_index("tensor")
    return {"tensor": mine + bit * (1 - 2 * (mine // bit % 2))}


def exchange_copies(bits, sources, targets, sems):
    return [
        pltpu.make_async_remote_copy(
            src_ref=source,
            dst_ref=target,
            send_sem=sems.at[0, index],
            recv_sem=sems.at[1, index],
            device_id=partner(bit),
            device_id_type=MESH_IDS,
        )
        for index, (bit, source, target) in enumerate(zip(bits, sources, targets, strict=True))
    ]


def meet(bits):
    barrier = pltpu.get_barrier_semaphore()
    for bit in sorted(set(bits)):
        pl.semaphore_signal(barrier, inc=1, device_id=partner(bit), device_id_type=MESH_IDS)
    pl.semaphore_wait(barrier, len(set(bits)))


def call_with_riders(body, outs, grid, in_specs, out_specs, args, name, riders, ident):
    bits = [bit for _, bit in riders]
    count, inputs, results = len(riders), len(args), len(outs)

    def riding(*refs):
        own_in, sources = refs[:inputs], refs[inputs : inputs + count]
        rest = refs[inputs + count :]
        own_out, targets, sems = rest[:results], rest[results : results + count], rest[-1]

        @pl.when(pl.program_id(0) == 0)
        def _():
            meet(bits)
            for copy in exchange_copies(bits, sources, targets, sems):
                copy.start()

        body(*own_in, *own_out)

        @pl.when(pl.program_id(0) == grid[0] - 1)
        def _():
            for copy in exchange_copies(bits, sources, targets, sems):
                copy.wait()

    far = pl.BlockSpec(memory_space=pl.ANY)
    return pl.pallas_call(
        riding,
        out_shape=list(outs) + [shape(array.shape, array.dtype) for array, _ in riders],
        grid_spec=pltpu.PrefetchScalarGridSpec(
            num_scalar_prefetch=0,
            grid=grid,
            in_specs=list(in_specs) + [far] * count,
            out_specs=list(out_specs) + [far] * count,
            scratch_shapes=[pltpu.SemaphoreType.DMA((2, count))],
        ),
        compiler_params=pltpu.CompilerParams(
            vmem_limit_bytes=VMEM_BYTES, collective_id=ident, has_side_effects=True
        ),
        cost_estimate=pl.CostEstimate(flops=1024, bytes_accessed=1024, transcendentals=0),
        name=name,
    )(*args, *[array for array, _ in riders])


def call(body, outs, grid, in_specs, out_specs, args, name, scalars=None, scratch=(), alias=None):
    count = 0 if scalars is None else 1
    return pl.pallas_call(
        body,
        out_shape=outs,
        grid_spec=pltpu.PrefetchScalarGridSpec(
            num_scalar_prefetch=count,
            grid=grid,
            in_specs=in_specs,
            out_specs=out_specs,
            scratch_shapes=scratch,
        ),
        compiler_params=pltpu.CompilerParams(vmem_limit_bytes=VMEM_BYTES),
        cost_estimate=pl.CostEstimate(flops=1024, bytes_accessed=1024, transcendentals=0),
        input_output_aliases=alias or {},
        name=name,
    )(*(() if scalars is None else (scalars,)), *args)


def whole(array):
    dims = array.shape
    return pl.BlockSpec(dims, lambda *_: (0,) * len(dims))


def rms_scale(values):
    return lax.rsqrt(jnp.mean(values * values, axis=-1, keepdims=True) + EPSILON)


def norm_back(values, gain, grad):
    scale = rms_scale(values)
    weighted = grad * gain
    along = jnp.mean(weighted * values, axis=-1, keepdims=True)
    grad_values = scale * weighted - values * (scale * scale * scale * along)
    grad_gain = jnp.sum(grad * (values * scale), axis=0, keepdims=True)
    return grad_values, grad_gain


def rope_tables():
    half = HEAD_SIZE // 2
    inverse = np.exp(np.arange(half) * (-2.0 * math.log(1000000.0) / HEAD_SIZE))
    angles = np.arange(SEQ_LEN)[:, None] * inverse[None, :]
    cos, sin = np.cos(angles), np.sin(angles)
    wide_cos = np.concatenate([cos, cos], axis=1).astype(np.float32)
    wide_sin = np.concatenate([-sin, sin], axis=1).astype(np.float32)
    return wide_cos, wide_sin


def rotate(values, cos, sin):
    return values * cos + pltpu.roll(values, HEAD_SIZE // 2, 1) * sin


def rotate_back(values, cos, sin):
    return values * cos - pltpu.roll(values, HEAD_SIZE // 2, 1) * sin


def head(index):
    return slice(index * HEAD_SIZE, (index + 1) * HEAD_SIZE)


def norm_query(stream, gain, w_q, rows):
    tokens, width = stream.shape
    cols = w_q.shape[1]

    def body(stream_ref, gain_ref, w_ref, normed_ref, query_ref):
        values = f32(stream_ref[...])
        normed = b16(values * rms_scale(values) * gain_ref[...])
        normed_ref[...] = normed
        query_ref[...] = dot(normed, w_ref[...])

    return call(
        body,
        [shape((tokens, width)), shape((tokens, cols), F32)],
        (tokens // rows,),
        [pl.BlockSpec((rows, width), lambda i: (i, 0)), whole(gain), whole(w_q)],
        [pl.BlockSpec((rows, width), lambda i: (i, 0)), pl.BlockSpec((rows, cols), lambda i: (i, 0))],
        (stream, gain, w_q),
        "norm_query",
    )


def rope_forward(q_raw, kv_raw, q_gain, k_gain, cos, sin, rows):
    tokens, q_cols = q_raw.shape
    kv_cols = kv_raw.shape[2]

    def body(q_ref, kv_ref, qg_ref, kg_ref, cos_ref, sin_ref, q_out, k_out, v_out):
        cos_rows, sin_rows = cos_ref[...], sin_ref[...]
        for h in range(q_cols // HEAD_SIZE):
            values = q_ref[:, head(h)]
            q_out[:, head(h)] = b16(rotate(values * rms_scale(values) * qg_ref[...], cos_rows, sin_rows))
        for h in range(kv_cols // HEAD_SIZE):
            values = kv_ref[0, :, head(h)]
            k_out[:, head(h)] = b16(rotate(values * rms_scale(values) * kg_ref[...], cos_rows, sin_rows))
        v_out[...] = b16(kv_ref[1])

    row = lambda cols: pl.BlockSpec((rows, cols), lambda i: (i, 0))
    return call(
        body,
        [shape((tokens, q_cols)), shape((tokens, kv_cols)), shape((tokens, kv_cols))],
        (tokens // rows,),
        [
            row(q_cols),
            pl.BlockSpec((2, rows, kv_cols), lambda i: (0, i, 0)),
            whole(q_gain),
            whole(k_gain),
            row(HEAD_SIZE),
            row(HEAD_SIZE),
        ],
        [row(q_cols), row(kv_cols), row(kv_cols)],
        (q_raw, kv_raw, q_gain, k_gain, cos, sin),
        "rope_forward",
    )


def key_limit(scalars, start, count, pieces):
    position = start + lax.broadcasted_iota(jnp.int32, (count, 1), 0)
    limit = position + 1
    for piece in range(pieces):
        first, last = scalars[2 + 2 * piece], scalars[3 + 2 * piece]
        inside = (position >= first) & (position < last)
        limit = jnp.where(inside, jnp.maximum(limit, last), limit)
    return jnp.minimum(limit, scalars[1])


def soft_weights(query, keys, limit):
    scores = dot(query, keys, NT) * SCALE
    key_pos = lax.broadcasted_iota(jnp.int32, scores.shape, 1)
    scores = jnp.where(key_pos < limit, scores, MASKED)
    shifted = jnp.exp(scores - jnp.max(scores, axis=-1, keepdims=True))
    return shifted / jnp.sum(shifted, axis=-1, keepdims=True)


def attend_forward(scalars, query, key, value, w_o, chunk, count, reach, pieces):
    q_cols, kv_cols, width = query.shape[1], key.shape[1], w_o.shape[0]
    heads, half = q_cols // HEAD_SIZE, count // 2
    repeat = q_cols // kv_cols

    def body(scalars, q_ref, k_ref, v_ref, w_ref, own_out, other_out, own_mix, other_mix, mixed):
        limit = key_limit(scalars, chunk * count, count, pieces)
        for h in range(heads):
            weights = soft_weights(q_ref[:, head(h)], k_ref[:, head(h // repeat)], limit)
            mixed[:, head(h)] = b16(dot(b16(weights), v_ref[:, head(h // repeat)]))
        core = scalars[0]
        other = mixed[pl.ds(pl.multiple_of((1 - core) * half, half), half), :]
        own = mixed[pl.ds(pl.multiple_of(core * half, half), half), :]
        other_mix[...] = other
        own_mix[...] = own
        other_out[...] = b16(dot(other, w_ref[...], NT))
        own_out[...] = b16(dot(own, w_ref[...], NT))

    return call(
        body,
        [shape((half, width)), shape((half, width)), shape((half, q_cols)), shape((half, q_cols))],
        (1,),
        [
            pl.BlockSpec((count, q_cols), lambda i, s: (chunk, 0)),
            pl.BlockSpec((reach, kv_cols), lambda i, s: (0, 0)),
            pl.BlockSpec((reach, kv_cols), lambda i, s: (0, 0)),
            whole(w_o),
        ],
        [
            pl.BlockSpec((half, width), lambda i, s: (0, 0)),
            pl.BlockSpec((half, width), lambda i, s: (0, 0)),
            pl.BlockSpec((half, q_cols), lambda i, s: (0, 0)),
            pl.BlockSpec((half, q_cols), lambda i, s: (0, 0)),
        ],
        (query, key, value, w_o),
        "attend_forward",
        scalars,
        [pltpu.VMEM((count, q_cols), BF16)],
    )


def row_specs(rows, sub, width, chunk):
    steps = rows // sub
    picked = pl.BlockSpec((sub, width), lambda i, s: ((2 * chunk + s[0]) * steps + i, 0))
    return picked, pl.BlockSpec((sub, width), lambda i, s: (i, 0))


def middle(scalars, stream, chip, part, gain, chunk, sub):
    rows, width = chip.shape

    def body(scalars, stream_ref, chip_ref, part_ref, gain_ref, resid_out, normed_out):
        resid = f32(stream_ref[...]) + (f32(chip_ref[...]) + f32(part_ref[...]))
        resid_out[...] = resid
        normed_out[...] = b16(resid * rms_scale(resid) * gain_ref[...])

    picked, row = row_specs(rows, sub, width, chunk)
    return call(
        body,
        [shape((rows, width), F32), shape((rows, width))],
        (rows // sub,),
        [picked, row, row, whole(gain)],
        [row, row],
        (stream, chip, part, gain),
        "middle",
        scalars,
    )


def gate_back(scalars, gate_up, grad_hidden, before, chunk, rows, sub):
    planes, _, cols = gate_up.shape
    tokens = grad_hidden.shape[0]
    steps = rows // sub
    natural = lambda i, s: ((2 * chunk + (s[0] + i // steps) % 2) * steps + i % steps, 0)

    def body(scalars, gu_ref, gh_ref, *rest):
        hidden_out, own_out, other_out = rest[-3:]
        gate, up, grad = gu_ref[0], gu_ref[1], gh_ref[...]
        logistic = 1.0 / (1.0 + jnp.exp(-gate))
        silu = gate * logistic
        hidden_out[...] = b16(silu * up)
        grad_gate = b16(grad * up * logistic * (1.0 + gate * (1.0 - logistic)))
        grad_up = b16(grad * silu)

        @pl.when(pl.program_id(0) < steps)
        def _():
            own_out[0], own_out[1] = grad_gate, grad_up

        @pl.when(pl.program_id(0) >= steps)
        def _():
            other_out[0], other_out[1] = grad_gate, grad_up

    args = [gate_up, grad_hidden]
    specs = [
        pl.BlockSpec((planes, sub, cols), lambda i, s: (0, i, 0)),
        pl.BlockSpec((sub, cols), natural),
    ]
    alias = None
    if before is not None:
        args += list(before)
        specs += [pl.BlockSpec(memory_space=pl.ANY)] * 3
        alias = {3: 0, 4: 1, 5: 2}
    part = shape((planes, tokens // 2, cols))
    return call(
        body,
        [shape((tokens, cols)), part, part],
        (2 * steps,),
        specs,
        [
            pl.BlockSpec((sub, cols), natural),
            pl.BlockSpec((planes, sub, cols), lambda i, s: (0, chunk * steps + jnp.minimum(i, steps - 1), 0)),
            pl.BlockSpec((planes, sub, cols), lambda i, s: (0, chunk * steps + jnp.maximum(i - steps, 0), 0)),
        ],
        args,
        "gate_back",
        scalars,
        (),
        alias,
    )


def by_side(groups, product, other_outs, own_out):
    @pl.when(pl.program_id(0) < groups)
    def _():
        for index, other_out in enumerate(other_outs):
            cols = other_out.shape[1]
            other_out[...] = product[:, index * cols : (index + 1) * cols]

    @pl.when(pl.program_id(0) >= groups)
    def _():
        own_out[...] = product


def side_specs(groups, rows, width):
    part = pl.BlockSpec((rows, width // SPLIT), lambda i, s: (jnp.minimum(i, groups - 1), 0))
    return [part] * SPLIT + [pl.BlockSpec((rows, width), lambda i, s: (jnp.maximum(i - groups, 0), 0))]


def project_other_first(scalars, values, weights, rows):
    tokens, depth = values.shape
    width = weights.shape[0]
    groups = tokens // (2 * rows)
    natural = lambda i, s: 2 * (i % groups) + (s[0] + 1 + i // groups) % 2

    def body(scalars, values_ref, weights_ref, *outs):
        product = b16(dot(values_ref[...], weights_ref[...], NT))
        by_side(groups, product, outs[:-1], outs[-1])

    return call(
        body,
        [shape((tokens // 2, width // SPLIT))] * SPLIT + [shape((tokens // 2, width))],
        (tokens // rows,),
        [pl.BlockSpec((rows, depth), lambda i, s: (natural(i, s), 0)), whole(weights)],
        side_specs(groups, rows, width),
        (values, weights),
        "project",
        scalars,
    )


def add_gain(gain_out, gain):
    @pl.when(pl.program_id(0) == 0)
    def _():
        gain_out[...] = jnp.zeros_like(gain_out)

    gain_out[...] += gain


def middle_back(scalars, resid, chip, part, cotangent, gain, chunk, sub):
    rows, width = resid.shape

    def body(scalars, resid_ref, chip_ref, part_ref, cot_ref, gain_ref, resid_out, attn_out, gain_out):
        grad = f32(chip_ref[...]) + f32(part_ref[...])
        back, gain_part = norm_back(resid_ref[...], gain_ref[...], grad)
        add_gain(gain_out, gain_part)
        total = f32(cot_ref[...]) + back
        resid_out[...] = total
        attn_out[...] = b16(total)

    picked, row = row_specs(rows, sub, width, chunk)
    return call(
        body,
        [shape((rows, width), F32), shape((rows, width)), shape((1, width), F32)],
        (rows // sub,),
        [row, row, row, picked, whole(gain)],
        [row, row, pl.BlockSpec((1, width), lambda i, s: (0, 0))],
        (resid, chip, part, cotangent, gain),
        "middle_back",
        scalars,
    )


def attend_backward(scalars, own, other, w_o, query, key, value, before, chunk, count, reach, pieces):
    tokens, q_cols = query.shape
    kv_cols, width = key.shape[1], w_o.shape[0]
    heads, half = q_cols // HEAD_SIZE, count // 2
    repeat = q_cols // kv_cols
    old = 0 if before is None else before[1].shape[0]

    def body(scalars, own_ref, other_ref, w_ref, q_ref, k_ref, v_ref, *rest):
        olds = rest[: len(rest) - 4]
        q_out, k_out, v_out, mixed = rest[len(rest) - 4 :]
        core = scalars[0]
        w = w_ref[...]
        mixed[pl.ds(pl.multiple_of(core * half, half), half), :] = b16(dot(own_ref[...], w))
        mixed[pl.ds(pl.multiple_of((1 - core) * half, half), half), :] = b16(dot(other_ref[...], w))
        limit = key_limit(scalars, chunk * count, count, pieces)
        for g in range(kv_cols // HEAD_SIZE):
            k_total, v_total = 0.0, 0.0
            for h in range(g * repeat, (g + 1) * repeat):
                q_head, k_head, grad = q_ref[:, head(h)], k_ref[:, head(g)], mixed[:, head(h)]
                weights = soft_weights(q_head, k_head, limit)
                grad_weights = dot(grad, v_ref[:, head(g)], NT)
                delta = jnp.sum(weights * grad_weights, axis=-1, keepdims=True)
                grad_scores = b16(weights * (grad_weights - delta))
                q_out[:, head(h)] = dot(grad_scores, k_head) * SCALE
                k_total = k_total + dot(grad_scores, q_head, TN)
                v_total = v_total + dot(b16(weights), grad, TN)
            k_out[:, head(g)] = k_total * SCALE
            v_out[:, head(g)] = v_total
        if old:
            k_out[:old, :] += olds[1][...]
            v_out[:old, :] += olds[2][...]

    flat = pl.BlockSpec((half, width), lambda i, s: (0, 0))
    keys = pl.BlockSpec((reach, kv_cols), lambda i, s: (0, 0))
    args = [own, other, w_o, query, key, value]
    specs = [flat, flat, whole(w_o), pl.BlockSpec((count, q_cols), lambda i, s: (chunk, 0)), keys, keys]
    alias = None
    if before is not None:
        args += list(before)
        specs += [pl.BlockSpec(memory_space=pl.ANY), whole(before[1]), whole(before[2])]
        alias = {7: 0}
    return call(
        body,
        [shape((tokens, q_cols), F32), shape((reach, kv_cols), F32), shape((reach, kv_cols), F32)],
        (1,),
        specs,
        [pl.BlockSpec((count, q_cols), lambda i, s: (chunk, 0)), keys, keys],
        args,
        "attend_backward",
        scalars,
        [pltpu.VMEM((count, q_cols), BF16)],
        alias,
    )


def rope_backward(scalars, grad_q, grad_k, grad_v, q_raw, kv_raw, q_gain, k_gain, cos, sin, w_q, w_k, w_v, rows):
    tokens, q_cols = q_raw.shape
    kv_cols, width = kv_raw.shape[2], w_q.shape[0]
    all_cols, heads = q_cols + 2 * kv_cols, q_cols // HEAD_SIZE
    groups = tokens // (2 * rows)
    natural = lambda i, s: 2 * (i % groups) + (s[0] + 1 + i // groups) % 2

    def body(
        scalars, gq_ref, gk_ref, gv_ref, q_ref, kv_ref, qg_ref, kg_ref, cos_ref, sin_ref, wq_ref, wk_ref, wv_ref,
        qkv_out, *outs,
    ):
        *other_outs, own_out, qg_out, kg_out = outs
        step = pl.program_id(0)

        @pl.when(step == 0)
        def _():
            qg_out[...] = jnp.zeros_like(qg_out)
            kg_out[...] = jnp.zeros_like(kg_out)

        cos_rows, sin_rows = cos_ref[...], sin_ref[...]
        for h in range(q_cols // HEAD_SIZE):
            grad = rotate_back(gq_ref[:, head(h)], cos_rows, sin_rows)
            back, gain = norm_back(q_ref[:, head(h)], qg_ref[...], grad)
            qkv_out[:, head(h)] = b16(back)
            qg_out[...] += gain
        for h in range(kv_cols // HEAD_SIZE):
            grad = rotate_back(gk_ref[:, head(h)], cos_rows, sin_rows)
            back, gain = norm_back(kv_ref[:, head(h)], kg_ref[...], grad)
            qkv_out[:, head(heads + h)] = b16(back)
            kg_out[...] += gain
        qkv_out[:, q_cols + kv_cols :] = b16(gv_ref[...])
        total = dot(qkv_out[:, :q_cols], wq_ref[...], NT)
        total = total + dot(qkv_out[:, q_cols : q_cols + kv_cols], wk_ref[...], NT)
        total = total + dot(qkv_out[:, q_cols + kv_cols :], wv_ref[...], NT)
        by_side(groups, b16(total), other_outs, own_out)

    row = lambda cols: pl.BlockSpec((rows, cols), lambda i, s: (natural(i, s), 0))
    gain_spec = pl.BlockSpec((1, HEAD_SIZE), lambda i, s: (0, 0))
    return call(
        body,
        [
            shape((tokens, all_cols)),
            *[shape((tokens // 2, width // SPLIT))] * SPLIT,
            shape((tokens // 2, width)),
            shape((1, HEAD_SIZE), F32),
            shape((1, HEAD_SIZE), F32),
        ],
        (tokens // rows,),
        [
            row(q_cols),
            row(kv_cols),
            row(kv_cols),
            row(q_cols),
            pl.BlockSpec((None, rows, kv_cols), lambda i, s: (0, natural(i, s), 0)),
            whole(q_gain),
            whole(k_gain),
            row(HEAD_SIZE),
            row(HEAD_SIZE),
            whole(w_q),
            whole(w_k),
            whole(w_v),
        ],
        [
            row(all_cols),
            *side_specs(groups, rows, width),
            gain_spec,
            gain_spec,
        ],
        (grad_q, grad_k, grad_v, q_raw, kv_raw, q_gain, k_gain, cos, sin, w_q, w_k, w_v),
        "rope_backward",
        scalars,
    )


def input_back(places, stream, kept, part, resids, gain, sub):
    rows, width = kept.shape

    def body(places, stream_ref, kept_ref, part_ref, first_ref, second_ref, gain_ref, out, gain_out):
        grad = f32(kept_ref[...]) + f32(part_ref[...])
        back, gain_part = norm_back(f32(stream_ref[...]), gain_ref[...], grad)
        add_gain(gain_out, gain_part)
        resid = jnp.where(places[0] == 0, first_ref[...], second_ref[...])
        out[...] = b16(resid + back)

    steps = rows // sub
    row = pl.BlockSpec((sub, width), lambda i, s: (i, 0))
    return call(
        body,
        [shape((rows, width)), shape((1, width), F32)],
        (steps,),
        [pl.BlockSpec((sub, width), lambda i, s: (s[1] * steps + i, 0)), row, row, row, row, whole(gain)],
        [row, pl.BlockSpec((1, width), lambda i, s: (0, 0))],
        (stream, kept, part, *resids, gain),
        "input_back",
        places,
    )


def layer_out(places, kept, part, resids, chips, parts, sub):
    rows, width = kept.shape
    steps = rows // sub

    def body(places, kept_ref, part_ref, *rest):
        resid_refs, chip_refs, part_refs = rest[0:2], rest[2:4], rest[4:6]
        out, sums_out = rest[6:]
        first = places[0] == 0
        ffn = f32(kept_ref[...]) + f32(part_ref[...])
        attns = [f32(chip_refs[i][...]) + f32(part_refs[i][...]) for i in range(2)]
        attn = jnp.where(first, attns[0], attns[1])
        total = jnp.where(first, resid_refs[0][...], resid_refs[1][...]) + ffn
        out[...] = b16(total)
        position = places[1] * rows + pl.program_id(0) * sub + lax.broadcasted_iota(jnp.int32, (sub, 1), 0)
        live = position < places[2]
        for index, values in enumerate((total, attn, ffn)):
            rows_sum = jnp.sum(jnp.where(live, values * values, 0.0), axis=1, keepdims=True)
            one = jnp.sum(rows_sum, axis=0, keepdims=True)
            add_row(sums_out, index, one)
        add_row(sums_out, 3, jnp.sum(jnp.where(live, 1.0, 0.0), axis=0, keepdims=True))

    row = pl.BlockSpec((sub, width), lambda i, s: (i, 0))
    return call(
        body,
        [shape((rows, width)), shape((8, HEAD_SIZE), F32)],
        (steps,),
        [row] * 8,
        [row, pl.BlockSpec((8, HEAD_SIZE), lambda i, s: (0, 0))],
        (kept, part, *resids, *chips, *parts),
        "layer_out",
        places,
    )


def add_row(sums_out, index, one):
    wide = jnp.broadcast_to(one, (1, HEAD_SIZE))

    @pl.when(pl.program_id(0) == 0)
    def _():
        sums_out[index : index + 1, :] = wide

    @pl.when(pl.program_id(0) > 0)
    def _():
        sums_out[index : index + 1, :] += wide


def split_pair(weights, rows):
    depth, _, cols = weights.shape

    def body(weights_ref, first_out, second_out):
        values = weights_ref[...]
        first_out[...] = values[:, 0, :]
        second_out[...] = values[:, 1, :]

    row = pl.BlockSpec((rows, cols), lambda i: (i, 0))
    return call(
        body,
        [shape((depth, cols)), shape((depth, cols))],
        (depth // rows,),
        [pl.BlockSpec((rows, 2, cols), lambda i: (i, 0, 0))],
        [row, row],
        (weights,),
        "split_pair",
    )


def block_order(bits):
    order = [0]
    for bit in reversed(bits[1:]):
        order = order + [k ^ bit for k in order]
    return order


def flipped(index, value):
    bit = 1
    while bit <= value:
        if value & bit:
            index = index + bit * (1 - 2 * (index // bit % 2))
        bit *= 2
    return index


def weight_grad(pairs, col, cols, bits, ways, riders, ident):
    width = pairs[0][0].shape[1]
    rows = width // ways
    own = block_order(bits)
    count, half = len(own), len(own) // 2

    def source(index):
        def place(i):
            mine = flipped(lax.axis_index("dp"), own[index])
            return (0, i * mine + (1 - i) * flipped(mine, bits[0]))

        return place

    args, specs = [], []
    for left, right, plane, block in pairs:
        depth = left.shape[0]
        args += [left] * count + [right]
        specs += [pl.BlockSpec((depth, rows), source(index)) for index in range(count)]
        if plane is None:
            specs.append(pl.BlockSpec((depth, cols), lambda i, b=block: (b, col)))
        else:
            specs.append(pl.BlockSpec((None, depth, cols), lambda i, p=plane, b=block: (p, b, col)))

    def body(*refs):
        send_out, keep_out, next_out = refs[-3:]
        total = 0.0
        for index in range(len(pairs)):
            part = refs[index * (count + 1) : (index + 1) * (count + 1)]
            left = jnp.concatenate([ref[...] for ref in part[:-1]], axis=1)
            total = total + dot(left, part[-1][...], TN)
        product = b16(total)

        @pl.when(pl.program_id(0) == 0)
        def _():
            send_out[...] = product

        @pl.when(pl.program_id(0) == 1)
        def _():
            keep_out[...] = product[: half * rows]
            next_out[...] = product[half * rows :]

    flat = lambda blocks: pl.BlockSpec((blocks * rows, cols), lambda i: (0, 0))
    outs = [shape((count * rows, cols)), shape((half * rows, cols)), shape((half * rows, cols))]
    out_specs = [flat(count), flat(half), flat(half)]
    if riders:
        return call_with_riders(body, outs, (2,), specs, out_specs, args, "weight_grad", riders, ident)
    return call(body, outs, (2,), specs, out_specs, args, "weight_grad")


def add_parts(parts, rows, kind, scalars=None):
    parts = [(array if isinstance(array, list) else [array], block) for array, block in parts]
    cols = sum(array.shape[1] for array in parts[0][0])
    steps = 4 if rows * cols >= 512 * 1024 else 2
    sub = rows // steps

    def body(*refs):
        refs = list(refs if scalars is None else refs[1:])
        total = 0.0
        for arrays, _ in parts:
            values = [f32(refs.pop(0)[...]) for _ in arrays]
            total = total + (values[0] if len(values) == 1 else jnp.concatenate(values, axis=1))
        refs[0][...] = total.astype(kind)

    def spec(block, cols):
        if callable(block):
            return pl.BlockSpec((sub, cols), lambda i, s: (block(s) * steps + i, 0))
        if block is FLIPPED:
            return pl.BlockSpec((sub, cols), lambda i, *s: ((i + steps // 2) % steps, 0))
        return pl.BlockSpec((sub, cols), lambda i, *s: (block * steps + i, 0))

    return call(
        body,
        shape((rows, cols), kind),
        (steps,),
        [spec(block, array.shape[1]) for arrays, block in parts for array in arrays],
        pl.BlockSpec((sub, cols), lambda i, *s: (i, 0)),
        [array for arrays, _ in parts for array in arrays],
        "add_parts",
        scalars,
    )


def swap(values, axis, bit):
    ways = lax.axis_size(axis)
    return lax.ppermute(values, axis, [(i, i ^ bit) for i in range(ways)])


def core_swap(values, ident):
    def body(in_ref, out_ref, sems):
        meet([1])
        (copy,) = exchange_copies([1], [in_ref], [out_ref], sems)
        copy.start()
        copy.wait()

    return pl.pallas_call(
        body,
        out_shape=shape(values.shape, values.dtype),
        in_specs=[pl.BlockSpec(memory_space=pl.ANY)],
        out_specs=pl.BlockSpec(memory_space=pl.ANY),
        scratch_shapes=[pltpu.SemaphoreType.DMA((2, 1))],
        compiler_params=pltpu.CompilerParams(collective_id=ident, has_side_effects=True),
        cost_estimate=pl.CostEstimate(flops=1024, bytes_accessed=1024, transcendentals=0),
        name="core_swap",
    )(values)


class Order:
    def __init__(self):
        self.last = None

    def __call__(self, function, first, *rest, **named):
        if self.last is not None:
            first, _ = lax.optimization_barrier((first, self.last))
        result = function(first, *rest, **named)
        self.last = jax.tree.leaves(result)[-1]
        return result


class Piece:
    def __init__(self, order, pairs, col, cols, bits, ways, riders, ident):
        self.order, self.bits = order, bits
        run = lambda array: weight_grad(
            [(array, *pairs[0][1:])] + pairs[1:], col, cols, bits, ways, riders, ident
        )
        self.send, self.keep, self.next, *self.rode = order(run, pairs[0][0])
        self.start()

    def start(self):
        self.arrived = swap(self.send, "dp", self.bits[0])


class LinePiece(Piece):
    def second(self):
        add = lambda arrived: add_parts([(arrived, 1), (self.next, 0)], self.next.shape[0], BF16)
        self.far = self.order(add, self.arrived)
        self.arrived2 = lax.ppermute(self.far, "dp", [(0, 2), (1, 3), (6, 4), (7, 5)])

    def third(self):
        add = lambda arrived: add_parts([(arrived, FLIPPED), (self.far, 0)], self.far.shape[0], BF16)
        self.arrived3 = lax.ppermute(self.order(add, self.arrived2), "dp", [(2, 4), (4, 2), (3, 5), (5, 3)])

    def fourth(self):
        half = self.keep.shape[0] // 2
        add = lambda arrived: add_parts([(arrived, 0), (self.arrived, 1), (self.keep, 1)], half, BF16)
        self.arrived4 = swap(self.order(add, self.arrived3), "dp", 2)

    def last(self):
        half = self.keep.shape[0] // 2
        add = lambda arrived: add_parts(
            [(arrived, 0), (self.arrived3, 1), (self.arrived, 0), (self.keep, 0)], half, F32
        )
        return self.order(add, self.arrived4)


class LineFirstPiece(Piece):
    def start(self):
        self.arrived = lax.ppermute(self.send, "dp", [(0, 2), (1, 3), (6, 4), (7, 5)])

    def second(self):
        add = lambda arrived: add_parts([(arrived, FLIPPED), (self.send, 0)], self.send.shape[0], BF16)
        self.arrived2 = lax.ppermute(self.order(add, self.arrived), "dp", [(2, 4), (4, 2), (3, 5), (5, 3)])

    def third(self):
        add = lambda arrived: add_parts([(arrived, 0), (self.next, 0)], self.next.shape[0], BF16)
        self.arrived3 = swap(self.order(add, self.arrived2), "dp", 2)

    def fourth(self):
        half = self.keep.shape[0] // 2
        add = lambda arrived: add_parts([(arrived, 1), (self.arrived2, 3), (self.keep, 1)], half, BF16)
        self.arrived4 = swap(self.order(add, self.arrived3), "dp", 1)

    def last(self):
        half = self.keep.shape[0] // 2
        add = lambda arrived: add_parts(
            [(arrived, 0), (self.arrived3, 0), (self.arrived2, 2), (self.keep, 0)], half, F32
        )
        return self.order(add, self.arrived4)


def per_device(
    stream,
    cotangent,
    live_mask,
    piece_start,
    piece_len,
    norm1_gain,
    w_q,
    key_value_weight,
    q_gain,
    k_gain,
    w_o,
    norm2_gain,
    w_gu,
    w_down,
):
    tokens, width = stream.shape
    pieces = piece_start.shape[1]
    piece_span = SEQ_LEN // pieces
    tensor_ways, dp_ways = lax.axis_size("tensor"), lax.axis_size("dp")
    assert tensor_ways == 4 and tokens == SEQ_LEN and piece_start.shape[0] == 1
    tensor_index = lax.axis_index("tensor")
    group, core = tensor_index // 2, tensor_index % 2
    share = tokens // tensor_ways
    sub = share // 4
    q_cols, kv_cols = w_q.shape[1], key_value_weight.shape[2]
    ff_cols = w_down.shape[1]
    chunk_rows = 2 * share
    reach = [-(-(chunk_rows * (i + 1)) // piece_span) * piece_span for i in range(2)]
    cos, sin = rope_tables()

    live_count = jnp.sum(live_mask)
    ends = piece_start[0] + piece_len[0]
    spans = jnp.stack([piece_start[0], ends], axis=1).reshape(-1)
    scalars = jnp.concatenate([jnp.stack([core, live_count]), spans]).astype(jnp.int32)
    places = jnp.stack([group, tensor_index, live_count]).astype(jnp.int32)
    gain1, gain2 = norm1_gain[None], norm2_gain[None]
    gain_q, gain_k = q_gain[None], k_gain[None]
    both = range(2)

    order = Order()
    normed_in, q_raw = order(lambda s: norm_query(s, gain1, w_q, share // 2), stream)
    kv_raw = order(
        lambda n: jnp.einsum("td,dcn->ctn", n, key_value_weight, preferred_element_type=F32), normed_in
    )
    query, key, value = order(
        lambda r: rope_forward(q_raw, r, gain_q, gain_k, cos, sin, share // 2), kv_raw
    )

    def attend(chunk):
        return order(
            lambda q: attend_forward(scalars, q, key, value, w_o, chunk, chunk_rows, reach[chunk], pieces),
            query,
        )

    def add(arrived, own, block=0):
        return add_parts([(arrived, block), (own, block)], share, BF16, places)

    attn_own, attn_arrived, mix_own, mix_other = [None] * 2, [None] * 2, [None] * 2, [None] * 2
    chip_attn, part_attn = [None] * 2, [None] * 2
    for chunk in both:
        attn_own[chunk], other, mix_own[chunk], mix_other[chunk] = attend(chunk)
        attn_arrived[chunk] = swap(other, "tensor", 1)
        if chunk == 0:
            w_k, w_v = order(lambda w: split_pair(w, share), key_value_weight)
        else:
            grad_hidden = order(lambda c: dot(c, w_down), cotangent)
        chip_attn[chunk] = order(add, attn_arrived[chunk], attn_own[chunk])
        part_attn[chunk] = swap(chip_attn[chunk], "tensor", 2)

    resids, mids_own, mids_other, backs = [], [], [], None
    for chunk in both:
        resid, mid = order(
            lambda part: middle(scalars, stream, chip_attn[chunk], part, gain2, chunk, sub),
            part_attn[chunk],
        )
        other = swap(mid, "tensor", 1)
        resids.append(resid)
        mids_own.append(mid)
        mids_other.append(other)
        mids = order(lambda o: jnp.concatenate([mid, o], axis=0), other)
        gate_up = order(lambda m: jnp.einsum("td,dcf->ctf", m, w_gu, preferred_element_type=F32), mids)
        backs = order(lambda gu: gate_back(scalars, gu, grad_hidden, backs, chunk, share, share // 2), gate_up)
    hidden, gu_own, gu_other = backs

    exchange = width // dp_ways % 128 == 0 and dp_ways == 8
    line, line_first = (1, 4, 2), (4, 2, 1)

    def piece(pairs, col, cols, bits, riders, ident):
        kind = LinePiece if bits == line else LineFirstPiece
        return kind(order, pairs, col, cols, bits, dp_ways, riders, ident)

    gu_pairs = [
        [
            (mids_own[0], gu_own, plane, 0),
            (mids_own[1], gu_own, plane, 1),
            (mids_other[0], gu_other, plane, 0),
            (mids_other[1], gu_other, plane, 1),
        ]
        for plane in both
    ]
    down_pairs = [(cotangent, hidden, None, 0)]

    def mid_part(grads):
        return order(
            lambda g: b16(jnp.einsum("ctf,dcf->td", g, w_gu, preferred_element_type=F32)), grads
        )

    riding = sum(RIDES.values(), ())
    grad_resids, grads_own, grads_other, gain2_parts = [None] * 2, [None] * 2, [None] * 2, [None] * 2
    chip_mid, part_mid, made, pieces_of, done = [None] * 2, [None] * 2, {}, {}, {}

    def start_piece(name):
        if not exchange:
            for ride in RIDES.get(name, ()):
                array, bit = rider(ride)
                landed(ride, swap(array, "tensor", bit))
            return
        pairs, col, cols = {
            GATE: (gu_pairs[0], 0, ff_cols),
            UP: (gu_pairs[1], 0, ff_cols),
            DOWN: (down_pairs, 0, ff_cols),
            QKV: ([(normed_in, made.get("qkv"), None, 0)], 0, q_cols + 2 * kv_cols),
            ATTN: (
                [
                    (grads_own[0], mix_own[0], None, 0),
                    (grads_own[1], mix_own[1], None, 0),
                    (grads_other[0], mix_other[0], None, 0),
                    (grads_other[1], mix_other[1], None, 0),
                ],
                0,
                q_cols,
            ),
        }[name]
        names = RIDES.get(name, ())
        bits = line_first if name in LINE_FIRST else line
        pieces_of[name] = piece(pairs, col, cols, bits, [rider(n) for n in names], 8 + len(pieces_of))
        for rode, arrived in zip(names, pieces_of[name].rode, strict=True):
            landed(rode, arrived)

    def rider(name):
        kind, chunk = name[:-1], int(name[-1])
        if kind == "core":
            return made["mid_part"], 1
        if kind == "input":
            return made["in_other"], 1
        return (chip_mid[chunk], 2) if kind == "middle" else (grads_own[chunk], 1)

    def landed(name, arrived):
        kind, chunk = name[:-1], int(name[-1])
        if kind == "core":
            made["mid_arrived"] = arrived
        elif kind == "input":
            made["in_arrived"] = [arrived]
        elif kind == "middle":
            part_mid[chunk] = arrived
        else:
            grads_other[chunk] = arrived

    def mid_other():
        made["mid_part"] = mid_part(gu_other)
        if "core0" not in riding:
            made["mid_arrived"] = order(lambda part: core_swap(part, 0), made["mid_part"])

    def mid_own():
        made["mid_own"] = mid_part(gu_own)

    def chip_middle(chunk):
        chip_mid[chunk] = order(lambda a: add(a, made["mid_own"], chunk), made["mid_arrived"])
        if f"middle{chunk}" not in riding:
            part_mid[chunk] = swap(chip_mid[chunk], "tensor", 2)

    def back_middle(chunk):
        grad_resids[chunk], grads_own[chunk], gain2_parts[chunk] = order(
            lambda part: middle_back(
                scalars, resids[chunk], chip_mid[chunk], part, cotangent, gain2, chunk, sub
            ),
            part_mid[chunk],
        )
        if f"grads{chunk}" not in riding:
            grads_other[chunk] = order(lambda own: core_swap(own, 1 + chunk), grads_own[chunk])

    def back_attend(chunk):
        made["backs"] = order(
            lambda other: attend_backward(
                scalars, grads_own[chunk], other, w_o, query, key, value, made.get("backs"),
                chunk, chunk_rows, reach[chunk], pieces,
            ),
            grads_other[chunk],
        )

    def rope():
        backs = made["backs"]
        made["qkv"], made["in_other"], made["in_own"], made["gain_q"], made["gain_k"] = order(
            lambda b: rope_backward(
                scalars, b, backs[1], backs[2], q_raw, kv_raw, gain_q, gain_k, cos, sin, w_q, w_k, w_v, share
            ),
            backs[0],
        )

    def scatter(own, arrived):
        def half_sum(block):
            return order(lambda first: add([first] + arrived[1:], own, block), arrived[0])

        sent = swap(half_sum(lambda s: 1 - s[0]), "tensor", 2)
        return half_sum(lambda s: s[0]), sent

    def in_scatter():
        made["in_kept"], made["in_sum"] = scatter(made["in_own"], made["in_arrived"])

    def project():
        *ffn_other, made["ffn_own"] = order(lambda h: project_other_first(scalars, h, w_down, share), hidden)
        made["ffn_arrived"] = [order(lambda part: core_swap(part, 4), part) for part in ffn_other]

    def ffn_scatter():
        made["ffn_kept"], made["ffn_sum"] = scatter(made["ffn_own"], made["ffn_arrived"])

    def stream_back():
        made["grad_stream"], made["gain1"] = order(
            lambda part: input_back(places, stream, made["in_kept"], part, grad_resids, gain1, sub),
            made["in_sum"],
        )

    def block_out():
        made["out"], made["stats"] = order(
            lambda part: layer_out(places, made["ffn_kept"], part, resids, chip_attn, part_attn, sub),
            made["ffn_sum"],
        )

    small_add = lambda mine, arrived: mine + arrived

    def small(axis, bit):
        made["packed"] = order(small_add, made["packed"], swap(made["packed"], axis, bit))

    def pack():
        made["packed"] = order(
            lambda g: jnp.concatenate(
                [g[0], (gain2_parts[0][0] + gain2_parts[1][0]) * 0.5, made["gain_q"][0], made["gain_k"][0]]
                + [made["stats"][i] for i in range(4)]
            ).reshape(-1, HEAD_SIZE),
            made["gain1"],
        )
        small("tensor", 1)
        small("tensor", 2)

    def second(name):
        if exchange:
            pieces_of[name].second()

    def third(name):
        if exchange:
            pieces_of[name].third()

    def fourth(name):
        if exchange:
            pieces_of[name].fourth()

    def last(name):
        if exchange:
            done[name] = pieces_of[name].last()

    def send_small(bit):
        if exchange:
            made["small"] = swap(made["packed"], "dp", bit)

    def add_small():
        if exchange:
            made["packed"] = order(small_add, made["packed"], made["small"])

    mid_other()
    start_piece(GATE)
    mid_own()
    chip_middle(0)
    chip_middle(1)
    start_piece(UP)
    start_piece(DOWN)
    back_middle(0)
    back_attend(0)
    back_middle(1)
    second(GATE)
    back_attend(1)
    second(UP)
    start_piece(ATTN)
    rope()
    start_piece(QKV)
    in_scatter()
    third(GATE)
    second(DOWN)
    project()
    third(UP)
    ffn_scatter()
    stream_back()
    fourth(GATE)
    second(QKV)
    block_out()
    third(DOWN)
    fourth(UP)
    second(ATTN)
    pack()
    send_small(1)
    last(GATE)
    add_small()
    send_small(2)
    third(QKV)
    last(UP)
    add_small()
    send_small(4)
    fourth(DOWN)
    fourth(QKV)
    add_small()
    third(ATTN)
    last(DOWN)
    fourth(ATTN)
    last(QKV)
    last(ATTN)
    if exchange:
        grad_w_o = done[ATTN]
        grad_w_q, grad_w_kv = done[QKV][:, :q_cols], done[QKV][:, q_cols:]
        grad_w_gu = jnp.stack([done[GATE], done[UP]], axis=1)
        grad_w_down = done[DOWN]
        totals = made["packed"].reshape(-1)
    else:
        bit = 1
        while bit < dp_ways:
            small("dp", bit)
            bit *= 2
        totals = made["packed"].reshape(-1)

        def reduced(pairs):
            total = sum(
                dot(left, (right if plane is None else right[plane])[block * left.shape[0] :][: left.shape[0]], TN)
                for left, right, plane, block in pairs
            )
            return f32(lax.psum_scatter(b16(total), "dp", scatter_dimension=0, tiled=True))

        qkv = reduced([(normed_in, made["qkv"], None, 0)])
        grad_w_q, grad_w_kv = qkv[:, :q_cols], qkv[:, q_cols:]
        grad_w_o = sum(
            dot(left, right, TN)
            for left, right in zip(grads_own + grads_other, mix_own + mix_other, strict=True)
        )
        grad_w_o = f32(lax.psum_scatter(b16(grad_w_o), "dp", scatter_dimension=0, tiled=True))
        grad_w_gu = jnp.stack([reduced(gu_pairs[0]), reduced(gu_pairs[1])], axis=1)
        grad_w_down = reduced(down_pairs)
    cuts = (width, 2 * width, 2 * width + HEAD_SIZE, 2 * width + 2 * HEAD_SIZE)
    stat_total = totals[cuts[3] :].reshape(4, HEAD_SIZE)[:, 0]
    stats = jnp.sqrt(stat_total[:3] / (stat_total[3] * MODEL_WIDTH))
    return (
        made["out"],
        made["grad_stream"],
        grad_w_q,
        grad_w_kv.reshape(-1, 2, kv_cols),
        grad_w_o,
        grad_w_gu,
        grad_w_down,
        totals[: cuts[0]],
        totals[cuts[0] : cuts[1]],
        totals[cuts[1] : cuts[2]],
        totals[cuts[2] : cuts[3]],
        stats,
    )


def solution(mesh):
    placed = (
        P("dp", None),
        P("dp", None),
        P("dp"),
        P("dp", None),
        P("dp", None),
        P(),
        P(None, "tensor"),
        P(None, None, "tensor"),
        P(),
        P(),
        P(None, "tensor"),
        P(),
        P(None, None, "tensor"),
        P(None, "tensor"),
    )
    return jax.shard_map(
        per_device,
        mesh=mesh,
        in_specs=placed,
        out_specs=(
            P(("dp", "tensor"), None),
            P(("dp", "tensor"), None),
            P("dp", "tensor"),
            P("dp", None, "tensor"),
            P("dp", "tensor"),
            P("dp", None, "tensor"),
            P("dp", "tensor"),
            P(),
            P(),
            P(),
            P(),
            P(),
        ),
        check_vma=False,
    )
```
